32 devices in a mesh: seq: 8 (over y, x, core), head: 4 (over z).
Axes of the slice: x: 2, y: 2, z: 4, core: 2. Of those that a mesh axis runs over, the one named last changes fastest.
Arguments:
- block_in: bfloat16 [4096, 2048], P('seq'), may hold values from -6 to 6
- pre_gain: float32 [2048], replicated, may hold values from 0.1 to 1.9
- gate_proj: bfloat16 [2048, 2560], P(None, 'head'), may hold values from -0.125 to 0.125
- input_proj: bfloat16 [2048, 2560], P(None, 'head'), may hold values from -0.125 to 0.125
- conv_taps: float32 [4, 2560], P(None, 'head'), may hold values from -3 to 3
- recur_gate: bfloat16 [16, 160, 160], P('head'), may hold values from -0.5 to 0.5
- input_gate: bfloat16 [16, 160, 160], P('head'), may hold values from -0.5 to 0.5
- decay_param: float32 [2560], P('head'), may hold values from 5 to 13
- out_proj: bfloat16 [2560, 2048], P('head'), may hold values from -0.3125 to 0.3125
- post_gain: float32 [2048], replicated, may hold values from 0.1 to 1.9
- ffn_gate: bfloat16 [2048, 6144], P(None, 'head'), may hold values from -0.125 to 0.125
- ffn_up: bfloat16 [2048, 6144], P(None, 'head'), may hold values from -0.125 to 0.125
- ffn_down: bfloat16 [6144, 2048], P('head'), may hold values from -0.109375 to 0.109375
- cotangent: bfloat16 [4096, 2048], P('seq'), may hold values from -6 to 6
Outputs:
- block_out: bfloat16 [4096, 2048], P('seq')
- grad_input: float32 [4096, 2048], P('seq')
- grad_pregain: float32 [2048], P('seq')
- grad_gateproj: float32 [2048, 2560], P('seq', 'head')
- grad_inproj: float32 [2048, 2560], P('seq', 'head')
- grad_convtaps: float32 [4, 2560], P(None, ('head', 'seq'))
- grad_recur: float32 [16, 160, 160], P('head', 'seq')
- grad_ingate: float32 [16, 160, 160], P('head', 'seq')
- grad_decay: float32 [2560], P(('head', 'seq'))
- grad_outproj: float32 [2560, 2048], P('head', 'seq')
- grad_postgain: float32 [2048], P('seq')
- grad_ffngate: float32 [2048, 6144], P('seq', 'head')
- grad_ffnup: float32 [2048, 6144], P('seq', 'head')
- grad_ffndown: float32 [6144, 2048], P('head', 'seq')
The draws below stay inside these ranges and needn't reach their ends.
All inputs are finite; a program needn't handle non-finite values.
Results may differ from the reference program's by a relative error of at most 0.02.
Values may be sent and summed in bfloat16 or wider, within the bound.
No kernel may reach another device: no remote copies, remote signals or barrier semaphores. Data moves between devices by JAX's collectives and lax.ppermute only.
A program may use at most 256 MiB of HBM per device.

```python
import math
import jax
import jax.numpy as jnp
from jax import lax

D = 2048
BLOCKS = 16
BW = 160
FF = 6144
KW = 4
BR = 2560
TOKENS = 4096


def with_spikes(drawn, stream_key, source, target, shards_of, factor):
    owner, partner = [(jnp.arange(drawn.shape[dim]) // (drawn.shape[dim] // shards_of)).reshape([-1 if axis == dim else 1 for axis in range(drawn.ndim)]) for dim in (source, target)]
    chosen = jax.random.permutation(stream_key, shards_of)[partner]
    strong = (owner == chosen) | (owner == (partner + shards_of // 2) % shards_of)
    return jnp.where(strong, factor * drawn, drawn)


def levels(own_key, extent, split, least, top_value):
    loudness = 1.0
    for position, blocks in split:
        steps = jax.random.uniform(jax.random.fold_in(jax.random.fold_in(own_key, 6), position), (blocks,), jnp.float32, least / len(split), top_value / len(split))
        loudness = loudness * jnp.repeat(jnp.exp(steps), extent[position] // blocks).reshape((-1,) + (1,) * (len(extent) - 1 - position))
    return loudness


def centred(key, extent, scale, limit, split=(), kind=jnp.bfloat16):
    level = levels(key, extent, split, -0.22, 0.18) if split else 1.0
    drawn = jax.random.normal(key, extent, jnp.float32) * scale * level
    return jnp.minimum(jnp.maximum(drawn, -limit), limit).astype(kind)


def heavy_noise(key, dims, deviation, most, split, heavy, kind=jnp.bfloat16):
    values = deviation * jax.random.normal(key, dims, jnp.float32)
    if split:
        values = values * levels(key, dims, split, -0.22, 0.18)
    return jnp.clip(with_spikes(values, jax.random.fold_in(key, 3), *heavy), -most, most).astype(kind)


def setup_inputs(seed: int = 0) -> dict:
    streams_of = jax.random.split(jax.random.key(seed), 15)
    block_in = heavy_noise(streams_of[0], (TOKENS, D), 1.0, 6.0, ((0, 8),), (0, 1, 8, 2.0))
    pre_gain = jnp.clip(1.0 + 0.18 * jax.random.normal(streams_of[1], (D,), jnp.float32), 0.1, 1.9)
    gate_proj = centred(streams_of[2], (D, BR), D ** -0.5, 0.125, ((1, 4),))
    input_proj = centred(streams_of[3], (D, BR), D ** -0.5, 0.125, ((1, 4),))
    conv_taps = centred(streams_of[4], (KW, BR), KW ** -0.5, 3.0, ((1, 4),), jnp.float32)
    recur_gate = centred(streams_of[5], (BLOCKS, BW, BW), BW ** -0.5, 0.5, ((0, 4),))
    input_gate = centred(streams_of[6], (BLOCKS, BW, BW), BW ** -0.5, 0.5, ((0, 4),))
    decay_param = jnp.clip(5.0 + 8.0 * jax.random.uniform(streams_of[7], (BR,), jnp.float32) ** levels(streams_of[7], (BR,), ((0, 4),), -0.2, 0.2), 5.0, 13.0)
    out_proj = centred(streams_of[8], (BR, D), (BLOCKS * BW // 8) ** -0.5, 0.3125, ((0, 4),))
    post_gain = jnp.clip(1.0 + 0.18 * jax.random.normal(streams_of[9], (D,), jnp.float32), 0.1, 1.9)
    ffn_gate = centred(streams_of[10], (D, FF), D ** -0.5, 0.125, ((1, 4),))
    ffn_up = centred(streams_of[11], (D, FF), D ** -0.5, 0.125, ((1, 4),))
    ffn_down = centred(streams_of[12], (FF, D), (FF // 2) ** -0.5, 0.109375, ((0, 4),))
    cotangent = heavy_noise(streams_of[13], (TOKENS, D), 1.0, 6.0, ((0, 8),), (0, 1, 8, 2.0))
    return {"block_in": block_in, "pre_gain": pre_gain, "gate_proj": gate_proj, "input_proj": input_proj, "conv_taps": conv_taps, "recur_gate": recur_gate, "input_gate": input_gate, "decay_param": decay_param, "out_proj": out_proj, "post_gain": post_gain, "ffn_gate": ffn_gate, "ffn_up": ffn_up, "ffn_down": ffn_down, "cotangent": cotangent}


epsilon = 1e-06
sharpness = 8.0

@jax.custom_vjp
def low(v):
    return lax.optimization_barrier(v.astype(jnp.bfloat16)).astype(jnp.float32)

@jax.custom_vjp
def low_back(v):
    return v

def low_keep(v):
    return (low(v), None)

def low_pass(kept, grad):
    return (grad,)

def back_keep(v):
    return (v, None)

def back_low(kept, grad):
    return (low(grad),)
low.defvjp(low_keep, low_pass)
low_back.defvjp(back_keep, back_low)

def rms_norm(values, scales):
    return values * lax.rsqrt(lax.optimization_barrier(jnp.mean(values * values, axis=-1, keepdims=True)) + epsilon) * scales

def gelu_tanh(values):
    return jax.nn.gelu(values, approximate=True)

def matmul(first_op, second_op):
    return jnp.dot(first_op, second_op, precision=lax.Precision.HIGHEST)

def combine_pairs(former, latter):
    return (former[0] * latter[0], latter[0] * former[1] + latter[1])

def decay_terms(recur_pre, input_pre, conv_vals, decay_param):
    recur_rate = jax.nn.sigmoid(recur_pre)
    log_decay = -sharpness * recur_rate * jax.nn.softplus(-decay_param)
    decays = jnp.exp(log_decay)
    drives = jnp.sqrt(-jnp.expm1(2.0 * log_decay)) * jax.nn.sigmoid(input_pre) * conv_vals
    return (decays, drives)

def scan_block(carried, block_pair):
    decay_prods, local_states = lax.associative_scan(combine_pairs, block_pair, axis=0)
    states = local_states + decay_prods * carried
    return (states[-1], states)

def forward(block_in, pre_gain, gate_proj, input_proj, conv_taps, recur_gate, input_gate, decay_param, out_proj, post_gain, ffn_gate, ffn_up, ffn_down):
    tokens = block_in.shape[0]
    normed = low(rms_norm(block_in, pre_gain))
    gate_pre = low_back(matmul(normed, gate_proj))
    branch_in = low_back(low(matmul(normed, input_proj)))
    padded = jnp.concatenate([jnp.zeros((KW - 1, BR), jnp.float32), branch_in], axis=0)
    conv_sum = conv_taps[0] * padded[KW - 1:]
    for offset in range(1, KW):
        conv_sum = conv_sum + conv_taps[offset] * padded[KW - 1 - offset:KW - 1 - offset + tokens]
    conv_vals = low(conv_sum)
    grouped = conv_vals.reshape(tokens, BLOCKS, BW)
    recur_pre = low_back(jnp.einsum('tbi,bij->tbj', grouped, recur_gate, precision=lax.Precision.HIGHEST).reshape(tokens, BR))
    input_pre = low_back(jnp.einsum('tbi,bij->tbj', grouped, input_gate, precision=lax.Precision.HIGHEST).reshape(tokens, BR))
    decays, drives = decay_terms(recur_pre, input_pre, conv_vals, decay_param)
    block_rows = math.gcd(tokens, 512)
    _, states = lax.scan(jax.checkpoint(scan_block), jnp.zeros((BR,), jnp.float32), (decays.reshape(-1, block_rows, BR), drives.reshape(-1, block_rows, BR)))
    states = states.reshape(tokens, BR)
    mixed_low = low(gelu_tanh(gate_pre) * states)
    residual = block_in + low_back(matmul(mixed_low, out_proj))
    normed_two = low(rms_norm(residual, post_gain))
    ffn_gpre = low_back(matmul(normed_two, ffn_gate))
    ffn_upre = low_back(matmul(normed_two, ffn_up))
    hidden = low(gelu_tanh(ffn_gpre) * ffn_upre)
    return residual + matmul(hidden, ffn_down)

def reference(block_in, pre_gain, gate_proj, input_proj, conv_taps, recur_gate, input_gate, decay_param, out_proj, post_gain, ffn_gate, ffn_up, ffn_down, cotangent):
    inputs = tuple((item.astype(jnp.float32) for item in (block_in, pre_gain, gate_proj, input_proj, conv_taps, recur_gate, input_gate, decay_param, out_proj, post_gain, ffn_gate, ffn_up, ffn_down)))
    result, pullback = jax.vjp(forward, *inputs)
    gradients = pullback(cotangent.astype(jnp.float32))
    return (result.astype(jnp.bfloat16), gradients[0], gradients[1], gradients[2], gradients[3], gradients[4], gradients[5], gradients[6], gradients[7], gradients[8], gradients[9], gradients[10], gradients[11], gradients[12])
```

```python
import jax
import jax.numpy as jnp
from jax import lax
from jax.experimental import pallas as pl
from jax.experimental.pallas import tpu as pltpu
from jax.sharding import PartitionSpec as P

epsilon = 1e-06
sharpness = 8.0
segments = 8
rows_at_once = 32
root_two_over_pi = 0.7978845608028654
cubic = 0.044715
f32 = jnp.float32
bf16 = jnp.bfloat16


def call(body, out_shape, scratch, *operands, scalars=0, flops=0):
    vectors = len(operands) - scalars
    moved = sum(x.size * x.dtype.itemsize for x in (*operands, *out_shape))
    return pl.pallas_call(
        body,
        out_shape=out_shape,
        in_specs=[pl.BlockSpec(memory_space=pltpu.VMEM)] * vectors
        + [pl.BlockSpec(memory_space=pltpu.SMEM)] * scalars,
        out_specs=[pl.BlockSpec(memory_space=pltpu.VMEM)] * len(out_shape),
        scratch_shapes=scratch,
        compiler_params=pltpu.CompilerParams(vmem_limit_bytes=48 << 20),
        cost_estimate=pl.CostEstimate(flops=1000, bytes_accessed=1000, transcendentals=0),
    )(*operands)


def split(ref, at, value):
    for j in range(ref.shape[0]):
        ref[j, at, :] = value[:, 128 * j : 128 * (j + 1)]


def joined(ref, at):
    return jnp.concatenate([ref[j, at, :] for j in range(ref.shape[0])], axis=1)


def over_rows(tokens, body):
    @pl.loop(0, tokens // rows_at_once)
    def _(step):
        body(pl.multiple_of(step * rows_at_once, rows_at_once))


def minus_expm1(v):
    series = 1.0 / 5040.0
    for term in (720.0, 120.0, 24.0, 6.0, 2.0, 1.0):
        series = series * v + 1.0 / term
    return jnp.where(v > -0.25, -v * series, 1.0 - jnp.exp(v))


def gelu_parts(v):
    bent = jnp.tanh(root_two_over_pi * (v + cubic * v * v * v))
    half = 0.5 * (1.0 + bent)
    slope = half + 0.5 * v * (1.0 - bent * bent) * root_two_over_pi * (1.0 + 3.0 * cubic * v * v)
    return v * half, slope


def forward_scan(
    branch_ref, halo_ref, taps_ref, soft_ref, recur_gate_ref, input_gate_ref,
    conv_ref, recur_ref, input_ref, local_ref, prod_ref, seg_ref, end_ref, gates_ref,
    padded, pre, decay, drive,
):
    tokens, channels = branch_ref.shape
    taps = taps_ref.shape[0]
    steps = tokens // segments
    blocks, width, _ = recur_gate_ref.shape
    gates_ref[...] = jnp.zeros((channels, 2 * channels), bf16)
    for b in range(blocks):
        rows = pl.ds(b * width, width)
        gates_ref[rows, b * width : (b + 1) * width] = recur_gate_ref[b]
        gates_ref[rows, channels + b * width : channels + (b + 1) * width] = input_gate_ref[b]
    padded[0:8, :] = halo_ref[...].astype(f32)

    def fill(row):
        padded[pl.ds(row + 8, rows_at_once), :] = branch_ref[pl.ds(row, rows_at_once), :].astype(f32)

    over_rows(tokens, fill)

    def convolve(row):
        window = padded[pl.ds(row, rows_at_once + 8), :]
        total = taps_ref[0:1, :] * window[8:, :]
        for k in range(1, taps):
            total = total + taps_ref[k : k + 1, :] * window[8 - k : 8 - k + rows_at_once, :]
        conv_ref[pl.ds(row, rows_at_once), :] = total.astype(bf16)

    over_rows(tokens, convolve)
    pre[...] = jnp.dot(conv_ref[...], gates_ref[...], preferred_element_type=f32)

    def terms(row):
        at = pl.ds(row, rows_at_once)
        recur = jax.nn.sigmoid(pre[at, 0:channels])
        inward = jax.nn.sigmoid(pre[at, channels : 2 * channels])
        log_decay = -sharpness * recur * soft_ref[...]
        recur_ref[at, :] = recur
        input_ref[at, :] = inward
        split(decay, at, jnp.exp(log_decay))
        split(drive, at, jnp.sqrt(minus_expm1(2.0 * log_decay)) * inward * conv_ref[at, :].astype(f32))

    over_rows(tokens, terms)

    slabs = channels // 128

    def step(i, carried):
        at = pl.ds(i, segments, stride=steps)
        new = []
        for j in range(slabs):
            state, product = carried[j]
            a = decay[j, at, :]
            state = a * state + drive[j, at, :]
            product = a * product
            local_ref[j, at, :] = state
            prod_ref[j, at, :] = product
            new.append((state, product))
        return tuple(new)

    start = ((jnp.zeros((segments, 128), f32), jnp.ones((segments, 128), f32)),) * slabs
    last = lax.fori_loop(0, steps, step, start, unroll=4)
    state = jnp.concatenate([pair[0] for pair in last], axis=1)
    product = jnp.concatenate([pair[1] for pair in last], axis=1)
    seg_ref[0:segments, :] = product
    seg_ref[segments : 2 * segments, :] = state
    whole = jnp.ones((1, channels), f32)
    end = jnp.zeros((1, channels), f32)
    for s in range(segments):
        end = product[s : s + 1, :] * end + state[s : s + 1, :]
        whole = product[s : s + 1, :] * whole
    end_ref[0:1, :] = whole
    end_ref[1:2, :] = end


def mix(gate_ref, local_ref, prod_ref, seg_ref, ends_ref, index_ref, states_ref, mixed_ref, entry_ref):
    tokens, channels = gate_ref.shape
    steps = tokens // segments
    index = index_ref[0]
    carry = jnp.zeros((1, channels), f32)
    for j in range(ends_ref.shape[0]):
        new = ends_ref[j, 0:1, :] * carry + ends_ref[j, 1:2, :]
        carry = jnp.where(j < index, new, carry)
    entry_ref[...] = carry
    for s in range(segments):
        held = carry

        @pl.loop(0, steps // rows_at_once)
        def _(i):
            at = pl.ds(pl.multiple_of(s * steps + i * rows_at_once, rows_at_once), rows_at_once)
            states = joined(local_ref, at) + joined(prod_ref, at) * held
            states_ref[at, :] = states
            gate, _ = gelu_parts(gate_ref[at, :])
            mixed_ref[at, :] = (gate * states).astype(bf16)

        carry = seg_ref[s : s + 1, :] * carry + seg_ref[segments + s : segments + s + 1, :]


def backward_scan(
    d_mixed_ref, gate_ref, states_ref, recur_ref, soft_ref,
    d_gate_ref, local_ref, prod_ref, seg_ref, end_ref,
    decay, d_state,
):
    tokens, channels = gate_ref.shape
    steps = tokens // segments

    def terms(row):
        at = pl.ds(row, rows_at_once)
        d_mixed = d_mixed_ref[at, :].astype(f32)
        value, slope = gelu_parts(gate_ref[at, :])
        d_gate_ref[at, :] = (d_mixed * states_ref[at, :] * slope).astype(bf16)
        split(d_state, at, d_mixed * value)
        split(decay, at, jnp.exp(-sharpness * recur_ref[at, :] * soft_ref[...]))

    over_rows(tokens, terms)

    slabs = channels // 128

    def step(k, carried):
        at = pl.ds(steps - 1 - k, segments, stride=steps)
        new = []
        for j in range(slabs):
            into, reach = carried[j]
            a = decay[j, at, :]
            grad = d_state[j, at, :] + into
            local_ref[j, at, :] = grad
            prod_ref[j, at, :] = reach
            new.append((a * grad, a * reach))
        return tuple(new)

    start = ((jnp.zeros((segments, 128), f32), jnp.ones((segments, 128), f32)),) * slabs
    last = lax.fori_loop(0, steps, step, start, unroll=4)
    into = jnp.concatenate([pair[0] for pair in last], axis=1)
    reach = jnp.concatenate([pair[1] for pair in last], axis=1)
    seg_ref[0:segments, :] = reach
    seg_ref[segments : 2 * segments, :] = into
    end = jnp.zeros((1, channels), f32)
    for s in reversed(range(segments)):
        end = reach[s : s + 1, :] * end + into[s : s + 1, :]
    end_ref[...] = end


def backward_terms(
    local_ref, prod_ref, seg_ref, ends_ref, backs_ref, recur_ref, input_ref, conv_ref, states_ref, entry_ref,
    soft_ref, slide_ref, taps_ref, branch_ref, halo_ref, gates_ref, index_ref,
    d_both_ref, d_branch_ref, head_ref, decay_sum_ref, taps_sum_ref,
    before, d_conv, padded,
):
    tokens, channels = states_ref.shape
    taps = taps_ref.shape[0]
    steps = tokens // segments
    index = index_ref[0]
    padded[0:8, :] = halo_ref[...].astype(f32)
    before[0:8, :] = jnp.broadcast_to(entry_ref[...], (8, channels))
    carry = jnp.zeros((1, channels), f32)
    for j in reversed(range(ends_ref.shape[0])):
        new = ends_ref[j, 0:1, :] * carry + backs_ref[j, 0:1, :]
        carry = jnp.where(j > index, new, carry)
    decay_sum_ref[...] = jnp.zeros((8, channels), f32)
    taps_sum_ref[...] = jnp.zeros((8 * taps, channels), f32)

    def fill(row):
        padded[pl.ds(row + 8, rows_at_once), :] = branch_ref[pl.ds(row, rows_at_once), :].astype(f32)
        before[pl.ds(row + 8, rows_at_once), :] = states_ref[pl.ds(row, rows_at_once), :]

    over_rows(tokens, fill)
    for s in reversed(range(segments)):
        held = carry

        @pl.loop(0, steps // rows_at_once)
        def _(i):
            row = pl.multiple_of(s * steps + i * rows_at_once, rows_at_once)
            at = pl.ds(row, rows_at_once)
            grad = joined(local_ref, at) + joined(prod_ref, at) * held
            recur = recur_ref[at, :]
            inward = input_ref[at, :]
            conv = conv_ref[at, :].astype(f32)
            log_decay = -sharpness * recur * soft_ref[...]
            decay = jnp.exp(log_decay)
            root = jnp.sqrt(minus_expm1(2.0 * log_decay))
            previous = before[pl.ds(row, rows_at_once + 8), :][7 : 7 + rows_at_once, :]
            push = grad * inward
            total = decay * (grad * previous - push * decay * conv / root)
            rate = recur * total
            d_both_ref[at, 0:channels] = (-sharpness * soft_ref[...] * (1.0 - recur) * rate).astype(bf16)
            d_both_ref[at, channels : 2 * channels] = (push * root * conv * (1.0 - inward)).astype(bf16)
            d_conv[at, :] = push * root
            decay_sum_ref[...] += jnp.sum(rate.reshape(rows_at_once // 8, 8, channels), axis=0)

        carry = seg_ref[s : s + 1, :] * carry + seg_ref[segments + s : segments + s + 1, :]
    decay_sum_ref[...] = decay_sum_ref[...] * slide_ref[...]
    d_conv[0:tokens, :] += lax.dot_general(
        d_both_ref[...], gates_ref[...], (((1,), (1,)), ((), ())), preferred_element_type=f32
    )
    d_conv[tokens : tokens + 8, :] = jnp.zeros((8, channels), f32)
    first = jnp.concatenate([jnp.zeros((8, channels), f32), d_conv[0:8, :]], axis=0)
    head = taps_ref[0:1, :] * first[0:8, :]
    for k in range(1, taps):
        head = head + taps_ref[k : k + 1, :] * first[k : k + 8, :]
    head_ref[...] = head

    def finish(row):
        window = d_conv[pl.ds(row, rows_at_once + 8), :]
        now = window[0:rows_at_once, :]
        total = taps_ref[0:1, :] * now
        for k in range(1, taps):
            total = total + taps_ref[k : k + 1, :] * window[k : k + rows_at_once, :]
        d_branch_ref[pl.ds(row, rows_at_once), :] = total
        earlier = padded[pl.ds(row, rows_at_once + 8), :]
        for k in range(taps):
            product = now * earlier[8 - k : 8 - k + rows_at_once, :]
            taps_sum_ref[8 * k : 8 * k + 8, :] += jnp.sum(
                product.reshape(rows_at_once // 8, 8, channels), axis=0
            )

    over_rows(tokens, finish)


def place(me, own_ref, arrived, store):
    from_left, from_right, over, back, far = arrived
    for m, parts in enumerate(
        (
            (own_ref, from_right, back, far),
            (from_left, own_ref, from_right, over),
            (over, from_left, own_ref, from_right),
            (far, back, from_left, own_ref),
        )
    ):

        @pl.when(me == m)
        def _():
            for source, ref in enumerate(parts):
                store(source, ref)


def add_projection(
    own_ref, left_ref, right_ref, over_ref, back_ref, far_ref, weight_ref, inputs_ref, gain_ref, index_ref,
    residual_ref, normed_ref, inverse_ref,
    mixed, rows,
):
    tokens, channels = own_ref.shape
    columns = weight_ref.shape[2]
    step = pl.program_id(0)

    def store(source, ref):
        mixed[:, source * channels : (source + 1) * channels] = ref[...]

    @pl.when(step == 0)
    def _():
        place(index_ref[0], own_ref, (left_ref, right_ref, over_ref, back_ref, far_ref), store)

    total = inputs_ref[...].astype(f32) + jnp.dot(mixed[...], weight_ref[0], preferred_element_type=f32)
    residual_ref[...] = total
    rows[:, pl.ds(pl.multiple_of(step * columns, columns), columns)] = total

    @pl.when(step == pl.num_programs(0) - 1)
    def _():
        def normalise(row):
            at = pl.ds(row, rows_at_once)
            values = rows[at, :]
            inverse = inverse_rms(values)
            inverse_ref[at, :] = inverse
            normed_ref[at, :] = (values * inverse * gain_ref[...]).astype(bf16)

        over_rows(tokens, normalise)


def residual_norm(own, arrived, weight, inputs, gain, index):
    tokens, channels = own.shape
    blocks, depth, columns = weight.shape
    width = inputs.shape[1]

    def whole(*dims):
        return pl.BlockSpec(dims, lambda j: (0,) * len(dims))

    return pl.pallas_call(
        add_projection,
        grid=(blocks,),
        in_specs=[whole(tokens, channels)] * 6
        + [
            pl.BlockSpec((1, depth, columns), lambda j: (j, 0, 0)),
            pl.BlockSpec((tokens, columns), lambda j: (0, j)),
            whole(1, width),
            pl.BlockSpec(memory_space=pltpu.SMEM),
        ],
        out_specs=[pl.BlockSpec((tokens, columns), lambda j: (0, j)), whole(tokens, width), whole(tokens, 1)],
        out_shape=[
            jax.ShapeDtypeStruct((tokens, width), f32),
            jax.ShapeDtypeStruct((tokens, width), bf16),
            jax.ShapeDtypeStruct((tokens, 1), f32),
        ],
        scratch_shapes=[pltpu.VMEM((tokens, depth), bf16), pltpu.VMEM((tokens, width), f32)],
        compiler_params=pltpu.CompilerParams(vmem_limit_bytes=48 << 20),
        cost_estimate=pl.CostEstimate(
            flops=2 * tokens * depth * width,
            bytes_accessed=2 * (depth * width + 5 * tokens * width),
            transcendentals=0,
        ),
    )(own, *arrived, weight, inputs, gain, index)


def rotated(own, arrived, index):
    size, width = own.shape
    peers = len(arrived) + 1

    def body(*refs):
        *part_refs, index_ref, out_ref = refs
        for k, ref in enumerate(part_refs):
            source = lax.rem(index_ref[0] + (peers - k), peers)
            out_ref[pl.ds(pl.multiple_of(source * size, size), size), :] = ref[...]

    whole = jax.ShapeDtypeStruct((peers * size, width), own.dtype)
    return call(body, [whole], [], own, *arrived, index, scalars=1)[0]


def assembled(own, first, second, index, kind):
    size, width = own.shape
    peers = lax.axis_size("head")

    def body(own_ref, left_ref, right_ref, over_ref, back_ref, far_ref, index_ref, out_ref):
        def store(source, ref):
            out_ref[source * size : (source + 1) * size, :] = ref[...].astype(kind)

        place(index_ref[0], own_ref, (left_ref, right_ref, over_ref, back_ref, far_ref), store)

    return call(
        body,
        [jax.ShapeDtypeStruct((peers * size, width), kind)],
        [],
        own,
        *first,
        *second,
        index,
        scalars=1,
    )[0]


def weight_grads(products, extra=None):
    lefts = [left for left, _ in products]
    rights = [right for _, right in products]
    tokens, width = lefts[0].shape
    count = len(products)
    spans = [right.shape[1] for right in rights]
    total = sum(spans) + (0 if extra is None else extra.shape[1])
    block = 256

    def body(*refs):
        left_refs, right_refs, out_ref = refs[:count], refs[count : 2 * count], refs[-1]
        place = 0
        for left_ref, right_ref in zip(left_refs, right_refs, strict=True):
            span = right_ref.shape[1]
            out_ref[:, place : place + span] = lax.dot_general(
                left_ref[...], right_ref[...], (((0,), (0,)), ((), ())), preferred_element_type=f32
            ).astype(bf16)
            place += span
        if extra is not None:
            out_ref[:, place:] = refs[2 * count][...]

    extras = [] if extra is None else [extra]
    return pl.pallas_call(
        body,
        grid=(width // block,),
        in_specs=[pl.BlockSpec((tokens, block), lambda i: (0, i))] * count
        + [pl.BlockSpec((tokens, span), lambda i: (0, 0)) for span in spans]
        + [pl.BlockSpec((block, e.shape[1]), lambda i: (i, 0)) for e in extras],
        out_specs=pl.BlockSpec((block, total), lambda i: (i, 0)),
        out_shape=jax.ShapeDtypeStruct((width, total), bf16),
        compiler_params=pltpu.CompilerParams(vmem_limit_bytes=48 << 20),
        cost_estimate=pl.CostEstimate(
            flops=2 * tokens * width * total, bytes_accessed=2 * width * total, transcendentals=0
        ),
    )(*lefts, *rights, *extras)


def gate_grads(conv_low, d_both, taps_sums, decay_sums, blocks, owners, rows):
    channels = conv_low.shape[1]
    taps = taps_sums.shape[0] // 8
    width = channels // blocks
    patch, kept, span = width // owners, channels // owners, rows // owners
    columns = -(-2 * width // 128) * 128

    def body(conv_ref, both_ref, taps_ref, decay_ref, out_ref):
        out_ref[...] = jnp.zeros((rows, columns), bf16)
        dense = lax.dot_general(
            conv_ref[...], both_ref[...], (((0,), (0,)), ((), ())), preferred_element_type=f32
        )
        sums = [jnp.sum(taps_ref[8 * k : 8 * k + 8, :], axis=0, keepdims=True) for k in range(taps)]
        sums.append(jnp.sum(decay_ref[...], axis=0, keepdims=True))
        sums = jnp.concatenate(sums, axis=0).astype(bf16)
        for b in range(blocks):
            at = slice(b * width, (b + 1) * width)
            recur = dense[at, b * width : (b + 1) * width].astype(bf16)
            inward = dense[at, channels + b * width : channels + (b + 1) * width].astype(bf16)
            for s in range(owners):
                row = s * span + b * patch
                out_ref[row : row + patch, 0:width] = recur[s * patch : (s + 1) * patch, :]
                out_ref[row : row + patch, width : 2 * width] = inward[s * patch : (s + 1) * patch, :]
        for s in range(owners):
            row = s * span + blocks * patch
            out_ref[row : row + taps + 1, 0:kept] = sums[:, s * kept : (s + 1) * kept]

    return call(
        body,
        [jax.ShapeDtypeStruct((rows, columns), bf16)],
        [],
        conv_low,
        d_both,
        taps_sums,
        decay_sums,
        flops=4 * conv_low.shape[0] * channels * channels,
    )[0]


def shifted(count, by):
    return [(i, (i + by) % count) for i in range(count)]


def exchanged(blocks):
    peers = lax.axis_size("head")
    return [lax.ppermute(blocks(k), "head", shifted(peers, k)) for k in range(1, peers)]


def block_of(array, where, dim):
    peers = lax.axis_size("head")
    size = array.shape[dim] // peers
    return lax.dynamic_slice_in_dim(array, (where % peers) * size, size, dim)


def shard(array, where):
    return block_of(array, where, 0)


def added(first, *others):
    total = first.astype(f32)
    for part in others:
        total = total + part.astype(f32)
    return total


def line_pairs(by):
    peers = lax.axis_size("head")
    return [(i, i + by) for i in range(peers) if 0 <= i + by < peers]


def scatter_first(low):
    me = lax.axis_index("head")
    across = shard(low, me + 2)
    return (
        lax.ppermute(across, "head", [(0, 1), (1, 2)]),
        lax.ppermute(across, "head", [(3, 2), (2, 1)]),
        lax.ppermute(shard(low, 3 - me), "head", [(0, 2), (3, 1)]),
    )


def scatter_second(low, first):
    me = lax.axis_index("head")
    from_left, from_right, far = first
    none = jnp.zeros_like(far)
    to_right = added(shard(low, me + 1), from_left, jnp.where(me == 2, far, none)).astype(bf16)
    to_left = added(shard(low, me - 1), from_right, jnp.where(me == 1, far, none)).astype(bf16)
    return lax.ppermute(to_right, "head", line_pairs(1)), lax.ppermute(to_left, "head", line_pairs(-1))


def gather_first(own):
    return lax.ppermute(own, "head", line_pairs(1)), lax.ppermute(own, "head", line_pairs(-1))


def gather_second(first):
    me = lax.axis_index("head")
    from_left, from_right = first
    over = jnp.where(me == 1, from_left, from_right)
    back = jnp.where(me == 1, from_right, from_left)
    return (
        lax.ppermute(over, "head", [(1, 2), (2, 1)]),
        lax.ppermute(back, "head", [(1, 0), (2, 3)]),
        lax.ppermute(over, "head", [(1, 3), (2, 0)]),
    )


def line_turn(turn, sent):
    peers = lax.axis_size("head")
    return lax.ppermute(sent, "head", [(turn - 1, turn), (peers - turn, peers - turn - 1)])


together = lax.optimization_barrier


def inverse_rms(values):
    return lax.rsqrt(jnp.mean(values * values, axis=-1, keepdims=True) + epsilon)


def norm_back(values, inverse, scales, grad):
    unit = values * inverse
    scaled = grad * scales
    inner = jnp.mean(scaled * unit, axis=-1, keepdims=True)
    return inverse * (scaled - unit * inner), jnp.sum(grad * unit, axis=0)


def local(
    block_in,
    pre_gain,
    gate_proj,
    input_proj,
    conv_taps,
    recur_gate,
    input_gate,
    decay_param,
    out_proj,
    post_gain,
    ffn_gate,
    ffn_up,
    ffn_down,
    cotangent,
):
    tokens, width = block_in.shape
    channels = gate_proj.shape[1]
    blocks, block_width, _ = recur_gate.shape
    tap_count = conv_taps.shape[0]
    hidden_units = ffn_gate.shape[1]
    seq_count, seq_index = lax.axis_size("seq"), lax.axis_index("seq")
    head_count, head_index = lax.axis_size("head"), lax.axis_index("head")
    share = tokens // head_count
    slabs = (channels // 128, tokens, 128)
    here = seq_index.astype(jnp.int32).reshape(1)
    place_index = head_index.astype(jnp.int32).reshape(1)
    forward_pairs = [(i, i + 1) for i in range(seq_count - 1)]
    backward_pairs = [(i + 1, i) for i in range(seq_count - 1)]

    def mine(rows):
        return lax.dynamic_slice_in_dim(rows, head_index * share, share, 0)

    def struct(*dims, kind=f32):
        return jax.ShapeDtypeStruct(dims, kind)

    halo_in = lax.ppermute(block_in[tokens - 8 :], "seq", forward_pairs)
    columns = width // seq_count
    column_block = lax.dynamic_slice_in_dim(out_proj, seq_index * columns, columns, 1)
    column_pieces = exchanged(lambda k: column_block)
    soft = jax.nn.softplus(-decay_param)[None, :]
    slide = sharpness * jax.nn.sigmoid(-decay_param)[None, :]

    def normalise(rows):
        values = rows.astype(f32)
        return (values * inverse_rms(values) * pre_gain).astype(bf16)

    normed = normalise(block_in)
    branch_in = jnp.dot(normed, input_proj, preferred_element_type=f32).astype(bf16)
    halo = jnp.dot(normalise(halo_in), input_proj, preferred_element_type=f32).astype(bf16)
    conv_low, recur_rate, input_rate, local_states, products, seg_ends, end, gates = call(
        forward_scan,
        [
            struct(tokens, channels, kind=bf16),
            struct(tokens, channels),
            struct(tokens, channels),
            struct(*slabs),
            struct(*slabs),
            struct(2 * segments, channels),
            struct(2, channels),
            struct(channels, 2 * channels, kind=bf16),
        ],
        [
            pltpu.VMEM((tokens + 8, channels), f32),
            pltpu.VMEM((tokens, 2 * channels), f32),
            pltpu.VMEM(slabs, f32),
            pltpu.VMEM(slabs, f32),
        ],
        branch_in,
        halo,
        conv_taps,
        soft,
        recur_gate,
        input_gate,
        flops=4 * tokens * channels * channels,
    )
    ends = lax.all_gather(end, "seq")
    column_pieces, ends = together((column_pieces, ends))
    projection = lax.all_gather(rotated(column_block, column_pieces, place_index), "seq")
    if columns % 128:
        projection = jnp.moveaxis(projection, 0, 1).reshape(1, head_count * channels, width)
    gate_pre = jnp.dot(normed, gate_proj, preferred_element_type=f32)
    states, mixed_low, entry = call(
        mix,
        [struct(tokens, channels), struct(tokens, channels, kind=bf16), struct(1, channels)],
        [],
        gate_pre,
        local_states,
        products,
        seg_ends,
        ends,
        here,
        scalars=1,
    )
    first = gather_first(mixed_low)
    second = gather_second(first)
    d_hidden = jnp.einsum("td,fd->tf", cotangent, ffn_down, preferred_element_type=f32)
    second, d_hidden = together((second, d_hidden))
    residual, normed_two, inverse_two = residual_norm(
        mixed_low,
        (*first, *second),
        projection,
        block_in,
        post_gain[None, :],
        place_index,
    )
    ffn_gpre = jnp.dot(normed_two, ffn_gate, preferred_element_type=f32)
    ffn_upre = jnp.dot(normed_two, ffn_up, preferred_element_type=f32)
    value, slope = gelu_parts(ffn_gpre)
    hidden = (value * ffn_upre).astype(bf16)
    d_gpre = (d_hidden * ffn_upre * slope).astype(bf16)
    d_upre = (d_hidden * value).astype(bf16)
    d_normed_two = jnp.einsum(
        "tf,df->td", d_gpre, ffn_gate, preferred_element_type=f32
    ) + jnp.einsum("tf,df->td", d_upre, ffn_up, preferred_element_type=f32)
    d_normed_two = d_normed_two.astype(bf16)
    d_normed_two, hidden, d_gpre, d_upre = together((d_normed_two, hidden, d_gpre, d_upre))
    first = scatter_first(d_normed_two)
    grad_ffn = weight_grads([(normed_two, d_gpre), (normed_two, d_upre), (cotangent, hidden)])
    first, grad_ffn = together((first, grad_ffn))
    grad_ffn = lax.psum_scatter(grad_ffn, "seq", scatter_dimension=0, tiled=True)
    second = scatter_second(d_normed_two, first)
    ffn_out = jnp.dot(hidden, ffn_down, preferred_element_type=f32).astype(bf16)
    second, ffn_out = together((second, ffn_out))
    d_normed_two = added(mine(d_normed_two), *second)
    d_norm_part, grad_postgain = norm_back(mine(residual), mine(inverse_two), post_gain, d_normed_two)
    d_resid = mine(cotangent).astype(f32) + d_norm_part
    d_out_share = d_resid.astype(bf16)
    first = gather_first(d_out_share)
    first, ffn_out = together((first, ffn_out))
    second = gather_second(first)
    half = tokens // 2
    ffn_halves = [ffn_out[:half], ffn_out[half:]]
    turn_one = [line_turn(1, ffn_halves[0])]
    d_out_low = assembled(d_out_share, first, second, place_index, bf16)
    d_out_low, ffn_halves[1] = together((d_out_low, ffn_halves[1]))
    turn_one.append(line_turn(1, ffn_halves[1]))
    d_mixed = jnp.einsum("td,cd->tc", d_out_low, out_proj, preferred_element_type=f32)
    sent = added(ffn_halves[0], turn_one[0]).astype(bf16)
    d_mixed, sent = together((d_mixed, sent))
    turn_two = [line_turn(2, sent)]
    d_gate_low, grad_local, grad_prod, grad_segs, grad_end = call(
        backward_scan,
        [
            struct(tokens, channels, kind=bf16),
            struct(*slabs),
            struct(*slabs),
            struct(2 * segments, channels),
            struct(1, channels),
        ],
        [pltpu.VMEM(slabs, f32), pltpu.VMEM(slabs, f32)],
        d_mixed,
        gate_pre,
        states,
        recur_rate,
        soft,
    )
    backs = lax.all_gather(grad_end, "seq")
    sent = added(ffn_halves[1], turn_one[1]).astype(bf16)
    backs, sent = together((backs, sent))
    turn_two.append(line_turn(2, sent))
    d_both, d_branch, head_rows, decay_sums, taps_sums = call(
        backward_terms,
        [
            struct(tokens, 2 * channels, kind=bf16),
            struct(tokens, channels),
            struct(8, channels),
            struct(8, channels),
            struct(8 * tap_count, channels),
        ],
        [
            pltpu.VMEM((tokens + 8, channels), f32),
            pltpu.VMEM((tokens + 8, channels), f32),
            pltpu.VMEM((tokens + 8, channels), f32),
        ],
        grad_local,
        grad_prod,
        grad_segs,
        ends,
        backs,
        recur_rate,
        input_rate,
        conv_low,
        states,
        entry,
        soft,
        slide,
        conv_taps,
        branch_in,
        halo,
        gates,
        here,
        scalars=1,
        flops=4 * tokens * channels * channels,
    )
    sent = added(ffn_halves[0], turn_two[0]).astype(bf16)
    head_rows, d_branch, d_both, sent = together((head_rows, d_branch, d_both, sent))
    later_rows = lax.ppermute(head_rows, "seq", backward_pairs)
    turn_three = [line_turn(3, sent)]
    d_branch_low = (d_branch + jnp.pad(later_rows, ((tokens - 8, 0), (0, 0)))).astype(bf16)
    d_normed = jnp.einsum("tc,dc->td", d_gate_low, gate_proj, preferred_element_type=f32) + jnp.einsum(
        "tc,dc->td", d_branch_low, input_proj, preferred_element_type=f32
    )
    d_normed = d_normed.astype(bf16)
    d_normed, conv_low, d_both = together((d_normed, conv_low, d_both))
    first = scatter_first(d_normed)
    packed = gate_grads(conv_low, d_both, taps_sums, decay_sums, blocks, seq_count, width)
    grad_rest = weight_grads([(normed, d_gate_low), (normed, d_branch_low), (d_out_low, mixed_low)], packed)
    first, grad_rest, turn_three, turn_two = together((first, grad_rest, turn_three, turn_two))
    second = scatter_second(d_normed, first)
    sent = added(ffn_halves[1], turn_two[1]).astype(bf16)
    second, sent = together((second, sent))
    turn_three.append(line_turn(3, sent))
    grad_rest = lax.psum_scatter(grad_rest, "seq", scatter_dimension=0, tiled=True)
    d_normed = added(mine(d_normed), *second)
    inputs = mine(block_in).astype(f32)
    inverse_one = inverse_rms(inputs)
    d_inputs, grad_pregain = norm_back(inputs, inverse_one, pre_gain, d_normed)
    grad_input = d_resid + d_inputs
    first = gather_first(grad_input.astype(bf16))
    gains = jnp.stack([grad_pregain, grad_postgain])
    gain_pieces = exchanged(lambda k: gains)
    second = gather_second(first)
    block_out = jnp.concatenate(
        [
            residual[half * h : half * (h + 1)] + added(ffn_halves[h], turn_one[h], turn_two[h], turn_three[h])
            for h in range(2)
        ],
        axis=0,
    ).astype(bf16)
    second, block_out = together((second, block_out))
    gains = jnp.sum(lax.all_gather(sum(gain_pieces, gains), "seq"), axis=0)
    gain_share = width // seq_count
    gains = lax.dynamic_slice_in_dim(gains, seq_index * gain_share, gain_share, 1)
    grad_ffn = grad_ffn.astype(f32)
    grad_ffn = (
        grad_ffn[:, :hidden_units],
        grad_ffn[:, hidden_units : 2 * hidden_units],
        grad_ffn[:, 2 * hidden_units :].T,
    )
    second, grad_rest, grad_ffn = together((second, grad_rest, grad_ffn))
    grad_input = assembled(grad_input, first, second, place_index, f32)
    grad_rest = grad_rest.astype(f32)
    packed = grad_rest[:, 3 * channels :]
    patch = block_width // seq_count
    kept = channels // seq_count
    small = packed[: blocks * patch, : 2 * block_width].reshape(blocks, patch, 2 * block_width)
    return (
        block_out,
        grad_input,
        gains[0],
        grad_rest[:, :channels],
        grad_rest[:, channels : 2 * channels],
        packed[blocks * patch : blocks * patch + tap_count, :kept],
        small[:, :, :block_width],
        small[:, :, block_width:],
        packed[blocks * patch + tap_count, :kept],
        grad_rest[:, 2 * channels : 3 * channels].T,
        gains[1],
        *grad_ffn,
    )


def solution(mesh):
    placed = (
        P("seq", None),
        P(),
        P(None, "head"),
        P(None, "head"),
        P(None, "head"),
        P("head", None, None),
        P("head", None, None),
        P("head"),
        P("head", None),
        P(),
        P(None, "head"),
        P(None, "head"),
        P("head", None),
        P("seq", None),
    )
    return jax.shard_map(
        local,
        mesh=mesh,
        in_specs=placed,
        out_specs=(
            P("seq", None),
            P("seq", None),
            P("seq"),
            P("seq", "head"),
            P("seq", "head"),
            P(None, ("head", "seq")),
            P("head", "seq", None),
            P("head", "seq", None),
            P(("head", "seq")),
            P("head", "seq"),
            P("seq"),
            P("seq", "head"),
            P("seq", "head"),
            P("head", "seq"),
        ),
        check_vma=False,
    )
```

```python
import jax
import jax.numpy as jnp
from jax import lax
from jax.experimental import pallas as pl
from jax.experimental.pallas import tpu as pltpu
from jax.sharding import PartitionSpec as P

epsilon = 1e-06
sharpness = 8.0
segments = 8
rows_at_once = 32
root_two_over_pi = 0.7978845608028654
cubic = 0.044715
f32 = jnp.float32
bf16 = jnp.bfloat16


def call(body, out_shape, scratch, *operands, scalars=0, flops=0):
    vectors = len(operands) - scalars
    moved = sum(x.size * x.dtype.itemsize for x in (*operands, *out_shape))
    return pl.pallas_call(
        body,
        out_shape=out_shape,
        in_specs=[pl.BlockSpec(memory_space=pltpu.VMEM)] * vectors
        + [pl.BlockSpec(memory_space=pltpu.SMEM)] * scalars,
        out_specs=[pl.BlockSpec(memory_space=pltpu.VMEM)] * len(out_shape),
        scratch_shapes=scratch,
        compiler_params=pltpu.CompilerParams(vmem_limit_bytes=26 << 20),
        cost_estimate=pl.CostEstimate(flops=1000, bytes_accessed=1000, transcendentals=0),
    )(*operands)


def split(ref, at, value):
    for j in range(ref.shape[0]):
        ref[j, at, :] = value[:, 128 * j : 128 * (j + 1)]


def joined(ref, at):
    return jnp.concatenate([ref[j, at, :] for j in range(ref.shape[0])], axis=1)


def over_rows(tokens, body):
    @pl.loop(0, tokens // rows_at_once)
    def _(step):
        body(pl.multiple_of(step * rows_at_once, rows_at_once))


def minus_expm1(v):
    series = 1.0 / 5040.0
    for term in (720.0, 120.0, 24.0, 6.0, 2.0, 1.0):
        series = series * v + 1.0 / term
    return jnp.where(v > -0.25, -v * series, 1.0 - jnp.exp(v))


def gelu_parts(v):
    bent = jnp.tanh(root_two_over_pi * (v + cubic * v * v * v))
    half = 0.5 * (1.0 + bent)
    slope = half + 0.5 * v * (1.0 - bent * bent) * root_two_over_pi * (1.0 + 3.0 * cubic * v * v)
    return v * half, slope


def forward_scan(
    branch_ref, halo_ref, taps_ref, soft_ref, recur_gate_ref, input_gate_ref,
    conv_ref, recur_ref, input_ref, local_ref, prod_ref, seg_ref, end_ref, gates_ref,
    padded, pre, decay, drive,
):
    tokens, channels = branch_ref.shape
    taps = taps_ref.shape[0]
    steps = tokens // segments
    blocks, width, _ = recur_gate_ref.shape
    gates_ref[...] = jnp.zeros((channels, 2 * channels), bf16)
    for b in range(blocks):
        rows = pl.ds(b * width, width)
        gates_ref[rows, b * width : (b + 1) * width] = recur_gate_ref[b]
        gates_ref[rows, channels + b * width : channels + (b + 1) * width] = input_gate_ref[b]
    padded[0:8, :] = halo_ref[...].astype(f32)

    def fill(row):
        padded[pl.ds(row + 8, rows_at_once), :] = branch_ref[pl.ds(row, rows_at_once), :].astype(f32)

    over_rows(tokens, fill)

    def convolve(row):
        window = padded[pl.ds(row, rows_at_once + 8), :]
        total = taps_ref[0:1, :] * window[8:, :]
        for k in range(1, taps):
            total = total + taps_ref[k : k + 1, :] * window[8 - k : 8 - k + rows_at_once, :]
        conv_ref[pl.ds(row, rows_at_once), :] = total.astype(bf16)

    over_rows(tokens, convolve)
    pre[...] = jnp.dot(conv_ref[...], gates_ref[...], preferred_element_type=f32)

    def terms(row):
        at = pl.ds(row, rows_at_once)
        recur = jax.nn.sigmoid(pre[at, 0:channels])
        inward = jax.nn.sigmoid(pre[at, channels : 2 * channels])
        log_decay = -sharpness * recur * soft_ref[...]
        recur_ref[at, :] = recur
        input_ref[at, :] = inward
        split(decay, at, jnp.exp(log_decay))
        split(drive, at, jnp.sqrt(minus_expm1(2.0 * log_decay)) * inward * conv_ref[at, :].astype(f32))

    over_rows(tokens, terms)

    slabs = channels // 128

    def step(i, carried):
        at = pl.ds(i, segments, stride=steps)
        new = []
        for j in range(slabs):
            state, product = carried[j]
            a = decay[j, at, :]
            state = a * state + drive[j, at, :]
            product = a * product
            local_ref[j, at, :] = state
            prod_ref[j, at, :] = product
            new.append((state, product))
        return tuple(new)

    start = ((jnp.zeros((segments, 128), f32), jnp.ones((segments, 128), f32)),) * slabs
    last = lax.fori_loop(0, steps, step, start, unroll=4)
    state = jnp.concatenate([pair[0] for pair in last], axis=1)
    product = jnp.concatenate([pair[1] for pair in last], axis=1)
    seg_ref[0:segments, :] = product
    seg_ref[segments : 2 * segments, :] = state
    whole = jnp.ones((1, channels), f32)
    end = jnp.zeros((1, channels), f32)
    for s in range(segments):
        end = product[s : s + 1, :] * end + state[s : s + 1, :]
        whole = product[s : s + 1, :] * whole
    end_ref[0:1, :] = whole
    end_ref[1:2, :] = end


def mix(gate_ref, local_ref, prod_ref, seg_ref, ends_ref, index_ref, states_ref, mixed_ref, entry_ref):
    tokens, channels = gate_ref.shape
    steps = tokens // segments
    index = index_ref[0]
    carry = jnp.zeros((1, channels), f32)
    for j in range(ends_ref.shape[0]):
        new = ends_ref[j, 0:1, :] * carry + ends_ref[j, 1:2, :]
        carry = jnp.where(j < index, new, carry)
    entry_ref[...] = carry
    for s in range(segments):
        held = carry

        @pl.loop(0, steps // rows_at_once)
        def _(i):
            at = pl.ds(pl.multiple_of(s * steps + i * rows_at_once, rows_at_once), rows_at_once)
            states = joined(local_ref, at) + joined(prod_ref, at) * held
            states_ref[at, :] = states
            gate, _ = gelu_parts(gate_ref[at, :])
            mixed_ref[at, :] = (gate * states).astype(bf16)

        carry = seg_ref[s : s + 1, :] * carry + seg_ref[segments + s : segments + s + 1, :]


def backward_scan(
    d_mixed_ref, gate_ref, states_ref, recur_ref, soft_ref,
    d_gate_ref, local_ref, prod_ref, seg_ref, end_ref,
    decay, d_state,
):
    tokens, channels = gate_ref.shape
    steps = tokens // segments

    def terms(row):
        at = pl.ds(row, rows_at_once)
        d_mixed = d_mixed_ref[at, :].astype(f32)
        value, slope = gelu_parts(gate_ref[at, :])
        d_gate_ref[at, :] = (d_mixed * states_ref[at, :] * slope).astype(bf16)
        split(d_state, at, d_mixed * value)
        split(decay, at, jnp.exp(-sharpness * recur_ref[at, :] * soft_ref[...]))

    over_rows(tokens, terms)

    slabs = channels // 128

    def step(k, carried):
        at = pl.ds(steps - 1 - k, segments, stride=steps)
        new = []
        for j in range(slabs):
            into, reach = carried[j]
            a = decay[j, at, :]
            grad = d_state[j, at, :] + into
            local_ref[j, at, :] = grad
            prod_ref[j, at, :] = reach
            new.append((a * grad, a * reach))
        return tuple(new)

    start = ((jnp.zeros((segments, 128), f32), jnp.ones((segments, 128), f32)),) * slabs
    last = lax.fori_loop(0, steps, step, start, unroll=4)
    into = jnp.concatenate([pair[0] for pair in last], axis=1)
    reach = jnp.concatenate([pair[1] for pair in last], axis=1)
    seg_ref[0:segments, :] = reach
    seg_ref[segments : 2 * segments, :] = into
    end = jnp.zeros((1, channels), f32)
    for s in reversed(range(segments)):
        end = reach[s : s + 1, :] * end + into[s : s + 1, :]
    end_ref[...] = end


def backward_terms(
    local_ref, prod_ref, seg_ref, ends_ref, backs_ref, recur_ref, input_ref, conv_ref, states_ref, entry_ref,
    soft_ref, slide_ref, taps_ref, branch_ref, halo_ref, gates_ref, index_ref,
    d_both_ref, d_branch_ref, head_ref, decay_sum_ref, taps_sum_ref,
    before, d_conv, padded,
):
    tokens, channels = states_ref.shape
    taps = taps_ref.shape[0]
    steps = tokens // segments
    index = index_ref[0]
    padded[0:8, :] = halo_ref[...].astype(f32)
    before[0:8, :] = jnp.broadcast_to(entry_ref[...], (8, channels))
    carry = jnp.zeros((1, channels), f32)
    for j in reversed(range(ends_ref.shape[0])):
        new = ends_ref[j, 0:1, :] * carry + backs_ref[j, 0:1, :]
        carry = jnp.where(j > index, new, carry)
    decay_sum_ref[...] = jnp.zeros((8, channels), f32)
    taps_sum_ref[...] = jnp.zeros((8 * taps, channels), f32)

    def fill(row):
        padded[pl.ds(row + 8, rows_at_once), :] = branch_ref[pl.ds(row, rows_at_once), :].astype(f32)
        before[pl.ds(row + 8, rows_at_once), :] = states_ref[pl.ds(row, rows_at_once), :]

    over_rows(tokens, fill)
    for s in reversed(range(segments)):
        held = carry

        @pl.loop(0, steps // rows_at_once)
        def _(i):
            row = pl.multiple_of(s * steps + i * rows_at_once, rows_at_once)
            at = pl.ds(row, rows_at_once)
            grad = joined(local_ref, at) + joined(prod_ref, at) * held
            recur = recur_ref[at, :]
            inward = input_ref[at, :]
            conv = conv_ref[at, :].astype(f32)
            log_decay = -sharpness * recur * soft_ref[...]
            decay = jnp.exp(log_decay)
            root = jnp.sqrt(minus_expm1(2.0 * log_decay))
            previous = before[pl.ds(row, rows_at_once + 8), :][7 : 7 + rows_at_once, :]
            push = grad * inward
            total = decay * (grad * previous - push * decay * conv / root)
            rate = recur * total
            d_both_ref[at, 0:channels] = (-sharpness * soft_ref[...] * (1.0 - recur) * rate).astype(bf16)
            d_both_ref[at, channels : 2 * channels] = (push * root * conv * (1.0 - inward)).astype(bf16)
            d_conv[at, :] = push * root
            decay_sum_ref[...] += jnp.sum(rate.reshape(rows_at_once // 8, 8, channels), axis=0)

        carry = seg_ref[s : s + 1, :] * carry + seg_ref[segments + s : segments + s + 1, :]
    decay_sum_ref[...] = decay_sum_ref[...] * slide_ref[...]
    d_conv[0:tokens, :] += lax.dot_general(
        d_both_ref[...], gates_ref[...], (((1,), (1,)), ((), ())), preferred_element_type=f32
    )
    d_conv[tokens : tokens + 8, :] = jnp.zeros((8, channels), f32)
    first = jnp.concatenate([jnp.zeros((8, channels), f32), d_conv[0:8, :]], axis=0)
    head = taps_ref[0:1, :] * first[0:8, :]
    for k in range(1, taps):
        head = head + taps_ref[k : k + 1, :] * first[k : k + 8, :]
    head_ref[...] = head

    def finish(row):
        window = d_conv[pl.ds(row, rows_at_once + 8), :]
        now = window[0:rows_at_once, :]
        total = taps_ref[0:1, :] * now
        for k in range(1, taps):
            total = total + taps_ref[k : k + 1, :] * window[k : k + rows_at_once, :]
        d_branch_ref[pl.ds(row, rows_at_once), :] = total
        earlier = padded[pl.ds(row, rows_at_once + 8), :]
        for k in range(taps):
            product = now * earlier[8 - k : 8 - k + rows_at_once, :]
            taps_sum_ref[8 * k : 8 * k + 8, :] += jnp.sum(
                product.reshape(rows_at_once // 8, 8, channels), axis=0
            )

    over_rows(tokens, finish)


def place(me, own_ref, arrived, store):
    from_left, from_right, over, back, far = arrived
    for m, parts in enumerate(
        (
            (own_ref, from_right, back, far),
            (from_left, own_ref, from_right, over),
            (over, from_left, own_ref, from_right),
            (far, back, from_left, own_ref),
        )
    ):

        @pl.when(me == m)
        def _():
            for source, ref in enumerate(parts):
                store(source, ref)


def add_projection(
    own_ref, left_ref, right_ref, over_ref, back_ref, far_ref, weight_ref, inputs_ref, gain_ref, index_ref,
    residual_ref, normed_ref, inverse_ref,
    mixed, rows,
):
    tokens, channels = own_ref.shape
    columns = weight_ref.shape[2]
    step = pl.program_id(0)

    def store(source, ref):
        mixed[:, source * channels : (source + 1) * channels] = ref[...]

    @pl.when(step == 0)
    def _():
        place(index_ref[0], own_ref, (left_ref, right_ref, over_ref, back_ref, far_ref), store)

    total = inputs_ref[...].astype(f32) + jnp.dot(mixed[...], weight_ref[0], preferred_element_type=f32)
    residual_ref[...] = total
    rows[:, pl.ds(pl.multiple_of(step * columns, columns), columns)] = total

    @pl.when(step == pl.num_programs(0) - 1)
    def _():
        def normalise(row):
            at = pl.ds(row, rows_at_once)
            values = rows[at, :]
            inverse = inverse_rms(values)
            inverse_ref[at, :] = inverse
            normed_ref[at, :] = (values * inverse * gain_ref[...]).astype(bf16)

        over_rows(tokens, normalise)


def residual_norm(own, arrived, weight, inputs, gain, index):
    tokens, channels = own.shape
    blocks, depth, columns = weight.shape
    width = inputs.shape[1]

    def whole(*dims):
        return pl.BlockSpec(dims, lambda j: (0,) * len(dims))

    return pl.pallas_call(
        add_projection,
        grid=(blocks,),
        in_specs=[whole(tokens, channels)] * 6
        + [
            pl.BlockSpec((1, depth, columns), lambda j: (j, 0, 0)),
            pl.BlockSpec((tokens, columns), lambda j: (0, j)),
            whole(1, width),
            pl.BlockSpec(memory_space=pltpu.SMEM),
        ],
        out_specs=[pl.BlockSpec((tokens, columns), lambda j: (0, j)), whole(tokens, width), whole(tokens, 1)],
        out_shape=[
            jax.ShapeDtypeStruct((tokens, width), f32),
            jax.ShapeDtypeStruct((tokens, width), bf16),
            jax.ShapeDtypeStruct((tokens, 1), f32),
        ],
        scratch_shapes=[pltpu.VMEM((tokens, depth), bf16), pltpu.VMEM((tokens, width), f32)],
        compiler_params=pltpu.CompilerParams(vmem_limit_bytes=48 << 20),
        cost_estimate=pl.CostEstimate(
            flops=2 * tokens * depth * width,
            bytes_accessed=2 * (depth * width + 5 * tokens * width),
            transcendentals=0,
        ),
    )(own, *arrived, weight, inputs, gain, index)


def assembled(own, first, second, index, kind):
    size, width = own.shape
    peers = lax.axis_size("head")

    def body(own_ref, left_ref, right_ref, over_ref, back_ref, far_ref, index_ref, out_ref):
        def store(source, ref):
            out_ref[source * size : (source + 1) * size, :] = ref[...].astype(kind)

        place(index_ref[0], own_ref, (left_ref, right_ref, over_ref, back_ref, far_ref), store)

    return call(
        body,
        [jax.ShapeDtypeStruct((peers * size, width), kind)],
        [],
        own,
        *first,
        *second,
        index,
        scalars=1,
    )[0]


def weight_grads(products, extra=None):
    lefts = [left for left, _ in products]
    rights = [right for _, right in products]
    tokens, width = lefts[0].shape
    count = len(products)
    spans = [right.shape[1] for right in rights]
    total = sum(spans) + (0 if extra is None else extra.shape[1])
    block = 256

    def body(*refs):
        left_refs, right_refs, out_ref = refs[:count], refs[count : 2 * count], refs[-1]
        place = 0
        for left_ref, right_ref in zip(left_refs, right_refs, strict=True):
            span = right_ref.shape[1]
            out_ref[:, place : place + span] = lax.dot_general(
                left_ref[...], right_ref[...], (((0,), (0,)), ((), ())), preferred_element_type=f32
            ).astype(bf16)
            place += span
        if extra is not None:
            out_ref[:, place:] = refs[2 * count][...]

    extras = [] if extra is None else [extra]
    return pl.pallas_call(
        body,
        grid=(width // block,),
        in_specs=[pl.BlockSpec((tokens, block), lambda i: (0, i))] * count
        + [pl.BlockSpec((tokens, span), lambda i: (0, 0)) for span in spans]
        + [pl.BlockSpec((block, e.shape[1]), lambda i: (i, 0)) for e in extras],
        out_specs=pl.BlockSpec((block, total), lambda i: (i, 0)),
        out_shape=jax.ShapeDtypeStruct((width, total), bf16),
        compiler_params=pltpu.CompilerParams(vmem_limit_bytes=48 << 20),
        cost_estimate=pl.CostEstimate(
            flops=2 * tokens * width * total, bytes_accessed=2 * width * total, transcendentals=0
        ),
    )(*lefts, *rights, *extras)


def finish_ffn(summed, count):
    rows, width = summed.shape
    span = width // count

    def body(in_ref, *out_refs):
        for k, ref in enumerate(out_refs):
            part = in_ref[:, k * span : (k + 1) * span].astype(f32)
            ref[...] = part.T if k == count - 1 else part

    shapes = [jax.ShapeDtypeStruct((rows, span), f32)] * (count - 1)
    return call(body, [*shapes, jax.ShapeDtypeStruct((span, rows), f32)], [], summed)


def finish_rest(summed, channels, blocks, block_width, taps, owners):
    rows = summed.shape[0]
    patch, kept = block_width // owners, channels // owners

    def body(in_ref, gate_ref, input_ref, out_ref, taps_ref, recur_ref, inward_ref, decay_ref):
        gate_ref[...] = in_ref[:, 0:channels].astype(f32)
        input_ref[...] = in_ref[:, channels : 2 * channels].astype(f32)
        out_ref[...] = in_ref[:, 2 * channels : 3 * channels].astype(f32).T
        small = in_ref[:, 3 * channels :].astype(f32)
        _, lanes = packed_shape(blocks, block_width, taps, owners, owners * rows)
        groups = -(-2 * block_width // lanes)
        for b in range(blocks):
            parts = []
            for g in range(groups):
                row = (g * blocks + b) * patch
                parts.append(small[row : row + patch, 0 : min(lanes, 2 * block_width - g * lanes)])
            both = jnp.concatenate(parts, axis=1)
            recur_ref[b] = both[:, 0:block_width]
            inward_ref[b] = both[:, block_width : 2 * block_width]
        used = groups * blocks * patch
        taps_ref[...] = small[used : used + taps, 0:kept]
        decay_ref[...] = small[used + taps : used + taps + 1, 0:kept]

    shapes = [
        (rows, channels),
        (rows, channels),
        (channels, rows),
        (taps, kept),
        (blocks, patch, block_width),
        (blocks, patch, block_width),
        (1, kept),
    ]
    return call(body, [jax.ShapeDtypeStruct(shape, f32) for shape in shapes], [], summed)


def add_last(base, last):
    cut = last[0].shape[0]

    def body(base_ref, first_ref, second_ref, out_ref):
        out_ref[0:cut, :] = (base_ref[0:cut, :] + first_ref[...].astype(f32)).astype(bf16)
        out_ref[cut:, :] = (base_ref[cut:, :] + second_ref[...].astype(f32)).astype(bf16)

    return call(body, [jax.ShapeDtypeStruct(base.shape, bf16)], [], base, *last)[0]


def packed_shape(blocks, width, taps, owners, rows):
    groups = -(-2 * width // 128)
    if groups * blocks * (width // owners) + taps + 1 <= rows // owners:
        return 128, 128
    return groups * 128, 2 * width


def gate_grads(conv_low, d_both, taps_sums, decay_sums, blocks, owners, rows):
    channels = conv_low.shape[1]
    taps = taps_sums.shape[0] // 8
    width = channels // blocks
    patch, kept, span = width // owners, channels // owners, rows // owners
    columns, lanes = packed_shape(blocks, width, taps, owners, rows)

    def body(conv_ref, both_ref, taps_ref, decay_ref, out_ref):
        out_ref[...] = jnp.zeros((rows, columns), bf16)
        dense = lax.dot_general(
            conv_ref[...], both_ref[...], (((0,), (0,)), ((), ())), preferred_element_type=f32
        )
        sums = [jnp.sum(taps_ref[8 * k : 8 * k + 8, :], axis=0, keepdims=True) for k in range(taps)]
        sums.append(jnp.sum(decay_ref[...], axis=0, keepdims=True))
        sums = jnp.concatenate(sums, axis=0).astype(bf16)
        for b in range(blocks):
            at = slice(b * width, (b + 1) * width)
            recur = dense[at, b * width : (b + 1) * width].astype(bf16)
            inward = dense[at, channels + b * width : channels + (b + 1) * width].astype(bf16)
            both = jnp.concatenate([recur, inward], axis=1)
            for s in range(owners):
                mine = both[s * patch : (s + 1) * patch, :]
                for g, start in enumerate(range(0, 2 * width, lanes)):
                    row = s * span + (g * blocks + b) * patch
                    part = mine[:, start : start + lanes]
                    out_ref[row : row + patch, 0 : part.shape[1]] = part
        used = -(-2 * width // lanes) * blocks * patch
        for s in range(owners):
            row = s * span + used
            out_ref[row : row + taps + 1, 0:kept] = sums[:, s * kept : (s + 1) * kept]

    return call(
        body,
        [jax.ShapeDtypeStruct((rows, columns), bf16)],
        [],
        conv_low,
        d_both,
        taps_sums,
        decay_sums,
        flops=4 * conv_low.shape[0] * channels * channels,
    )[0]


def shifted(count, by):
    return [(i, (i + by) % count) for i in range(count)]


def exchanged(blocks):
    peers = lax.axis_size("head")
    return [lax.ppermute(blocks(k), "head", shifted(peers, k)) for k in range(1, peers)]


def block_of(array, where, dim):
    peers = lax.axis_size("head")
    size = array.shape[dim] // peers
    return lax.dynamic_slice_in_dim(array, (where % peers) * size, size, dim)


def shard(array, where):
    return block_of(array, where, 0)


def added(first, *others):
    total = first.astype(f32)
    for part in others:
        total = total + part.astype(f32)
    return total


def line_pairs(by):
    peers = lax.axis_size("head")
    return [(i, i + by) for i in range(peers) if 0 <= i + by < peers]


def scatter_first(low):
    me = lax.axis_index("head")
    across = shard(low, me + 2)
    return (
        lax.ppermute(across, "head", [(0, 1), (1, 2)]),
        lax.ppermute(across, "head", [(3, 2), (2, 1)]),
        lax.ppermute(shard(low, 3 - me), "head", [(0, 2), (3, 1)]),
    )


def scatter_second(low, first):
    me = lax.axis_index("head")
    from_left, from_right, far = first
    none = jnp.zeros_like(far)
    to_right = added(shard(low, me + 1), from_left, jnp.where(me == 2, far, none)).astype(bf16)
    to_left = added(shard(low, me - 1), from_right, jnp.where(me == 1, far, none)).astype(bf16)
    return lax.ppermute(to_right, "head", line_pairs(1)), lax.ppermute(to_left, "head", line_pairs(-1))


def gather_first(own):
    return lax.ppermute(own, "head", line_pairs(1)), lax.ppermute(own, "head", line_pairs(-1))


def gather_second(first):
    me = lax.axis_index("head")
    from_left, from_right = first
    over = jnp.where(me == 1, from_left, from_right)
    back = jnp.where(me == 1, from_right, from_left)
    return (
        lax.ppermute(over, "head", [(1, 2), (2, 1)]),
        lax.ppermute(back, "head", [(1, 0), (2, 3)]),
        lax.ppermute(over, "head", [(1, 3), (2, 0)]),
    )


def line_turn(turn, sent):
    peers = lax.axis_size("head")
    return lax.ppermute(sent, "head", [(turn - 1, turn), (peers - turn, peers - turn - 1)])


together = lax.optimization_barrier


def inverse_rms(values):
    return lax.rsqrt(jnp.mean(values * values, axis=-1, keepdims=True) + epsilon)


def norm_back(values, inverse, scales, grad):
    unit = values * inverse
    scaled = grad * scales
    inner = jnp.mean(scaled * unit, axis=-1, keepdims=True)
    return inverse * (scaled - unit * inner), jnp.sum(grad * unit, axis=0)


def local(
    block_in,
    pre_gain,
    gate_proj,
    input_proj,
    conv_taps,
    recur_gate,
    input_gate,
    decay_param,
    out_proj,
    post_gain,
    ffn_gate,
    ffn_up,
    ffn_down,
    cotangent,
):
    tokens, width = block_in.shape
    channels = gate_proj.shape[1]
    blocks, block_width, _ = recur_gate.shape
    tap_count = conv_taps.shape[0]
    hidden_units = ffn_gate.shape[1]
    seq_count, seq_index = lax.axis_size("seq"), lax.axis_index("seq")
    head_count, head_index = lax.axis_size("head"), lax.axis_index("head")
    share = tokens // head_count
    slabs = (channels // 128, tokens, 128)
    here = seq_index.astype(jnp.int32).reshape(1)
    place_index = head_index.astype(jnp.int32).reshape(1)
    forward_pairs = [(i, i + 1) for i in range(seq_count - 1)]
    backward_pairs = [(i + 1, i) for i in range(seq_count - 1)]

    def mine(rows):
        return lax.dynamic_slice_in_dim(rows, head_index * share, share, 0)

    def struct(*dims, kind=f32):
        return jax.ShapeDtypeStruct(dims, kind)

    halo_in = lax.ppermute(block_in[tokens - 8 :], "seq", forward_pairs)
    columns = width // seq_count
    column_block = lax.dynamic_slice_in_dim(out_proj, seq_index * columns, columns, 1)
    column_block = lax.all_gather(column_block, "head").reshape(head_count * channels, columns)
    soft = jax.nn.softplus(-decay_param)[None, :]
    slide = sharpness * jax.nn.sigmoid(-decay_param)[None, :]

    def normalise(rows):
        values = rows.astype(f32)
        return (values * inverse_rms(values) * pre_gain).astype(bf16)

    normed = normalise(block_in)
    branch_in = jnp.dot(normed, input_proj, preferred_element_type=f32).astype(bf16)
    halo = jnp.dot(normalise(halo_in), input_proj, preferred_element_type=f32).astype(bf16)
    conv_low, recur_rate, input_rate, local_states, products, seg_ends, end, gates = call(
        forward_scan,
        [
            struct(tokens, channels, kind=bf16),
            struct(tokens, channels),
            struct(tokens, channels),
            struct(*slabs),
            struct(*slabs),
            struct(2 * segments, channels),
            struct(2, channels),
            struct(channels, 2 * channels, kind=bf16),
        ],
        [
            pltpu.VMEM((tokens + 8, channels), f32),
            pltpu.VMEM((tokens, 2 * channels), f32),
            pltpu.VMEM(slabs, f32),
            pltpu.VMEM(slabs, f32),
        ],
        branch_in,
        halo,
        conv_taps,
        soft,
        recur_gate,
        input_gate,
        flops=4 * tokens * channels * channels,
    )
    ends = lax.all_gather(end, "seq")
    gate_pre = jnp.dot(normed, gate_proj, preferred_element_type=f32)
    states, mixed_low, entry = call(
        mix,
        [struct(tokens, channels), struct(tokens, channels, kind=bf16), struct(1, channels)],
        [],
        gate_pre,
        local_states,
        products,
        seg_ends,
        ends,
        here,
        scalars=1,
    )
    column_block, mixed_low = together((column_block, mixed_low))
    projection = lax.all_gather(column_block, "seq")
    if columns % 128:
        projection = jnp.moveaxis(projection, 0, 1).reshape(1, head_count * channels, width)
    first = gather_first(mixed_low)
    second = gather_second(first)
    d_hidden = jnp.einsum("td,fd->tf", cotangent, ffn_down, preferred_element_type=f32)
    second, d_hidden = together((second, d_hidden))
    residual, normed_two, inverse_two = residual_norm(
        mixed_low,
        (*first, *second),
        projection,
        block_in,
        post_gain[None, :],
        place_index,
    )
    ffn_gpre = jnp.dot(normed_two, ffn_gate, preferred_element_type=f32)
    ffn_upre = jnp.dot(normed_two, ffn_up, preferred_element_type=f32)
    value, slope = gelu_parts(ffn_gpre)
    hidden = (value * ffn_upre).astype(bf16)
    d_gpre = (d_hidden * ffn_upre * slope).astype(bf16)
    d_upre = (d_hidden * value).astype(bf16)
    d_normed_two = jnp.einsum(
        "tf,df->td", d_gpre, ffn_gate, preferred_element_type=f32
    ) + jnp.einsum("tf,df->td", d_upre, ffn_up, preferred_element_type=f32)
    d_normed_two = d_normed_two.astype(bf16)
    d_normed_two, hidden, d_gpre, d_upre = together((d_normed_two, hidden, d_gpre, d_upre))
    first = scatter_first(d_normed_two)
    grad_ffn = weight_grads([(normed_two, d_gpre), (normed_two, d_upre), (cotangent, hidden)])
    first, grad_ffn = together((first, grad_ffn))
    grad_ffn = lax.psum_scatter(grad_ffn, "seq", scatter_dimension=0, tiled=True)
    second = scatter_second(d_normed_two, first)
    ffn_out = jnp.dot(hidden, ffn_down, preferred_element_type=f32).astype(bf16)
    second, ffn_out = together((second, ffn_out))
    d_normed_two = added(mine(d_normed_two), *second)
    d_norm_part, grad_postgain = norm_back(mine(residual), mine(inverse_two), post_gain, d_normed_two)
    d_resid = mine(cotangent).astype(f32) + d_norm_part
    d_out_share = d_resid.astype(bf16)
    first = gather_first(d_out_share)
    first, ffn_out = together((first, ffn_out))
    second = gather_second(first)
    cut = tokens * 5 // 8
    ffn_halves = [ffn_out[:cut], ffn_out[cut:]]
    turn_one = [line_turn(1, ffn_halves[0])]
    d_out_low = assembled(d_out_share, first, second, place_index, bf16)
    d_out_low, ffn_halves[1] = together((d_out_low, ffn_halves[1]))
    turn_one.append(line_turn(1, ffn_halves[1]))
    d_mixed = jnp.einsum("td,cd->tc", d_out_low, out_proj, preferred_element_type=f32)
    sent = added(ffn_halves[0], turn_one[0]).astype(bf16)
    d_mixed, sent = together((d_mixed, sent))
    turn_two = [line_turn(2, sent)]
    d_gate_low, grad_local, grad_prod, grad_segs, grad_end = call(
        backward_scan,
        [
            struct(tokens, channels, kind=bf16),
            struct(*slabs),
            struct(*slabs),
            struct(2 * segments, channels),
            struct(1, channels),
        ],
        [pltpu.VMEM(slabs, f32), pltpu.VMEM(slabs, f32)],
        d_mixed,
        gate_pre,
        states,
        recur_rate,
        soft,
    )
    backs = lax.all_gather(grad_end, "seq")
    sent = added(ffn_halves[1], turn_one[1]).astype(bf16)
    backs, sent = together((backs, sent))
    turn_two.append(line_turn(2, sent))
    d_both, d_branch, head_rows, decay_sums, taps_sums = call(
        backward_terms,
        [
            struct(tokens, 2 * channels, kind=bf16),
            struct(tokens, channels),
            struct(8, channels),
            struct(8, channels),
            struct(8 * tap_count, channels),
        ],
        [
            pltpu.VMEM((tokens + 8, channels), f32),
            pltpu.VMEM((tokens + 8, channels), f32),
            pltpu.VMEM((tokens + 8, channels), f32),
        ],
        grad_local,
        grad_prod,
        grad_segs,
        ends,
        backs,
        recur_rate,
        input_rate,
        conv_low,
        states,
        entry,
        soft,
        slide,
        conv_taps,
        branch_in,
        halo,
        gates,
        here,
        scalars=1,
        flops=4 * tokens * channels * channels,
    )
    sent = added(ffn_halves[0], turn_two[0]).astype(bf16)
    head_rows, d_branch, d_both, sent = together((head_rows, d_branch, d_both, sent))
    later_rows = lax.ppermute(head_rows, "seq", backward_pairs)
    turn_three = [line_turn(3, sent)]
    d_branch_low = (d_branch + jnp.pad(later_rows, ((tokens - 8, 0), (0, 0)))).astype(bf16)
    d_normed = jnp.einsum("tc,dc->td", d_gate_low, gate_proj, preferred_element_type=f32) + jnp.einsum(
        "tc,dc->td", d_branch_low, input_proj, preferred_element_type=f32
    )
    d_normed = d_normed.astype(bf16)
    d_normed, conv_low, d_both = together((d_normed, conv_low, d_both))
    first = scatter_first(d_normed)
    packed = gate_grads(conv_low, d_both, taps_sums, decay_sums, blocks, seq_count, width)
    grad_rest = weight_grads([(normed, d_gate_low), (normed, d_branch_low), (d_out_low, mixed_low)], packed)
    first, grad_rest, turn_three, turn_two = together((first, grad_rest, turn_three, turn_two))
    second = scatter_second(d_normed, first)
    sent = added(ffn_halves[1], turn_two[1]).astype(bf16)
    turn_three.append(line_turn(3, sent))
    grad_rest = lax.psum_scatter(grad_rest, "seq", scatter_dimension=0, tiled=True)
    d_normed = added(mine(d_normed), *second)
    inputs = mine(block_in).astype(f32)
    inverse_one = inverse_rms(inputs)
    d_inputs, grad_pregain = norm_back(inputs, inverse_one, pre_gain, d_normed)
    grad_input = d_resid + d_inputs
    first = gather_first(grad_input.astype(bf16))
    gains = jnp.stack([grad_pregain, grad_postgain])
    gain_pieces = exchanged(lambda k: gains)
    base = residual + added(ffn_out, jnp.concatenate(turn_one), jnp.concatenate(turn_two))
    block_out = add_last(base, turn_three)
    grad_ffn = finish_ffn(grad_ffn, 3)
    first, block_out, grad_ffn = together((first, block_out, grad_ffn))
    second = gather_second(first)
    gains = jnp.sum(lax.all_gather(sum(gain_pieces, gains), "seq"), axis=0)
    gain_share = width // seq_count
    gains = lax.dynamic_slice_in_dim(gains, seq_index * gain_share, gain_share, 1)
    grad_rest, grad_ffn = together((grad_rest, grad_ffn))
    grad_input = assembled(grad_input, first, second, place_index, f32)
    grad_gate_proj, grad_input_proj, grad_out_proj, grad_taps, grad_recur, grad_inward, grad_decay = finish_rest(
        grad_rest, channels, blocks, block_width, tap_count, seq_count
    )
    return (
        block_out,
        grad_input,
        gains[0],
        grad_gate_proj,
        grad_input_proj,
        grad_taps,
        grad_recur,
        grad_inward,
        grad_decay[0],
        grad_out_proj,
        gains[1],
        *grad_ffn,
    )


def solution(mesh):
    placed = (
        P("seq", None),
        P(),
        P(None, "head"),
        P(None, "head"),
        P(None, "head"),
        P("head", None, None),
        P("head", None, None),
        P("head"),
        P("head", None),
        P(),
        P(None, "head"),
        P(None, "head"),
        P("head", None),
        P("seq", None),
    )
    return jax.shard_map(
        local,
        mesh=mesh,
        in_specs=placed,
        out_specs=(
            P("seq", None),
            P("seq", None),
            P("seq"),
            P("seq", "head"),
            P("seq", "head"),
            P(None, ("head", "seq")),
            P("head", "seq", None),
            P("head", "seq", None),
            P(("head", "seq")),
            P("head", "seq"),
            P("seq"),
            P("seq", "head"),
            P("seq", "head"),
            P("head", "seq"),
        ),
        check_vma=False,
    )
```

```python
import jax
import jax.numpy as jnp
from jax import lax
from jax.experimental import pallas as pl
from jax.experimental.pallas import tpu as pltpu
from jax.sharding import PartitionSpec as P

epsilon = 1e-06
sharpness = 8.0
segments = 8
rows_at_once = 32
root_two_over_pi = 0.7978845608028654
cubic = 0.044715
f32 = jnp.float32
bf16 = jnp.bfloat16


def call(body, out_shape, scratch, *operands, scalars=0, flops=0):
    vectors = len(operands) - scalars
    moved = sum(x.size * x.dtype.itemsize for x in (*operands, *out_shape))
    return pl.pallas_call(
        body,
        out_shape=out_shape,
        in_specs=[pl.BlockSpec(memory_space=pltpu.VMEM)] * vectors
        + [pl.BlockSpec(memory_space=pltpu.SMEM)] * scalars,
        out_specs=[pl.BlockSpec(memory_space=pltpu.VMEM)] * len(out_shape),
        scratch_shapes=scratch,
        compiler_params=pltpu.CompilerParams(vmem_limit_bytes=26 << 20),
        cost_estimate=pl.CostEstimate(flops=1000, bytes_accessed=1000, transcendentals=0),
    )(*operands)


def split(ref, at, value):
    for j in range(ref.shape[0]):
        ref[j, at, :] = value[:, 128 * j : 128 * (j + 1)]


def joined(ref, at):
    return jnp.concatenate([ref[j, at, :] for j in range(ref.shape[0])], axis=1)


def over_rows(tokens, body):
    @pl.loop(0, tokens // rows_at_once)
    def _(step):
        body(pl.multiple_of(step * rows_at_once, rows_at_once))


def minus_expm1(v):
    series = 1.0 / 5040.0
    for term in (720.0, 120.0, 24.0, 6.0, 2.0, 1.0):
        series = series * v + 1.0 / term
    return jnp.where(v > -0.25, -v * series, 1.0 - jnp.exp(v))


def gelu_parts(v):
    bent = jnp.tanh(root_two_over_pi * (v + cubic * v * v * v))
    half = 0.5 * (1.0 + bent)
    slope = half + 0.5 * v * (1.0 - bent * bent) * root_two_over_pi * (1.0 + 3.0 * cubic * v * v)
    return v * half, slope


def forward_scan(
    branch_ref, halo_ref, taps_ref, soft_ref, recur_gate_ref, input_gate_ref,
    conv_ref, recur_ref, input_ref, local_ref, prod_ref, seg_ref, end_ref, gates_ref,
    padded, pre, decay, drive,
):
    tokens, channels = branch_ref.shape
    taps = taps_ref.shape[0]
    steps = tokens // segments
    blocks, width, _ = recur_gate_ref.shape
    gates_ref[...] = jnp.zeros((channels, 2 * channels), bf16)
    for b in range(blocks):
        rows = pl.ds(b * width, width)
        gates_ref[rows, b * width : (b + 1) * width] = recur_gate_ref[b]
        gates_ref[rows, channels + b * width : channels + (b + 1) * width] = input_gate_ref[b]
    padded[0:8, :] = halo_ref[...].astype(f32)

    def fill(row):
        padded[pl.ds(row + 8, rows_at_once), :] = branch_ref[pl.ds(row, rows_at_once), :].astype(f32)

    over_rows(tokens, fill)

    def convolve(row):
        window = padded[pl.ds(row, rows_at_once + 8), :]
        total = taps_ref[0:1, :] * window[8:, :]
        for k in range(1, taps):
            total = total + taps_ref[k : k + 1, :] * window[8 - k : 8 - k + rows_at_once, :]
        conv_ref[pl.ds(row, rows_at_once), :] = total.astype(bf16)

    over_rows(tokens, convolve)
    pre[...] = jnp.dot(conv_ref[...], gates_ref[...], preferred_element_type=f32)

    def terms(row):
        at = pl.ds(row, rows_at_once)
        recur = jax.nn.sigmoid(pre[at, 0:channels])
        inward = jax.nn.sigmoid(pre[at, channels : 2 * channels])
        log_decay = -sharpness * recur * soft_ref[...]
        recur_ref[at, :] = recur
        input_ref[at, :] = inward
        split(decay, at, jnp.exp(log_decay))
        split(drive, at, jnp.sqrt(minus_expm1(2.0 * log_decay)) * inward * conv_ref[at, :].astype(f32))

    over_rows(tokens, terms)

    slabs = channels // 128

    def step(i, carried):
        at = pl.ds(i, segments, stride=steps)
        new = []
        for j in range(slabs):
            state, product = carried[j]
            a = decay[j, at, :]
            state = a * state + drive[j, at, :]
            product = a * product
            local_ref[j, at, :] = state
            prod_ref[j, at, :] = product
            new.append((state, product))
        return tuple(new)

    start = ((jnp.zeros((segments, 128), f32), jnp.ones((segments, 128), f32)),) * slabs
    last = lax.fori_loop(0, steps, step, start, unroll=4)
    state = jnp.concatenate([pair[0] for pair in last], axis=1)
    product = jnp.concatenate([pair[1] for pair in last], axis=1)
    seg_ref[0:segments, :] = product
    seg_ref[segments : 2 * segments, :] = state
    whole = jnp.ones((1, channels), f32)
    end = jnp.zeros((1, channels), f32)
    for s in range(segments):
        end = product[s : s + 1, :] * end + state[s : s + 1, :]
        whole = product[s : s + 1, :] * whole
    end_ref[0:1, :] = whole
    end_ref[1:2, :] = end


def mix(gate_ref, local_ref, prod_ref, seg_ref, ends_ref, index_ref, states_ref, mixed_ref, entry_ref):
    tokens, channels = gate_ref.shape
    steps = tokens // segments
    index = index_ref[0]
    carry = jnp.zeros((1, channels), f32)
    for j in range(ends_ref.shape[0]):
        new = ends_ref[j, 0:1, :] * carry + ends_ref[j, 1:2, :]
        carry = jnp.where(j < index, new, carry)
    entry_ref[...] = carry
    for s in range(segments):
        held = carry

        @pl.loop(0, steps // rows_at_once)
        def _(i):
            at = pl.ds(pl.multiple_of(s * steps + i * rows_at_once, rows_at_once), rows_at_once)
            states = joined(local_ref, at) + joined(prod_ref, at) * held
            states_ref[at, :] = states
            gate, _ = gelu_parts(gate_ref[at, :])
            mixed_ref[at, :] = (gate * states).astype(bf16)

        carry = seg_ref[s : s + 1, :] * carry + seg_ref[segments + s : segments + s + 1, :]


def backward_scan(
    d_mixed_ref, gate_ref, states_ref, recur_ref, soft_ref,
    d_gate_ref, local_ref, prod_ref, seg_ref, end_ref,
    decay, d_state,
):
    tokens, channels = gate_ref.shape
    steps = tokens // segments

    def terms(row):
        at = pl.ds(row, rows_at_once)
        d_mixed = d_mixed_ref[at, :].astype(f32)
        value, slope = gelu_parts(gate_ref[at, :])
        d_gate_ref[at, :] = (d_mixed * states_ref[at, :] * slope).astype(bf16)
        split(d_state, at, d_mixed * value)
        split(decay, at, jnp.exp(-sharpness * recur_ref[at, :] * soft_ref[...]))

    over_rows(tokens, terms)

    slabs = channels // 128

    def step(k, carried):
        at = pl.ds(steps - 1 - k, segments, stride=steps)
        new = []
        for j in range(slabs):
            into, reach = carried[j]
            a = decay[j, at, :]
            grad = d_state[j, at, :] + into
            local_ref[j, at, :] = grad
            prod_ref[j, at, :] = reach
            new.append((a * grad, a * reach))
        return tuple(new)

    start = ((jnp.zeros((segments, 128), f32), jnp.ones((segments, 128), f32)),) * slabs
    last = lax.fori_loop(0, steps, step, start, unroll=4)
    into = jnp.concatenate([pair[0] for pair in last], axis=1)
    reach = jnp.concatenate([pair[1] for pair in last], axis=1)
    seg_ref[0:segments, :] = reach
    seg_ref[segments : 2 * segments, :] = into
    end = jnp.zeros((1, channels), f32)
    for s in reversed(range(segments)):
        end = reach[s : s + 1, :] * end + into[s : s + 1, :]
    end_ref[...] = end


def backward_terms(
    local_ref, prod_ref, seg_ref, ends_ref, backs_ref, recur_ref, input_ref, conv_ref, states_ref, entry_ref,
    soft_ref, slide_ref, taps_ref, branch_ref, halo_ref, gates_ref, index_ref,
    d_both_ref, d_branch_ref, head_ref, decay_sum_ref, taps_sum_ref,
    before, d_conv, padded,
):
    tokens, channels = states_ref.shape
    taps = taps_ref.shape[0]
    steps = tokens // segments
    index = index_ref[0]
    padded[0:8, :] = halo_ref[...].astype(f32)
    before[0:8, :] = jnp.broadcast_to(entry_ref[...], (8, channels))
    carry = jnp.zeros((1, channels), f32)
    for j in reversed(range(ends_ref.shape[0])):
        new = ends_ref[j, 0:1, :] * carry + backs_ref[j, 0:1, :]
        carry = jnp.where(j > index, new, carry)
    decay_sum_ref[...] = jnp.zeros((8, channels), f32)
    taps_sum_ref[...] = jnp.zeros((8 * taps, channels), f32)

    def fill(row):
        padded[pl.ds(row + 8, rows_at_once), :] = branch_ref[pl.ds(row, rows_at_once), :].astype(f32)
        before[pl.ds(row + 8, rows_at_once), :] = states_ref[pl.ds(row, rows_at_once), :]

    over_rows(tokens, fill)
    for s in reversed(range(segments)):
        held = carry

        @pl.loop(0, steps // rows_at_once)
        def _(i):
            row = pl.multiple_of(s * steps + i * rows_at_once, rows_at_once)
            at = pl.ds(row, rows_at_once)
            grad = joined(local_ref, at) + joined(prod_ref, at) * held
            recur = recur_ref[at, :]
            inward = input_ref[at, :]
            conv = conv_ref[at, :].astype(f32)
            log_decay = -sharpness * recur * soft_ref[...]
            decay = jnp.exp(log_decay)
            root = jnp.sqrt(minus_expm1(2.0 * log_decay))
            previous = before[pl.ds(row, rows_at_once + 8), :][7 : 7 + rows_at_once, :]
            push = grad * inward
            total = decay * (grad * previous - push * decay * conv / root)
            rate = recur * total
            d_both_ref[at, 0:channels] = (-sharpness * soft_ref[...] * (1.0 - recur) * rate).astype(bf16)
            d_both_ref[at, channels : 2 * channels] = (push * root * conv * (1.0 - inward)).astype(bf16)
            d_conv[at, :] = push * root
            decay_sum_ref[...] += jnp.sum(rate.reshape(rows_at_once // 8, 8, channels), axis=0)

        carry = seg_ref[s : s + 1, :] * carry + seg_ref[segments + s : segments + s + 1, :]
    decay_sum_ref[...] = decay_sum_ref[...] * slide_ref[...]
    d_conv[0:tokens, :] += lax.dot_general(
        d_both_ref[...], gates_ref[...], (((1,), (1,)), ((), ())), preferred_element_type=f32
    )
    d_conv[tokens : tokens + 8, :] = jnp.zeros((8, channels), f32)
    first = jnp.concatenate([jnp.zeros((8, channels), f32), d_conv[0:8, :]], axis=0)
    head = taps_ref[0:1, :] * first[0:8, :]
    for k in range(1, taps):
        head = head + taps_ref[k : k + 1, :] * first[k : k + 8, :]
    head_ref[...] = head

    def finish(row):
        window = d_conv[pl.ds(row, rows_at_once + 8), :]
        now = window[0:rows_at_once, :]
        total = taps_ref[0:1, :] * now
        for k in range(1, taps):
            total = total + taps_ref[k : k + 1, :] * window[k : k + rows_at_once, :]
        d_branch_ref[pl.ds(row, rows_at_once), :] = total
        earlier = padded[pl.ds(row, rows_at_once + 8), :]
        for k in range(taps):
            product = now * earlier[8 - k : 8 - k + rows_at_once, :]
            taps_sum_ref[8 * k : 8 * k + 8, :] += jnp.sum(
                product.reshape(rows_at_once // 8, 8, channels), axis=0
            )

    over_rows(tokens, finish)


def place(me, own_ref, arrived, store):
    from_left, from_right, over, back, far = arrived
    for m, parts in enumerate(
        (
            (own_ref, from_right, back, far),
            (from_left, own_ref, from_right, over),
            (over, from_left, own_ref, from_right),
            (far, back, from_left, own_ref),
        )
    ):

        @pl.when(me == m)
        def _():
            for source, ref in enumerate(parts):
                store(source, ref)


def add_projection(
    own_ref, left_ref, right_ref, over_ref, back_ref, far_ref, weight_ref, inputs_ref, gain_ref, index_ref,
    residual_ref, normed_ref,
    mixed, rows,
):
    tokens, channels = own_ref.shape
    columns = weight_ref.shape[2]
    step = pl.program_id(0)

    def store(source, ref):
        def copy(row):
            at = pl.ds(row, rows_at_once)
            mixed[at, source * channels : (source + 1) * channels] = ref[at, :]

        over_rows(tokens, copy)

    @pl.when(step == 0)
    def _():
        place(index_ref[0], own_ref, (left_ref, right_ref, over_ref, back_ref, far_ref), store)

    total = inputs_ref[...].astype(f32) + jnp.dot(mixed[...], weight_ref[0], preferred_element_type=f32)
    residual_ref[...] = total
    rows[:, pl.ds(pl.multiple_of(step * columns, columns), columns)] = total

    @pl.when(step == pl.num_programs(0) - 1)
    def _():
        def normalise(row):
            at = pl.ds(row, rows_at_once)
            values = rows[at, :]
            inverse = inverse_rms(values)
            normed_ref[at, :] = (values * inverse * gain_ref[...]).astype(bf16)

        over_rows(tokens, normalise)


def residual_norm(own, arrived, weight, inputs, gain, index):
    tokens, channels = own.shape
    blocks, depth, columns = weight.shape
    width = inputs.shape[1]

    def whole(*dims):
        return pl.BlockSpec(dims, lambda j: (0,) * len(dims))

    return pl.pallas_call(
        add_projection,
        grid=(blocks,),
        in_specs=[whole(tokens, channels)] * 6
        + [
            pl.BlockSpec((1, depth, columns), lambda j: (j, 0, 0)),
            pl.BlockSpec((tokens, columns), lambda j: (0, j)),
            whole(1, width),
            pl.BlockSpec(memory_space=pltpu.SMEM),
        ],
        out_specs=[pl.BlockSpec((tokens, columns), lambda j: (0, j)), whole(tokens, width)],
        out_shape=[
            jax.ShapeDtypeStruct((tokens, width), f32),
            jax.ShapeDtypeStruct((tokens, width), bf16),
        ],
        scratch_shapes=[pltpu.VMEM((tokens, depth), bf16), pltpu.VMEM((tokens, width), f32)],
        compiler_params=pltpu.CompilerParams(vmem_limit_bytes=60 << 20),
        cost_estimate=pl.CostEstimate(
            flops=2 * tokens * depth * width,
            bytes_accessed=2 * (depth * width + 5 * tokens * width),
            transcendentals=0,
        ),
    )(own, *arrived, weight, inputs, gain, index)


def assembled(own, first, second, index, kind):
    size, width = own.shape
    peers = lax.axis_size("head")

    def body(index_ref, own_ref, left_ref, right_ref, over_ref, back_ref, far_ref, out_ref):
        step = pl.program_id(0)

        def store(source, ref):
            @pl.when(step == source)
            def _():
                def copy(row):
                    at = pl.ds(row, rows_at_once)
                    out_ref[at, :] = ref[at, :].astype(kind)

                over_rows(size, copy)

        place(index_ref[0], own_ref, (left_ref, right_ref, over_ref, back_ref, far_ref), store)

    return pl.pallas_call(
        body,
        grid_spec=pltpu.PrefetchScalarGridSpec(
            num_scalar_prefetch=1,
            grid=(peers,),
            in_specs=[pl.BlockSpec((size, width), lambda i, m: (0, 0))] * 6,
            out_specs=pl.BlockSpec((size, width), lambda i, m: (i, 0)),
        ),
        out_shape=jax.ShapeDtypeStruct((peers * size, width), kind),
        compiler_params=pltpu.CompilerParams(vmem_limit_bytes=26 << 20),
        cost_estimate=pl.CostEstimate(flops=1000, bytes_accessed=1000, transcendentals=0),
    )(index, own, *first, *second)


def weight_grads(products, extra=None):
    lefts = [left for left, _ in products]
    rights = [right for _, right in products]
    tokens, width = lefts[0].shape
    count = len(products)
    spans = [right.shape[1] for right in rights]
    total = sum(spans) + (0 if extra is None else extra.shape[1])
    block = 256

    def body(*refs):
        left_refs, right_refs, out_ref = refs[:count], refs[count : 2 * count], refs[-1]
        place = 0
        for left_ref, right_ref in zip(left_refs, right_refs, strict=True):
            span = right_ref.shape[1]
            out_ref[:, place : place + span] = lax.dot_general(
                left_ref[...], right_ref[...], (((0,), (0,)), ((), ())), preferred_element_type=f32
            ).astype(bf16)
            place += span
        if extra is not None:
            out_ref[:, place:] = refs[2 * count][...]

    extras = [] if extra is None else [extra]
    return pl.pallas_call(
        body,
        grid=(width // block,),
        in_specs=[pl.BlockSpec((tokens, block), lambda i: (0, i))] * count
        + [pl.BlockSpec((tokens, span), lambda i: (0, 0)) for span in spans]
        + [pl.BlockSpec((block, e.shape[1]), lambda i: (i, 0)) for e in extras],
        out_specs=pl.BlockSpec((block, total), lambda i: (i, 0)),
        out_shape=jax.ShapeDtypeStruct((width, total), bf16),
        compiler_params=pltpu.CompilerParams(vmem_limit_bytes=48 << 20),
        cost_estimate=pl.CostEstimate(
            flops=2 * tokens * width * total, bytes_accessed=2 * width * total, transcendentals=0
        ),
    )(*lefts, *rights, *extras)


def finish_ffn(summed, count):
    rows, width = summed.shape
    span = width // count

    def body(in_ref, *out_refs):
        def convert(row):
            at = pl.ds(row, rows_at_once)
            for k, ref in enumerate(out_refs[:-1]):
                ref[at, :] = in_ref[at, k * span : (k + 1) * span].astype(f32)

        over_rows(rows, convert)
        for place in range(0, span, 128):
            part = in_ref[:, (count - 1) * span + place : (count - 1) * span + place + 128]
            out_refs[-1][place : place + 128, :] = part.astype(f32).T

    shapes = [jax.ShapeDtypeStruct((rows, span), f32)] * (count - 1)
    return call(body, [*shapes, jax.ShapeDtypeStruct((span, rows), f32)], [], summed)


def finish_rest(summed, channels, blocks, block_width, taps, owners):
    rows = summed.shape[0]
    patch, kept = block_width // owners, channels // owners

    def body(in_ref, gate_ref, input_ref, out_ref, taps_ref, recur_ref, inward_ref, decay_ref):
        def convert(row):
            at = pl.ds(row, rows_at_once)
            gate_ref[at, :] = in_ref[at, 0:channels].astype(f32)
            input_ref[at, :] = in_ref[at, channels : 2 * channels].astype(f32)

        over_rows(rows, convert)
        out_ref[...] = in_ref[:, 2 * channels : 3 * channels].astype(f32).T
        small = in_ref[:, 3 * channels :].astype(f32)
        _, lanes = packed_shape(blocks, block_width, taps, owners, owners * rows)
        groups = -(-2 * block_width // lanes)
        for b in range(blocks):
            parts = []
            for g in range(groups):
                row = (g * blocks + b) * patch
                parts.append(small[row : row + patch, 0 : min(lanes, 2 * block_width - g * lanes)])
            both = jnp.concatenate(parts, axis=1)
            recur_ref[b] = both[:, 0:block_width]
            inward_ref[b] = both[:, block_width : 2 * block_width]
        used = groups * blocks * patch
        taps_ref[...] = small[used : used + taps, 0:kept]
        decay_ref[...] = small[used + taps : used + taps + 1, 0:kept]

    shapes = [
        (rows, channels),
        (rows, channels),
        (channels, rows),
        (taps, kept),
        (blocks, patch, block_width),
        (blocks, patch, block_width),
        (1, kept),
    ]
    return call(body, [jax.ShapeDtypeStruct(shape, f32) for shape in shapes], [], summed)


def add_last(base, last):
    cut = last[0].shape[0]

    def body(base_ref, first_ref, second_ref, out_ref):
        for start, ref in ((0, first_ref), (cut, second_ref)):

            def add(row):
                at = pl.ds(start + row, rows_at_once)
                out_ref[at, :] = (base_ref[at, :] + ref[pl.ds(row, rows_at_once), :].astype(f32)).astype(bf16)

            over_rows(ref.shape[0], add)

    return call(body, [jax.ShapeDtypeStruct(base.shape, bf16)], [], base, *last)[0]


def packed_shape(blocks, width, taps, owners, rows):
    groups = -(-2 * width // 128)
    if groups * blocks * (width // owners) + taps + 1 <= rows // owners:
        return 128, 128
    return groups * 128, 2 * width


def gate_grads(conv_low, d_both, taps_sums, decay_sums, blocks, owners, rows):
    channels = conv_low.shape[1]
    taps = taps_sums.shape[0] // 8
    width = channels // blocks
    patch, kept, span = width // owners, channels // owners, rows // owners
    columns, lanes = packed_shape(blocks, width, taps, owners, rows)

    def body(conv_ref, both_ref, taps_ref, decay_ref, out_ref):
        out_ref[...] = jnp.zeros((rows, columns), bf16)
        dense = lax.dot_general(
            conv_ref[...], both_ref[...], (((0,), (0,)), ((), ())), preferred_element_type=f32
        )
        sums = [jnp.sum(taps_ref[8 * k : 8 * k + 8, :], axis=0, keepdims=True) for k in range(taps)]
        sums.append(jnp.sum(decay_ref[...], axis=0, keepdims=True))
        sums = jnp.concatenate(sums, axis=0).astype(bf16)
        for b in range(blocks):
            at = slice(b * width, (b + 1) * width)
            recur = dense[at, b * width : (b + 1) * width].astype(bf16)
            inward = dense[at, channels + b * width : channels + (b + 1) * width].astype(bf16)
            both = jnp.concatenate([recur, inward], axis=1)
            for s in range(owners):
                mine = both[s * patch : (s + 1) * patch, :]
                for g, start in enumerate(range(0, 2 * width, lanes)):
                    row = s * span + (g * blocks + b) * patch
                    part = mine[:, start : start + lanes]
                    out_ref[row : row + patch, 0 : part.shape[1]] = part
        used = -(-2 * width // lanes) * blocks * patch
        for s in range(owners):
            row = s * span + used
            out_ref[row : row + taps + 1, 0:kept] = sums[:, s * kept : (s + 1) * kept]

    return call(
        body,
        [jax.ShapeDtypeStruct((rows, columns), bf16)],
        [],
        conv_low,
        d_both,
        taps_sums,
        decay_sums,
        flops=4 * conv_low.shape[0] * channels * channels,
    )[0]


def shifted(count, by):
    return [(i, (i + by) % count) for i in range(count)]


def exchanged(blocks):
    peers = lax.axis_size("head")
    return [lax.ppermute(blocks(k), "head", shifted(peers, k)) for k in range(1, peers)]


def block_of(array, where, dim):
    peers = lax.axis_size("head")
    size = array.shape[dim] // peers
    return lax.dynamic_slice_in_dim(array, (where % peers) * size, size, dim)


def shard(array, where):
    return block_of(array, where, 0)


def added(first, *others):
    total = first.astype(f32)
    for part in others:
        total = total + part.astype(f32)
    return total


def line_pairs(by):
    peers = lax.axis_size("head")
    return [(i, i + by) for i in range(peers) if 0 <= i + by < peers]


def scatter_first(low):
    me = lax.axis_index("head")
    across = shard(low, me + 2)
    return (
        lax.ppermute(across, "head", [(0, 1), (1, 2)]),
        lax.ppermute(across, "head", [(3, 2), (2, 1)]),
        lax.ppermute(shard(low, 3 - me), "head", [(0, 2), (3, 1)]),
    )


def by_rows(body, index, shares, rest, outputs, grant=60 << 20):
    peers = lax.axis_size("head")
    arrays = [array for array, _ in shares]
    rows = min(array.shape[0] // (1 if where is None else peers) for array, where in shares)
    size = min(rows, 64)
    steps = rows // size

    def row_spec(array, where):
        if where is None:
            return pl.BlockSpec((size, array.shape[1]), lambda i, m: (i, 0))
        return pl.BlockSpec(
            (size, array.shape[1]), lambda i, m, where=where: (lax.rem(m[0] + where + peers, peers) * steps + i, 0)
        )

    return pl.pallas_call(
        body,
        grid_spec=pltpu.PrefetchScalarGridSpec(
            num_scalar_prefetch=1,
            grid=(steps,),
            in_specs=[row_spec(*share) for share in shares]
            + [pl.BlockSpec(array.shape, lambda i, m: (0, 0)) for array in rest],
            out_specs=[
                pl.BlockSpec((1, width), lambda i, m: (0, 0))
                if height == 1
                else pl.BlockSpec((size, width), lambda i, m: (i, 0))
                for (height, width), _ in outputs
            ],
        ),
        out_shape=[jax.ShapeDtypeStruct(shape, kind) for shape, kind in outputs],
        compiler_params=pltpu.CompilerParams(vmem_limit_bytes=grant),
        cost_estimate=pl.CostEstimate(flops=1000, bytes_accessed=1000, transcendentals=0),
    )(index, *arrays, *rest)


def both_ways(me_ref, right_ref, left_ref, from_left_ref, from_right_ref, far_ref, to_right_ref, to_left_ref):
    far = far_ref[...].astype(f32)
    me = me_ref[0]
    to_right = right_ref[...].astype(f32) + from_left_ref[...].astype(f32)
    to_right_ref[...] = (to_right + jnp.where(me == 2, far, 0.0)).astype(bf16)
    to_left = left_ref[...].astype(f32) + from_right_ref[...].astype(f32)
    to_left_ref[...] = (to_left + jnp.where(me == 1, far, 0.0)).astype(bf16)


def scatter_second(low, first, index):
    from_left, from_right, far = first
    shape = far.shape
    to_right, to_left = by_rows(
        both_ways,
        index,
        [(low, 1), (low, -1), (from_left, None), (from_right, None), (far, None)],
        [],
        [(shape, bf16), (shape, bf16)],
    )
    return lax.ppermute(to_right, "head", line_pairs(1)), lax.ppermute(to_left, "head", line_pairs(-1))


def gather_first(own):
    return lax.ppermute(own, "head", line_pairs(1)), lax.ppermute(own, "head", line_pairs(-1))


def gather_second(first):
    me = lax.axis_index("head")
    from_left, from_right = first
    over = jnp.where(me == 1, from_left, from_right)
    back = jnp.where(me == 1, from_right, from_left)
    return (
        lax.ppermute(over, "head", [(1, 2), (2, 1)]),
        lax.ppermute(back, "head", [(1, 0), (2, 3)]),
        lax.ppermute(over, "head", [(1, 3), (2, 0)]),
    )


def line_turn(turn, sent):
    peers = lax.axis_size("head")
    return lax.ppermute(sent, "head", [(turn - 1, turn), (peers - turn, peers - turn - 1)])


together = lax.optimization_barrier


def inverse_rms(values):
    return lax.rsqrt(jnp.mean(values * values, axis=-1, keepdims=True) + epsilon)


def sum_up(ref, row):
    @pl.when(pl.program_id(0) == 0)
    def _():
        ref[...] = jnp.zeros(ref.shape, f32)

    ref[...] += row


def norm_grads(values, scales, grad):
    inverse = inverse_rms(values)
    unit = values * inverse
    scaled = grad * scales
    inner = jnp.mean(scaled * unit, axis=-1, keepdims=True)
    return inverse * (scaled - unit * inner), jnp.sum(grad * unit, axis=0, keepdims=True)


def second_norm(
    me_ref, own_ref, residual_ref, cotangent_ref, right_ref, left_ref, gain_ref, low_ref, d_resid_ref, sum_ref
):
    grad = own_ref[...].astype(f32) + right_ref[...].astype(f32) + left_ref[...].astype(f32)
    part, gains = norm_grads(residual_ref[...], gain_ref[...], grad)
    total = cotangent_ref[...].astype(f32) + part
    d_resid_ref[...] = total
    low_ref[...] = total.astype(bf16)
    sum_up(sum_ref, gains)


def first_norm(me_ref, own_ref, inputs_ref, right_ref, left_ref, d_resid_ref, gain_ref, low_ref, grad_ref, sum_ref):
    grad = own_ref[...].astype(f32) + right_ref[...].astype(f32) + left_ref[...].astype(f32)
    part, gains = norm_grads(inputs_ref[...].astype(f32), gain_ref[...], grad)
    total = d_resid_ref[...] + part
    grad_ref[...] = total
    low_ref[...] = total.astype(bf16)
    sum_up(sum_ref, gains)


def local(
    block_in,
    pre_gain,
    gate_proj,
    input_proj,
    conv_taps,
    recur_gate,
    input_gate,
    decay_param,
    out_proj,
    post_gain,
    ffn_gate,
    ffn_up,
    ffn_down,
    cotangent,
):
    tokens, width = block_in.shape
    channels = gate_proj.shape[1]
    blocks, block_width, _ = recur_gate.shape
    tap_count = conv_taps.shape[0]
    hidden_units = ffn_gate.shape[1]
    seq_count, seq_index = lax.axis_size("seq"), lax.axis_index("seq")
    head_count, head_index = lax.axis_size("head"), lax.axis_index("head")
    share = tokens // head_count
    slabs = (channels // 128, tokens, 128)
    here = seq_index.astype(jnp.int32).reshape(1)
    place_index = head_index.astype(jnp.int32).reshape(1)
    forward_pairs = [(i, i + 1) for i in range(seq_count - 1)]
    backward_pairs = [(i + 1, i) for i in range(seq_count - 1)]

    def mine(rows):
        return lax.dynamic_slice_in_dim(rows, head_index * share, share, 0)

    def struct(*dims, kind=f32):
        return jax.ShapeDtypeStruct(dims, kind)

    halo_in = lax.ppermute(block_in[tokens - 8 :], "seq", forward_pairs)
    columns = width // seq_count
    column_block = lax.dynamic_slice_in_dim(out_proj, seq_index * columns, columns, 1)
    column_block = lax.all_gather(column_block, "head").reshape(head_count * channels, columns)
    soft = jax.nn.softplus(-decay_param)[None, :]
    slide = sharpness * jax.nn.sigmoid(-decay_param)[None, :]

    def normalise(rows):
        values = rows.astype(f32)
        return (values * inverse_rms(values) * pre_gain).astype(bf16)

    normed = normalise(block_in)
    branch_in = jnp.dot(normed, input_proj, preferred_element_type=f32).astype(bf16)
    halo = jnp.dot(normalise(halo_in), input_proj, preferred_element_type=f32).astype(bf16)
    conv_low, recur_rate, input_rate, local_states, products, seg_ends, end, gates = call(
        forward_scan,
        [
            struct(tokens, channels, kind=bf16),
            struct(tokens, channels),
            struct(tokens, channels),
            struct(*slabs),
            struct(*slabs),
            struct(2 * segments, channels),
            struct(2, channels),
            struct(channels, 2 * channels, kind=bf16),
        ],
        [
            pltpu.VMEM((tokens + 8, channels), f32),
            pltpu.VMEM((tokens, 2 * channels), f32),
            pltpu.VMEM(slabs, f32),
            pltpu.VMEM(slabs, f32),
        ],
        branch_in,
        halo,
        conv_taps,
        soft,
        recur_gate,
        input_gate,
        flops=4 * tokens * channels * channels,
    )
    ends = lax.all_gather(end, "seq")
    gate_pre = jnp.dot(normed, gate_proj, preferred_element_type=f32)
    states, mixed_low, entry = call(
        mix,
        [struct(tokens, channels), struct(tokens, channels, kind=bf16), struct(1, channels)],
        [],
        gate_pre,
        local_states,
        products,
        seg_ends,
        ends,
        here,
        scalars=1,
    )
    column_block, mixed_low = together((column_block, mixed_low))
    projection = lax.all_gather(column_block, "seq")
    if columns % 128:
        projection = jnp.moveaxis(projection, 0, 1).reshape(1, head_count * channels, width)
    first = gather_first(mixed_low)
    second = gather_second(first)
    d_hidden = jnp.einsum("td,fd->tf", cotangent, ffn_down, preferred_element_type=f32)
    second, d_hidden = together((second, d_hidden))
    residual, normed_two = residual_norm(
        mixed_low,
        (*first, *second),
        projection,
        block_in,
        post_gain[None, :],
        place_index,
    )
    ffn_gpre = jnp.dot(normed_two, ffn_gate, preferred_element_type=f32)
    ffn_upre = jnp.dot(normed_two, ffn_up, preferred_element_type=f32)
    value, slope = gelu_parts(ffn_gpre)
    hidden = (value * ffn_upre).astype(bf16)
    d_gpre = (d_hidden * ffn_upre * slope).astype(bf16)
    d_upre = (d_hidden * value).astype(bf16)
    d_normed_two = jnp.einsum(
        "tf,df->td", d_gpre, ffn_gate, preferred_element_type=f32
    ) + jnp.einsum("tf,df->td", d_upre, ffn_up, preferred_element_type=f32)
    d_normed_two = d_normed_two.astype(bf16)
    d_normed_two, hidden, d_gpre, d_upre = together((d_normed_two, hidden, d_gpre, d_upre))
    first = scatter_first(d_normed_two)
    grad_ffn = weight_grads([(normed_two, d_gpre), (normed_two, d_upre), (cotangent, hidden)])
    first, grad_ffn = together((first, grad_ffn))
    grad_ffn = lax.psum_scatter(grad_ffn, "seq", scatter_dimension=0, tiled=True)
    second = scatter_second(d_normed_two, first, place_index)
    ffn_out = jnp.dot(hidden, ffn_down, preferred_element_type=f32).astype(bf16)
    second, ffn_out = together((second, ffn_out))
    own_rows = (share, width)
    d_out_share, d_resid, grad_postgain = by_rows(
        second_norm,
        place_index,
        [(d_normed_two, 0), (residual, 0), (cotangent, 0), (second[0], None), (second[1], None)],
        [post_gain[None, :]],
        [(own_rows, bf16), (own_rows, f32), ((1, width), f32)],
        grant=26 << 20,
    )
    first = gather_first(d_out_share)
    first, ffn_out = together((first, ffn_out))
    second = gather_second(first)
    cut = tokens * 5 // 8
    ffn_halves = [ffn_out[:cut], ffn_out[cut:]]
    turn_one = [line_turn(1, ffn_halves[0])]
    d_out_low = assembled(d_out_share, first, second, place_index, bf16)
    d_out_low, ffn_halves[1] = together((d_out_low, ffn_halves[1]))
    turn_one.append(line_turn(1, ffn_halves[1]))
    d_mixed = jnp.einsum("td,cd->tc", d_out_low, out_proj, preferred_element_type=f32)
    sent = added(ffn_halves[0], turn_one[0]).astype(bf16)
    d_mixed, sent = together((d_mixed, sent))
    turn_two = [line_turn(2, sent)]
    d_gate_low, grad_local, grad_prod, grad_segs, grad_end = call(
        backward_scan,
        [
            struct(tokens, channels, kind=bf16),
            struct(*slabs),
            struct(*slabs),
            struct(2 * segments, channels),
            struct(1, channels),
        ],
        [pltpu.VMEM(slabs, f32), pltpu.VMEM(slabs, f32)],
        d_mixed,
        gate_pre,
        states,
        recur_rate,
        soft,
    )
    backs = lax.all_gather(grad_end, "seq")
    sent = added(ffn_halves[1], turn_one[1]).astype(bf16)
    backs, sent = together((backs, sent))
    turn_two.append(line_turn(2, sent))
    d_both, d_branch, head_rows, decay_sums, taps_sums = call(
        backward_terms,
        [
            struct(tokens, 2 * channels, kind=bf16),
            struct(tokens, channels),
            struct(8, channels),
            struct(8, channels),
            struct(8 * tap_count, channels),
        ],
        [
            pltpu.VMEM((tokens + 8, channels), f32),
            pltpu.VMEM((tokens + 8, channels), f32),
            pltpu.VMEM((tokens + 8, channels), f32),
        ],
        grad_local,
        grad_prod,
        grad_segs,
        ends,
        backs,
        recur_rate,
        input_rate,
        conv_low,
        states,
        entry,
        soft,
        slide,
        conv_taps,
        branch_in,
        halo,
        gates,
        here,
        scalars=1,
        flops=4 * tokens * channels * channels,
    )
    sent = added(ffn_halves[0], turn_two[0]).astype(bf16)
    head_rows, d_branch, d_both, sent = together((head_rows, d_branch, d_both, sent))
    later_rows = lax.ppermute(head_rows, "seq", backward_pairs)
    turn_three = [line_turn(3, sent)]
    d_branch_low = (d_branch + jnp.pad(later_rows, ((tokens - 8, 0), (0, 0)))).astype(bf16)
    d_normed = jnp.einsum("tc,dc->td", d_gate_low, gate_proj, preferred_element_type=f32) + jnp.einsum(
        "tc,dc->td", d_branch_low, input_proj, preferred_element_type=f32
    )
    d_normed = d_normed.astype(bf16)
    d_normed, conv_low, d_both = together((d_normed, conv_low, d_both))
    first = scatter_first(d_normed)
    packed = gate_grads(conv_low, d_both, taps_sums, decay_sums, blocks, seq_count, width)
    grad_rest = weight_grads([(normed, d_gate_low), (normed, d_branch_low), (d_out_low, mixed_low)], packed)
    grad_ffn = finish_ffn(grad_ffn, 3)
    first, grad_rest, turn_three, turn_two, grad_ffn = together(
        (first, grad_rest, turn_three, turn_two, grad_ffn)
    )
    second = scatter_second(d_normed, first, place_index)
    sent = added(ffn_halves[1], turn_two[1]).astype(bf16)
    turn_three.append(line_turn(3, sent))
    grad_rest = lax.psum_scatter(grad_rest, "seq", scatter_dimension=0, tiled=True)
    grad_low, grad_input, grad_pregain = by_rows(
        first_norm,
        place_index,
        [(d_normed, 0), (block_in, 0), (second[0], None), (second[1], None), (d_resid, None)],
        [pre_gain[None, :]],
        [(own_rows, bf16), (own_rows, f32), ((1, width), f32)],
    )
    first = gather_first(grad_low)
    gains = jnp.concatenate([grad_pregain, grad_postgain], axis=0)
    gain_pieces = exchanged(lambda k: gains)
    base = residual + added(ffn_out, jnp.concatenate(turn_one), jnp.concatenate(turn_two))
    block_out = add_last(base, turn_three)
    first, block_out = together((first, block_out))
    second = gather_second(first)
    gains = jnp.sum(lax.all_gather(sum(gain_pieces, gains), "seq"), axis=0)
    gain_share = width // seq_count
    gains = lax.dynamic_slice_in_dim(gains, seq_index * gain_share, gain_share, 1)
    grad_rest, grad_ffn = together((grad_rest, grad_ffn))
    grad_rest = finish_rest(grad_rest, channels, blocks, block_width, tap_count, seq_count)
    second, grad_rest = together((second, grad_rest))
    grad_gate_proj, grad_input_proj, grad_out_proj, grad_taps, grad_recur, grad_inward, grad_decay = grad_rest
    grad_input = assembled(grad_input, first, second, place_index, f32)
    return (
        block_out,
        grad_input,
        gains[0],
        grad_gate_proj,
        grad_input_proj,
        grad_taps,
        grad_recur,
        grad_inward,
        grad_decay[0],
        grad_out_proj,
        gains[1],
        *grad_ffn,
    )


def solution(mesh):
    placed = (
        P("seq", None),
        P(),
        P(None, "head"),
        P(None, "head"),
        P(None, "head"),
        P("head", None, None),
        P("head", None, None),
        P("head"),
        P("head", None),
        P(),
        P(None, "head"),
        P(None, "head"),
        P("head", None),
        P("seq", None),
    )
    return jax.shard_map(
        local,
        mesh=mesh,
        in_specs=placed,
        out_specs=(
            P("seq", None),
            P("seq", None),
            P("seq"),
            P("seq", "head"),
            P("seq", "head"),
            P(None, ("head", "seq")),
            P("head", "seq", None),
            P("head", "seq", None),
            P(("head", "seq")),
            P("head", "seq"),
            P("seq"),
            P("seq", "head"),
            P("seq", "head"),
            P("head", "seq"),
        ),
        check_vma=False,
    )
```

```python
import jax
import jax.numpy as jnp
from jax import lax
from jax.experimental import pallas as pl
from jax.experimental.pallas import tpu as pltpu
from jax.sharding import PartitionSpec as P

epsilon = 1e-06
sharpness = 8.0
segments = 8
rows_at_once = 32
root_two_over_pi = 0.7978845608028654
cubic = 0.044715
f32 = jnp.float32
bf16 = jnp.bfloat16


def call(body, out_shape, scratch, *operands, scalars=0, flops=0):
    vectors = len(operands) - scalars
    moved = sum(x.size * x.dtype.itemsize for x in (*operands, *out_shape))
    return pl.pallas_call(
        body,
        out_shape=out_shape,
        in_specs=[pl.BlockSpec(memory_space=pltpu.VMEM)] * vectors
        + [pl.BlockSpec(memory_space=pltpu.SMEM)] * scalars,
        out_specs=[pl.BlockSpec(memory_space=pltpu.VMEM)] * len(out_shape),
        scratch_shapes=scratch,
        compiler_params=pltpu.CompilerParams(vmem_limit_bytes=26 << 20),
        cost_estimate=pl.CostEstimate(flops=1000, bytes_accessed=1000, transcendentals=0),
    )(*operands)


def split(ref, at, value):
    for j in range(ref.shape[0]):
        ref[j, at, :] = value[:, 128 * j : 128 * (j + 1)]


def joined(ref, at):
    return jnp.concatenate([ref[j, at, :] for j in range(ref.shape[0])], axis=1)


def over_rows(tokens, body):
    @pl.loop(0, tokens // rows_at_once)
    def _(step):
        body(pl.multiple_of(step * rows_at_once, rows_at_once))


def minus_expm1(v):
    series = 1.0 / 5040.0
    for term in (720.0, 120.0, 24.0, 6.0, 2.0, 1.0):
        series = series * v + 1.0 / term
    return jnp.where(v > -0.25, -v * series, 1.0 - jnp.exp(v))


def gelu_parts(v):
    bent = jnp.tanh(root_two_over_pi * (v + cubic * v * v * v))
    half = 0.5 * (1.0 + bent)
    slope = half + 0.5 * v * (1.0 - bent * bent) * root_two_over_pi * (1.0 + 3.0 * cubic * v * v)
    return v * half, slope


def forward_scan(
    branch_ref, halo_ref, taps_ref, soft_ref, recur_gate_ref, input_gate_ref,
    conv_ref, recur_ref, input_ref, local_ref, prod_ref, seg_ref, end_ref, gates_ref,
    padded, pre, decay, drive,
):
    tokens, channels = branch_ref.shape
    taps = taps_ref.shape[0]
    steps = tokens // segments
    blocks, width, _ = recur_gate_ref.shape
    gates_ref[...] = jnp.zeros((channels, 2 * channels), bf16)
    for b in range(blocks):
        rows = pl.ds(b * width, width)
        gates_ref[rows, b * width : (b + 1) * width] = recur_gate_ref[b]
        gates_ref[rows, channels + b * width : channels + (b + 1) * width] = input_gate_ref[b]
    padded[0:8, :] = halo_ref[...].astype(f32)

    def fill(row):
        padded[pl.ds(row + 8, rows_at_once), :] = branch_ref[pl.ds(row, rows_at_once), :].astype(f32)

    over_rows(tokens, fill)

    def convolve(row):
        window = padded[pl.ds(row, rows_at_once + 8), :]
        total = taps_ref[0:1, :] * window[8:, :]
        for k in range(1, taps):
            total = total + taps_ref[k : k + 1, :] * window[8 - k : 8 - k + rows_at_once, :]
        conv_ref[pl.ds(row, rows_at_once), :] = total.astype(bf16)

    over_rows(tokens, convolve)
    pre[...] = jnp.dot(conv_ref[...], gates_ref[...], preferred_element_type=f32)

    def terms(row):
        at = pl.ds(row, rows_at_once)
        recur = jax.nn.sigmoid(pre[at, 0:channels])
        inward = jax.nn.sigmoid(pre[at, channels : 2 * channels])
        log_decay = -sharpness * recur * soft_ref[...]
        recur_ref[at, :] = recur
        input_ref[at, :] = inward
        split(decay, at, jnp.exp(log_decay))
        split(drive, at, jnp.sqrt(minus_expm1(2.0 * log_decay)) * inward * conv_ref[at, :].astype(f32))

    over_rows(tokens, terms)

    slabs = channels // 128

    def step(i, carried):
        at = pl.ds(i, segments, stride=steps)
        new = []
        for j in range(slabs):
            state, product = carried[j]
            a = decay[j, at, :]
            state = a * state + drive[j, at, :]
            product = a * product
            local_ref[j, at, :] = state
            prod_ref[j, at, :] = product
            new.append((state, product))
        return tuple(new)

    start = ((jnp.zeros((segments, 128), f32), jnp.ones((segments, 128), f32)),) * slabs
    last = lax.fori_loop(0, steps, step, start, unroll=4)
    state = jnp.concatenate([pair[0] for pair in last], axis=1)
    product = jnp.concatenate([pair[1] for pair in last], axis=1)
    seg_ref[0:segments, :] = product
    seg_ref[segments : 2 * segments, :] = state
    whole = jnp.ones((1, channels), f32)
    end = jnp.zeros((1, channels), f32)
    for s in range(segments):
        end = product[s : s + 1, :] * end + state[s : s + 1, :]
        whole = product[s : s + 1, :] * whole
    end_ref[0:1, :] = whole
    end_ref[1:2, :] = end


def mix(gate_ref, local_ref, prod_ref, seg_ref, ends_ref, index_ref, states_ref, mixed_ref, entry_ref):
    tokens, channels = gate_ref.shape
    steps = tokens // segments
    index = index_ref[0]
    carry = jnp.zeros((1, channels), f32)
    for j in range(ends_ref.shape[0]):
        new = ends_ref[j, 0:1, :] * carry + ends_ref[j, 1:2, :]
        carry = jnp.where(j < index, new, carry)
    entry_ref[...] = carry
    for s in range(segments):
        held = carry

        @pl.loop(0, steps // rows_at_once)
        def _(i):
            at = pl.ds(pl.multiple_of(s * steps + i * rows_at_once, rows_at_once), rows_at_once)
            states = joined(local_ref, at) + joined(prod_ref, at) * held
            states_ref[at, :] = states
            gate, _ = gelu_parts(gate_ref[at, :])
            mixed_ref[at, :] = (gate * states).astype(bf16)

        carry = seg_ref[s : s + 1, :] * carry + seg_ref[segments + s : segments + s + 1, :]


def backward_scan(
    d_mixed_ref, gate_ref, states_ref, recur_ref, soft_ref,
    d_gate_ref, local_ref, prod_ref, seg_ref, end_ref,
    decay, d_state,
):
    tokens, channels = gate_ref.shape
    steps = tokens // segments

    def terms(row):
        at = pl.ds(row, rows_at_once)
        d_mixed = d_mixed_ref[at, :].astype(f32)
        value, slope = gelu_parts(gate_ref[at, :])
        d_gate_ref[at, :] = (d_mixed * states_ref[at, :] * slope).astype(bf16)
        split(d_state, at, d_mixed * value)
        split(decay, at, jnp.exp(-sharpness * recur_ref[at, :] * soft_ref[...]))

    over_rows(tokens, terms)

    slabs = channels // 128

    def step(k, carried):
        at = pl.ds(steps - 1 - k, segments, stride=steps)
        new = []
        for j in range(slabs):
            into, reach = carried[j]
            a = decay[j, at, :]
            grad = d_state[j, at, :] + into
            local_ref[j, at, :] = grad
            prod_ref[j, at, :] = reach
            new.append((a * grad, a * reach))
        return tuple(new)

    start = ((jnp.zeros((segments, 128), f32), jnp.ones((segments, 128), f32)),) * slabs
    last = lax.fori_loop(0, steps, step, start, unroll=4)
    into = jnp.concatenate([pair[0] for pair in last], axis=1)
    reach = jnp.concatenate([pair[1] for pair in last], axis=1)
    seg_ref[0:segments, :] = reach
    seg_ref[segments : 2 * segments, :] = into
    end = jnp.zeros((1, channels), f32)
    for s in reversed(range(segments)):
        end = reach[s : s + 1, :] * end + into[s : s + 1, :]
    end_ref[...] = end


def backward_terms(
    local_ref, prod_ref, seg_ref, ends_ref, backs_ref, recur_ref, input_ref, conv_ref, states_ref, entry_ref,
    soft_ref, slide_ref, taps_ref, branch_ref, halo_ref, gates_ref, index_ref,
    d_both_ref, d_branch_ref, head_ref, decay_sum_ref, taps_sum_ref,
    before, d_conv, padded,
):
    tokens, channels = states_ref.shape
    taps = taps_ref.shape[0]
    steps = tokens // segments
    index = index_ref[0]
    padded[0:8, :] = halo_ref[...].astype(f32)
    before[0:8, :] = jnp.broadcast_to(entry_ref[...], (8, channels))
    carry = jnp.zeros((1, channels), f32)
    for j in reversed(range(ends_ref.shape[0])):
        new = ends_ref[j, 0:1, :] * carry + backs_ref[j, 0:1, :]
        carry = jnp.where(j > index, new, carry)
    decay_sum_ref[...] = jnp.zeros((8, channels), f32)
    taps_sum_ref[...] = jnp.zeros((8 * taps, channels), f32)

    def fill(row):
        padded[pl.ds(row + 8, rows_at_once), :] = branch_ref[pl.ds(row, rows_at_once), :].astype(f32)
        before[pl.ds(row + 8, rows_at_once), :] = states_ref[pl.ds(row, rows_at_once), :]

    over_rows(tokens, fill)
    for s in reversed(range(segments)):
        held = carry

        @pl.loop(0, steps // rows_at_once)
        def _(i):
            row = pl.multiple_of(s * steps + i * rows_at_once, rows_at_once)
            at = pl.ds(row, rows_at_once)
            grad = joined(local_ref, at) + joined(prod_ref, at) * held
            recur = recur_ref[at, :]
            inward = input_ref[at, :]
            conv = conv_ref[at, :].astype(f32)
            log_decay = -sharpness * recur * soft_ref[...]
            decay = jnp.exp(log_decay)
            root = jnp.sqrt(minus_expm1(2.0 * log_decay))
            previous = before[pl.ds(row, rows_at_once + 8), :][7 : 7 + rows_at_once, :]
            push = grad * inward
            total = decay * (grad * previous - push * decay * conv / root)
            rate = recur * total
            d_both_ref[at, 0:channels] = (-sharpness * soft_ref[...] * (1.0 - recur) * rate).astype(bf16)
            d_both_ref[at, channels : 2 * channels] = (push * root * conv * (1.0 - inward)).astype(bf16)
            d_conv[at, :] = push * root
            decay_sum_ref[...] += jnp.sum(rate.reshape(rows_at_once // 8, 8, channels), axis=0)

        carry = seg_ref[s : s + 1, :] * carry + seg_ref[segments + s : segments + s + 1, :]
    decay_sum_ref[...] = decay_sum_ref[...] * slide_ref[...]
    d_conv[0:tokens, :] += lax.dot_general(
        d_both_ref[...], gates_ref[...], (((1,), (1,)), ((), ())), preferred_element_type=f32
    )
    d_conv[tokens : tokens + 8, :] = jnp.zeros((8, channels), f32)
    first = jnp.concatenate([jnp.zeros((8, channels), f32), d_conv[0:8, :]], axis=0)
    head = taps_ref[0:1, :] * first[0:8, :]
    for k in range(1, taps):
        head = head + taps_ref[k : k + 1, :] * first[k : k + 8, :]
    head_ref[...] = head

    def finish(row):
        window = d_conv[pl.ds(row, rows_at_once + 8), :]
        now = window[0:rows_at_once, :]
        total = taps_ref[0:1, :] * now
        for k in range(1, taps):
            total = total + taps_ref[k : k + 1, :] * window[k : k + rows_at_once, :]
        d_branch_ref[pl.ds(row, rows_at_once), :] = total
        earlier = padded[pl.ds(row, rows_at_once + 8), :]
        for k in range(taps):
            product = now * earlier[8 - k : 8 - k + rows_at_once, :]
            taps_sum_ref[8 * k : 8 * k + 8, :] += jnp.sum(
                product.reshape(rows_at_once // 8, 8, channels), axis=0
            )

    over_rows(tokens, finish)


def place(me, own_ref, arrived, store):
    from_left, from_right, over, back, far = arrived
    for m, parts in enumerate(
        (
            (own_ref, from_right, back, far),
            (from_left, own_ref, from_right, over),
            (over, from_left, own_ref, from_right),
            (far, back, from_left, own_ref),
        )
    ):

        @pl.when(me == m)
        def _():
            for source, ref in enumerate(parts):
                store(source, ref)


def add_projection(
    own_ref, left_ref, right_ref, over_ref, back_ref, far_ref, weight_ref, inputs_ref, gain_ref, index_ref,
    residual_ref, normed_ref,
    mixed, rows,
):
    tokens, channels = own_ref.shape
    columns = weight_ref.shape[2]
    step = pl.program_id(0)

    def store(source, ref):
        def copy(row):
            at = pl.ds(row, rows_at_once)
            mixed[at, source * channels : (source + 1) * channels] = ref[at, :]

        over_rows(tokens, copy)

    @pl.when(step == 0)
    def _():
        place(index_ref[0], own_ref, (left_ref, right_ref, over_ref, back_ref, far_ref), store)

    total = inputs_ref[...].astype(f32) + jnp.dot(mixed[...], weight_ref[0], preferred_element_type=f32)
    residual_ref[...] = total
    rows[:, pl.ds(pl.multiple_of(step * columns, columns), columns)] = total

    @pl.when(step == pl.num_programs(0) - 1)
    def _():
        def normalise(row):
            at = pl.ds(row, rows_at_once)
            values = rows[at, :]
            inverse = inverse_rms(values)
            normed_ref[at, :] = (values * inverse * gain_ref[...]).astype(bf16)

        over_rows(tokens, normalise)


def residual_norm(own, arrived, weight, inputs, gain, index):
    tokens, channels = own.shape
    blocks, depth, columns = weight.shape
    width = inputs.shape[1]

    def whole(*dims):
        return pl.BlockSpec(dims, lambda j: (0,) * len(dims))

    return pl.pallas_call(
        add_projection,
        grid=(blocks,),
        in_specs=[whole(tokens, channels)] * 6
        + [
            pl.BlockSpec((1, depth, columns), lambda j: (j, 0, 0)),
            pl.BlockSpec((tokens, columns), lambda j: (0, j)),
            whole(1, width),
            pl.BlockSpec(memory_space=pltpu.SMEM),
        ],
        out_specs=[pl.BlockSpec((tokens, columns), lambda j: (0, j)), whole(tokens, width)],
        out_shape=[
            jax.ShapeDtypeStruct((tokens, width), f32),
            jax.ShapeDtypeStruct((tokens, width), bf16),
        ],
        scratch_shapes=[pltpu.VMEM((tokens, depth), bf16), pltpu.VMEM((tokens, width), f32)],
        compiler_params=pltpu.CompilerParams(vmem_limit_bytes=60 << 20),
        cost_estimate=pl.CostEstimate(
            flops=2 * tokens * depth * width,
            bytes_accessed=2 * (depth * width + 5 * tokens * width),
            transcendentals=0,
        ),
    )(own, *arrived, weight, inputs, gain, index)


def assembled(own, first, second, index, kind):
    size, width = own.shape
    peers = lax.axis_size("head")

    def body(index_ref, own_ref, left_ref, right_ref, over_ref, back_ref, far_ref, out_ref):
        step = pl.program_id(0)

        def store(source, ref):
            @pl.when(step == source)
            def _():
                def copy(row):
                    at = pl.ds(row, rows_at_once)
                    out_ref[at, :] = ref[at, :].astype(kind)

                over_rows(size, copy)

        place(index_ref[0], own_ref, (left_ref, right_ref, over_ref, back_ref, far_ref), store)

    return pl.pallas_call(
        body,
        grid_spec=pltpu.PrefetchScalarGridSpec(
            num_scalar_prefetch=1,
            grid=(peers,),
            in_specs=[pl.BlockSpec((size, width), lambda i, m: (0, 0))] * 6,
            out_specs=pl.BlockSpec((size, width), lambda i, m: (i, 0)),
        ),
        out_shape=jax.ShapeDtypeStruct((peers * size, width), kind),
        compiler_params=pltpu.CompilerParams(vmem_limit_bytes=26 << 20),
        cost_estimate=pl.CostEstimate(flops=1000, bytes_accessed=1000, transcendentals=0),
    )(index, own, *first, *second)


def weight_grads(products, extra=None):
    lefts = [left for left, _ in products]
    rights = [right for _, right in products]
    tokens, width = lefts[0].shape
    count = len(products)
    spans = [right.shape[1] for right in rights]
    total = sum(spans) + (0 if extra is None else extra.shape[1])
    block = 256

    def body(*refs):
        left_refs, right_refs, out_ref = refs[:count], refs[count : 2 * count], refs[-1]
        place = 0
        for left_ref, right_ref in zip(left_refs, right_refs, strict=True):
            span = right_ref.shape[1]
            out_ref[:, place : place + span] = lax.dot_general(
                left_ref[...], right_ref[...], (((0,), (0,)), ((), ())), preferred_element_type=f32
            ).astype(bf16)
            place += span
        if extra is not None:
            out_ref[:, place:] = refs[2 * count][...]

    extras = [] if extra is None else [extra]
    return pl.pallas_call(
        body,
        grid=(width // block,),
        in_specs=[pl.BlockSpec((tokens, block), lambda i: (0, i))] * count
        + [pl.BlockSpec((tokens, span), lambda i: (0, 0)) for span in spans]
        + [pl.BlockSpec((block, e.shape[1]), lambda i: (i, 0)) for e in extras],
        out_specs=pl.BlockSpec((block, total), lambda i: (i, 0)),
        out_shape=jax.ShapeDtypeStruct((width, total), bf16),
        compiler_params=pltpu.CompilerParams(vmem_limit_bytes=60 << 20),
        cost_estimate=pl.CostEstimate(
            flops=2 * tokens * width * total, bytes_accessed=2 * width * total, transcendentals=0
        ),
    )(*lefts, *rights, *extras)


def finish_ffn(summed, count):
    rows, width = summed.shape
    span = width // count

    def body(in_ref, *out_refs):
        def convert(row):
            at = pl.ds(row, rows_at_once)
            for k, ref in enumerate(out_refs[:-1]):
                ref[at, :] = in_ref[at, k * span : (k + 1) * span].astype(f32)

        over_rows(rows, convert)
        for place in range(0, span, 128):
            part = in_ref[:, (count - 1) * span + place : (count - 1) * span + place + 128]
            out_refs[-1][place : place + 128, :] = part.astype(f32).T

    shapes = [jax.ShapeDtypeStruct((rows, span), f32)] * (count - 1)
    return call(body, [*shapes, jax.ShapeDtypeStruct((span, rows), f32)], [], summed)


def finish_rest(summed, channels, blocks, block_width, taps, owners):
    rows = summed.shape[0]
    patch, kept = block_width // owners, channels // owners

    def body(in_ref, gate_ref, input_ref, out_ref, taps_ref, recur_ref, inward_ref, decay_ref):
        def convert(row):
            at = pl.ds(row, rows_at_once)
            gate_ref[at, :] = in_ref[at, 0:channels].astype(f32)
            input_ref[at, :] = in_ref[at, channels : 2 * channels].astype(f32)

        over_rows(rows, convert)
        out_ref[...] = in_ref[:, 2 * channels : 3 * channels].astype(f32).T
        small = in_ref[:, 3 * channels :].astype(f32)
        _, lanes = packed_shape(blocks, block_width, taps, owners, owners * rows)
        groups = -(-2 * block_width // lanes)
        for b in range(blocks):
            parts = []
            for g in range(groups):
                row = (g * blocks + b) * patch
                parts.append(small[row : row + patch, 0 : min(lanes, 2 * block_width - g * lanes)])
            both = jnp.concatenate(parts, axis=1)
            recur_ref[b] = both[:, 0:block_width]
            inward_ref[b] = both[:, block_width : 2 * block_width]
        used = groups * blocks * patch
        taps_ref[...] = small[used : used + taps, 0:kept]
        decay_ref[...] = small[used + taps : used + taps + 1, 0:kept]

    shapes = [
        (rows, channels),
        (rows, channels),
        (channels, rows),
        (taps, kept),
        (blocks, patch, block_width),
        (blocks, patch, block_width),
        (1, kept),
    ]
    return call(body, [jax.ShapeDtypeStruct(shape, f32) for shape in shapes], [], summed)


def add_last(base, last):
    cut = last[0].shape[0]

    def body(base_ref, first_ref, second_ref, out_ref):
        for start, ref in ((0, first_ref), (cut, second_ref)):

            def add(row):
                at = pl.ds(start + row, rows_at_once)
                out_ref[at, :] = (base_ref[at, :] + ref[pl.ds(row, rows_at_once), :].astype(f32)).astype(bf16)

            over_rows(ref.shape[0], add)

    return call(body, [jax.ShapeDtypeStruct(base.shape, bf16)], [], base, *last)[0]


def packed_shape(blocks, width, taps, owners, rows):
    groups = -(-2 * width // 128)
    if groups * blocks * (width // owners) + taps + 1 <= rows // owners:
        return 128, 128
    return groups * 128, 2 * width


def gate_grads(conv_low, d_both, taps_sums, decay_sums, blocks, owners, rows):
    channels = conv_low.shape[1]
    taps = taps_sums.shape[0] // 8
    width = channels // blocks
    patch, kept, span = width // owners, channels // owners, rows // owners
    columns, lanes = packed_shape(blocks, width, taps, owners, rows)

    def body(conv_ref, both_ref, taps_ref, decay_ref, out_ref):
        out_ref[...] = jnp.zeros((rows, columns), bf16)
        dense = lax.dot_general(
            conv_ref[...], both_ref[...], (((0,), (0,)), ((), ())), preferred_element_type=f32
        )
        sums = [jnp.sum(taps_ref[8 * k : 8 * k + 8, :], axis=0, keepdims=True) for k in range(taps)]
        sums.append(jnp.sum(decay_ref[...], axis=0, keepdims=True))
        sums = jnp.concatenate(sums, axis=0).astype(bf16)
        for b in range(blocks):
            at = slice(b * width, (b + 1) * width)
            recur = dense[at, b * width : (b + 1) * width].astype(bf16)
            inward = dense[at, channels + b * width : channels + (b + 1) * width].astype(bf16)
            both = jnp.concatenate([recur, inward], axis=1)
            for s in range(owners):
                mine = both[s * patch : (s + 1) * patch, :]
                for g, start in enumerate(range(0, 2 * width, lanes)):
                    row = s * span + (g * blocks + b) * patch
                    part = mine[:, start : start + lanes]
                    out_ref[row : row + patch, 0 : part.shape[1]] = part
        used = -(-2 * width // lanes) * blocks * patch
        for s in range(owners):
            row = s * span + used
            out_ref[row : row + taps + 1, 0:kept] = sums[:, s * kept : (s + 1) * kept]

    return call(
        body,
        [jax.ShapeDtypeStruct((rows, columns), bf16)],
        [],
        conv_low,
        d_both,
        taps_sums,
        decay_sums,
        flops=4 * conv_low.shape[0] * channels * channels,
    )[0]


def shifted(count, by):
    return [(i, (i + by) % count) for i in range(count)]


def exchanged(blocks):
    peers = lax.axis_size("head")
    return [lax.ppermute(blocks(k), "head", shifted(peers, k)) for k in range(1, peers)]


def block_of(array, where, dim):
    peers = lax.axis_size("head")
    size = array.shape[dim] // peers
    return lax.dynamic_slice_in_dim(array, (where % peers) * size, size, dim)


def shard(array, where):
    return block_of(array, where, 0)


def added(first, *others):
    total = first.astype(f32)
    for part in others:
        total = total + part.astype(f32)
    return total


def line_pairs(by):
    peers = lax.axis_size("head")
    return [(i, i + by) for i in range(peers) if 0 <= i + by < peers]


def scatter_first(low):
    me = lax.axis_index("head")
    across = shard(low, me + 2)
    return (
        lax.ppermute(across, "head", [(0, 1), (1, 2)]),
        lax.ppermute(across, "head", [(3, 2), (2, 1)]),
        lax.ppermute(shard(low, 3 - me), "head", [(0, 2), (3, 1)]),
    )


def by_rows(body, index, shares, rest, outputs, grant=60 << 20):
    peers = lax.axis_size("head")
    arrays = [array for array, _ in shares]
    rows = min(array.shape[0] // (1 if where is None else peers) for array, where in shares)
    size = min(rows, 64)
    steps = rows // size

    def row_spec(array, where):
        if where is None:
            return pl.BlockSpec((size, array.shape[1]), lambda i, m: (i, 0))
        return pl.BlockSpec(
            (size, array.shape[1]), lambda i, m, where=where: (lax.rem(m[0] + where + peers, peers) * steps + i, 0)
        )

    return pl.pallas_call(
        body,
        grid_spec=pltpu.PrefetchScalarGridSpec(
            num_scalar_prefetch=1,
            grid=(steps,),
            in_specs=[row_spec(*share) for share in shares]
            + [pl.BlockSpec(array.shape, lambda i, m: (0, 0)) for array in rest],
            out_specs=[
                pl.BlockSpec((1, width), lambda i, m: (0, 0))
                if height == 1
                else pl.BlockSpec((size, width), lambda i, m: (i, 0))
                for (height, width), _ in outputs
            ],
        ),
        out_shape=[jax.ShapeDtypeStruct(shape, kind) for shape, kind in outputs],
        compiler_params=pltpu.CompilerParams(vmem_limit_bytes=grant),
        cost_estimate=pl.CostEstimate(flops=1000, bytes_accessed=1000, transcendentals=0),
    )(index, *arrays, *rest)


def both_ways(me_ref, right_ref, left_ref, from_left_ref, from_right_ref, far_ref, to_right_ref, to_left_ref):
    far = far_ref[...].astype(f32)
    me = me_ref[0]
    to_right = right_ref[...].astype(f32) + from_left_ref[...].astype(f32)
    to_right_ref[...] = (to_right + jnp.where(me == 2, far, 0.0)).astype(bf16)
    to_left = left_ref[...].astype(f32) + from_right_ref[...].astype(f32)
    to_left_ref[...] = (to_left + jnp.where(me == 1, far, 0.0)).astype(bf16)


def scatter_second(low, first, index):
    from_left, from_right, far = first
    shape = far.shape
    to_right, to_left = by_rows(
        both_ways,
        index,
        [(low, 1), (low, -1), (from_left, None), (from_right, None), (far, None)],
        [],
        [(shape, bf16), (shape, bf16)],
    )
    return lax.ppermute(to_right, "head", line_pairs(1)), lax.ppermute(to_left, "head", line_pairs(-1))


def gather_first(own):
    return lax.ppermute(own, "head", line_pairs(1)), lax.ppermute(own, "head", line_pairs(-1))


def gather_second(first):
    me = lax.axis_index("head")
    from_left, from_right = first
    over = jnp.where(me == 1, from_left, from_right)
    back = jnp.where(me == 1, from_right, from_left)
    return (
        lax.ppermute(over, "head", [(1, 2), (2, 1)]),
        lax.ppermute(back, "head", [(1, 0), (2, 3)]),
        lax.ppermute(over, "head", [(1, 3), (2, 0)]),
    )


def line_turn(turn, sent):
    peers = lax.axis_size("head")
    return lax.ppermute(sent, "head", [(turn - 1, turn), (peers - turn, peers - turn - 1)])


together = lax.optimization_barrier


def inverse_rms(values):
    return lax.rsqrt(jnp.mean(values * values, axis=-1, keepdims=True) + epsilon)


def sum_up(ref, row):
    @pl.when(pl.program_id(0) == 0)
    def _():
        ref[...] = jnp.zeros(ref.shape, f32)

    ref[...] += row


def norm_grads(values, scales, grad):
    inverse = inverse_rms(values)
    unit = values * inverse
    scaled = grad * scales
    inner = jnp.mean(scaled * unit, axis=-1, keepdims=True)
    return inverse * (scaled - unit * inner), jnp.sum(grad * unit, axis=0, keepdims=True)


def second_norm(
    me_ref, own_ref, residual_ref, cotangent_ref, right_ref, left_ref, gain_ref, low_ref, d_resid_ref, sum_ref
):
    grad = own_ref[...].astype(f32) + right_ref[...].astype(f32) + left_ref[...].astype(f32)
    part, gains = norm_grads(residual_ref[...], gain_ref[...], grad)
    total = cotangent_ref[...].astype(f32) + part
    d_resid_ref[...] = total
    low_ref[...] = total.astype(bf16)
    sum_up(sum_ref, gains)


def first_norm(me_ref, own_ref, inputs_ref, right_ref, left_ref, d_resid_ref, gain_ref, low_ref, grad_ref, sum_ref):
    grad = own_ref[...].astype(f32) + right_ref[...].astype(f32) + left_ref[...].astype(f32)
    part, gains = norm_grads(inputs_ref[...].astype(f32), gain_ref[...], grad)
    total = d_resid_ref[...] + part
    grad_ref[...] = total
    low_ref[...] = total.astype(bf16)
    sum_up(sum_ref, gains)


def local(
    block_in,
    pre_gain,
    gate_proj,
    input_proj,
    conv_taps,
    recur_gate,
    input_gate,
    decay_param,
    out_proj,
    post_gain,
    ffn_gate,
    ffn_up,
    ffn_down,
    cotangent,
):
    tokens, width = block_in.shape
    channels = gate_proj.shape[1]
    blocks, block_width, _ = recur_gate.shape
    tap_count = conv_taps.shape[0]
    hidden_units = ffn_gate.shape[1]
    seq_count, seq_index = lax.axis_size("seq"), lax.axis_index("seq")
    head_count, head_index = lax.axis_size("head"), lax.axis_index("head")
    share = tokens // head_count
    slabs = (channels // 128, tokens, 128)
    here = seq_index.astype(jnp.int32).reshape(1)
    place_index = head_index.astype(jnp.int32).reshape(1)
    forward_pairs = [(i, i + 1) for i in range(seq_count - 1)]
    backward_pairs = [(i + 1, i) for i in range(seq_count - 1)]

    def mine(rows):
        return lax.dynamic_slice_in_dim(rows, head_index * share, share, 0)

    def struct(*dims, kind=f32):
        return jax.ShapeDtypeStruct(dims, kind)

    halo_in = lax.ppermute(block_in[tokens - 8 :], "seq", forward_pairs)
    columns = width // seq_count
    column_block = lax.dynamic_slice_in_dim(out_proj, seq_index * columns, columns, 1)
    column_block = lax.all_gather(column_block, "head").reshape(head_count * channels, columns)
    soft = jax.nn.softplus(-decay_param)[None, :]
    slide = sharpness * jax.nn.sigmoid(-decay_param)[None, :]

    def normalise(rows):
        values = rows.astype(f32)
        return (values * inverse_rms(values) * pre_gain).astype(bf16)

    normed = normalise(block_in)
    branch_in = jnp.dot(normed, input_proj, preferred_element_type=f32).astype(bf16)
    halo = jnp.dot(normalise(halo_in), input_proj, preferred_element_type=f32).astype(bf16)
    conv_low, recur_rate, input_rate, local_states, products, seg_ends, end, gates = call(
        forward_scan,
        [
            struct(tokens, channels, kind=bf16),
            struct(tokens, channels),
            struct(tokens, channels),
            struct(*slabs),
            struct(*slabs),
            struct(2 * segments, channels),
            struct(2, channels),
            struct(channels, 2 * channels, kind=bf16),
        ],
        [
            pltpu.VMEM((tokens + 8, channels), f32),
            pltpu.VMEM((tokens, 2 * channels), f32),
            pltpu.VMEM(slabs, f32),
            pltpu.VMEM(slabs, f32),
        ],
        branch_in,
        halo,
        conv_taps,
        soft,
        recur_gate,
        input_gate,
        flops=4 * tokens * channels * channels,
    )
    ends = lax.all_gather(end, "seq")
    gate_pre = jnp.dot(normed, gate_proj, preferred_element_type=f32)
    states, mixed_low, entry = call(
        mix,
        [struct(tokens, channels), struct(tokens, channels, kind=bf16), struct(1, channels)],
        [],
        gate_pre,
        local_states,
        products,
        seg_ends,
        ends,
        here,
        scalars=1,
    )
    column_block, _ = together((column_block, mixed_low))
    projection = lax.all_gather(column_block, "seq")
    if columns % 128:
        projection = jnp.moveaxis(projection, 0, 1).reshape(1, head_count * channels, width)
    first = gather_first(mixed_low)
    second = gather_second(first)
    d_hidden = jnp.einsum("td,fd->tf", cotangent, ffn_down, preferred_element_type=f32)
    second, d_hidden = together((second, d_hidden))
    residual, normed_two = residual_norm(
        mixed_low,
        (*first, *second),
        projection,
        block_in,
        post_gain[None, :],
        place_index,
    )
    ffn_gpre = jnp.dot(normed_two, ffn_gate, preferred_element_type=f32)
    ffn_upre = jnp.dot(normed_two, ffn_up, preferred_element_type=f32)
    value, slope = gelu_parts(ffn_gpre)
    hidden = (value * ffn_upre).astype(bf16)
    d_gpre = (d_hidden * ffn_upre * slope).astype(bf16)
    d_upre = (d_hidden * value).astype(bf16)
    d_normed_two = jnp.einsum(
        "tf,df->td", d_gpre, ffn_gate, preferred_element_type=f32
    ) + jnp.einsum("tf,df->td", d_upre, ffn_up, preferred_element_type=f32)
    d_normed_two = d_normed_two.astype(bf16)
    d_normed_two, hidden, d_gpre, d_upre = together((d_normed_two, hidden, d_gpre, d_upre))
    first = scatter_first(d_normed_two)
    grad_ffn = weight_grads([(normed_two, d_gpre), (normed_two, d_upre), (cotangent, hidden)])
    first, grad_ffn = together((first, grad_ffn))
    grad_ffn = lax.psum_scatter(grad_ffn, "seq", scatter_dimension=0, tiled=True)
    second = scatter_second(d_normed_two, first, place_index)
    ffn_out = jnp.dot(hidden, ffn_down, preferred_element_type=f32).astype(bf16)
    second, ffn_out = together((second, ffn_out))
    own_rows = (share, width)
    d_out_share, d_resid, grad_postgain = by_rows(
        second_norm,
        place_index,
        [(d_normed_two, 0), (residual, 0), (cotangent, 0), (second[0], None), (second[1], None)],
        [post_gain[None, :]],
        [(own_rows, bf16), (own_rows, f32), ((1, width), f32)],
        grant=26 << 20,
    )
    first = gather_first(d_out_share)
    first, ffn_out = together((first, ffn_out))
    second = gather_second(first)
    cut = tokens * 5 // 8
    ffn_halves = [ffn_out[:cut], ffn_out[cut:]]
    turn_one = [line_turn(1, ffn_halves[0])]
    d_out_low = assembled(d_out_share, first, second, place_index, bf16)
    d_out_low, ffn_halves[1] = together((d_out_low, ffn_halves[1]))
    turn_one.append(line_turn(1, ffn_halves[1]))
    d_mixed = jnp.einsum("td,cd->tc", d_out_low, out_proj, preferred_element_type=f32)
    sent = added(ffn_halves[0], turn_one[0]).astype(bf16)
    d_mixed, sent = together((d_mixed, sent))
    turn_two = [line_turn(2, sent)]
    d_gate_low, grad_local, grad_prod, grad_segs, grad_end = call(
        backward_scan,
        [
            struct(tokens, channels, kind=bf16),
            struct(*slabs),
            struct(*slabs),
            struct(2 * segments, channels),
            struct(1, channels),
        ],
        [pltpu.VMEM(slabs, f32), pltpu.VMEM(slabs, f32)],
        d_mixed,
        gate_pre,
        states,
        recur_rate,
        soft,
    )
    backs = lax.all_gather(grad_end, "seq")
    sent = added(ffn_halves[1], turn_one[1]).astype(bf16)
    backs, sent = together((backs, sent))
    turn_two.append(line_turn(2, sent))
    d_both, d_branch, head_rows, decay_sums, taps_sums = call(
        backward_terms,
        [
            struct(tokens, 2 * channels, kind=bf16),
            struct(tokens, channels),
            struct(8, channels),
            struct(8, channels),
            struct(8 * tap_count, channels),
        ],
        [
            pltpu.VMEM((tokens + 8, channels), f32),
            pltpu.VMEM((tokens + 8, channels), f32),
            pltpu.VMEM((tokens + 8, channels), f32),
        ],
        grad_local,
        grad_prod,
        grad_segs,
        ends,
        backs,
        recur_rate,
        input_rate,
        conv_low,
        states,
        entry,
        soft,
        slide,
        conv_taps,
        branch_in,
        halo,
        gates,
        here,
        scalars=1,
        flops=4 * tokens * channels * channels,
    )
    sent = added(ffn_halves[0], turn_two[0]).astype(bf16)
    head_rows, d_branch, d_both, sent = together((head_rows, d_branch, d_both, sent))
    later_rows = lax.ppermute(head_rows, "seq", backward_pairs)
    turn_three = [line_turn(3, sent)]
    d_branch_low = (d_branch + jnp.pad(later_rows, ((tokens - 8, 0), (0, 0)))).astype(bf16)
    d_normed = jnp.einsum("tc,dc->td", d_gate_low, gate_proj, preferred_element_type=f32) + jnp.einsum(
        "tc,dc->td", d_branch_low, input_proj, preferred_element_type=f32
    )
    d_normed = d_normed.astype(bf16)
    d_normed, conv_low, d_both = together((d_normed, conv_low, d_both))
    first = scatter_first(d_normed)
    packed = gate_grads(conv_low, d_both, taps_sums, decay_sums, blocks, seq_count, width)
    grad_rest = weight_grads([(normed, d_gate_low), (normed, d_branch_low), (d_out_low, mixed_low)], packed)
    grad_ffn = finish_ffn(grad_ffn, 3)
    first, grad_rest, turn_three, turn_two, grad_ffn = together(
        (first, grad_rest, turn_three, turn_two, grad_ffn)
    )
    second = scatter_second(d_normed, first, place_index)
    sent = added(ffn_halves[1], turn_two[1]).astype(bf16)
    turn_three.append(line_turn(3, sent))
    grad_rest = lax.psum_scatter(grad_rest, "seq", scatter_dimension=0, tiled=True)
    grad_low, grad_input, grad_pregain = by_rows(
        first_norm,
        place_index,
        [(d_normed, 0), (block_in, 0), (second[0], None), (second[1], None), (d_resid, None)],
        [pre_gain[None, :]],
        [(own_rows, bf16), (own_rows, f32), ((1, width), f32)],
    )
    first = gather_first(grad_low)
    gains = jnp.concatenate([grad_pregain, grad_postgain], axis=0)
    gain_pieces = exchanged(lambda k: gains)
    base = residual + added(ffn_out, jnp.concatenate(turn_one), jnp.concatenate(turn_two))
    block_out = add_last(base, turn_three)
    first, block_out = together((first, block_out))
    second = gather_second(first)
    gains = jnp.sum(lax.all_gather(sum(gain_pieces, gains), "seq"), axis=0)
    gain_share = width // seq_count
    gains = lax.dynamic_slice_in_dim(gains, seq_index * gain_share, gain_share, 1)
    grad_rest, grad_ffn = together((grad_rest, grad_ffn))
    grad_rest = finish_rest(grad_rest, channels, blocks, block_width, tap_count, seq_count)
    second, grad_rest = together((second, grad_rest))
    grad_gate_proj, grad_input_proj, grad_out_proj, grad_taps, grad_recur, grad_inward, grad_decay = grad_rest
    grad_input = assembled(grad_input, first, second, place_index, f32)
    return (
        block_out,
        grad_input,
        gains[0],
        grad_gate_proj,
        grad_input_proj,
        grad_taps,
        grad_recur,
        grad_inward,
        grad_decay[0],
        grad_out_proj,
        gains[1],
        *grad_ffn,
    )


def solution(mesh):
    placed = (
        P("seq", None),
        P(),
        P(None, "head"),
        P(None, "head"),
        P(None, "head"),
        P("head", None, None),
        P("head", None, None),
        P("head"),
        P("head", None),
        P(),
        P(None, "head"),
        P(None, "head"),
        P("head", None),
        P("seq", None),
    )
    return jax.shard_map(
        local,
        mesh=mesh,
        in_specs=placed,
        out_specs=(
            P("seq", None),
            P("seq", None),
            P("seq"),
            P("seq", "head"),
            P("seq", "head"),
            P(None, ("head", "seq")),
            P("head", "seq", None),
            P("head", "seq", None),
            P(("head", "seq")),
            P("head", "seq"),
            P("seq"),
            P("seq", "head"),
            P("seq", "head"),
            P("head", "seq"),
        ),
        check_vma=False,
    )
```

```python
import jax
import jax.numpy as jnp
from jax import lax
from jax.experimental import pallas as pl
from jax.experimental.pallas import tpu as pltpu
from jax.sharding import PartitionSpec as P

epsilon = 1e-06
sharpness = 8.0
segments = 8
rows_at_once = 32
root_two_over_pi = 0.7978845608028654
cubic = 0.044715
f32 = jnp.float32
bf16 = jnp.bfloat16


def call(body, out_shape, scratch, *operands, scalars=0, flops=0):
    vectors = len(operands) - scalars
    moved = sum(x.size * x.dtype.itemsize for x in (*operands, *out_shape))
    return pl.pallas_call(
        body,
        out_shape=out_shape,
        in_specs=[pl.BlockSpec(memory_space=pltpu.VMEM)] * vectors
        + [pl.BlockSpec(memory_space=pltpu.SMEM)] * scalars,
        out_specs=[pl.BlockSpec(memory_space=pltpu.VMEM)] * len(out_shape),
        scratch_shapes=scratch,
        compiler_params=pltpu.CompilerParams(vmem_limit_bytes=32 << 20),
        cost_estimate=pl.CostEstimate(flops=1000, bytes_accessed=1000, transcendentals=0),
    )(*operands)


def split(ref, at, value):
    for j in range(ref.shape[0]):
        ref[j, at, :] = value[:, 128 * j : 128 * (j + 1)]


def joined(ref, at):
    return jnp.concatenate([ref[j, at, :] for j in range(ref.shape[0])], axis=1)


def over_rows(tokens, body):
    @pl.loop(0, tokens // rows_at_once)
    def _(step):
        body(pl.multiple_of(step * rows_at_once, rows_at_once))


def minus_expm1(v):
    series = 1.0 / 5040.0
    for term in (720.0, 120.0, 24.0, 6.0, 2.0, 1.0):
        series = series * v + 1.0 / term
    return jnp.where(v > -0.25, -v * series, 1.0 - jnp.exp(v))


def gelu_parts(v):
    bent = jnp.tanh(root_two_over_pi * (v + cubic * v * v * v))
    half = 0.5 * (1.0 + bent)
    slope = half + 0.5 * v * (1.0 - bent * bent) * root_two_over_pi * (1.0 + 3.0 * cubic * v * v)
    return v * half, slope


def forward_scan(
    branch_ref, halo_ref, taps_ref, soft_ref, recur_gate_ref, input_gate_ref,
    conv_ref, recur_ref, input_ref, local_ref, prod_ref, seg_ref, end_ref, gates_ref,
    padded, pre, decay, drive,
):
    tokens, channels = branch_ref.shape
    taps = taps_ref.shape[0]
    steps = tokens // segments
    blocks, width, _ = recur_gate_ref.shape
    gates_ref[...] = jnp.zeros((channels, 2 * channels), bf16)
    for b in range(blocks):
        rows = pl.ds(b * width, width)
        gates_ref[rows, b * width : (b + 1) * width] = recur_gate_ref[b]
        gates_ref[rows, channels + b * width : channels + (b + 1) * width] = input_gate_ref[b]
    padded[0:8, :] = halo_ref[...].astype(f32)

    def fill(row):
        padded[pl.ds(row + 8, rows_at_once), :] = branch_ref[pl.ds(row, rows_at_once), :].astype(f32)

    over_rows(tokens, fill)

    def convolve(row):
        window = padded[pl.ds(row, rows_at_once + 8), :]
        total = taps_ref[0:1, :] * window[8:, :]
        for k in range(1, taps):
            total = total + taps_ref[k : k + 1, :] * window[8 - k : 8 - k + rows_at_once, :]
        conv_ref[pl.ds(row, rows_at_once), :] = total.astype(bf16)

    over_rows(tokens, convolve)
    pre[...] = jnp.dot(conv_ref[...], gates_ref[...], preferred_element_type=f32)

    def terms(row):
        at = pl.ds(row, rows_at_once)
        recur = jax.nn.sigmoid(pre[at, 0:channels])
        inward = jax.nn.sigmoid(pre[at, channels : 2 * channels])
        log_decay = -sharpness * recur * soft_ref[...]
        recur_ref[at, :] = recur
        input_ref[at, :] = inward
        split(decay, at, jnp.exp(log_decay))
        split(drive, at, jnp.sqrt(minus_expm1(2.0 * log_decay)) * inward * conv_ref[at, :].astype(f32))

    over_rows(tokens, terms)

    slabs = channels // 128

    def step(i, carried):
        at = pl.ds(i, segments, stride=steps)
        new = []
        for j in range(slabs):
            state, product = carried[j]
            a = decay[j, at, :]
            state = a * state + drive[j, at, :]
            product = a * product
            local_ref[j, at, :] = state
            prod_ref[j, at, :] = product
            new.append((state, product))
        return tuple(new)

    start = ((jnp.zeros((segments, 128), f32), jnp.ones((segments, 128), f32)),) * slabs
    last = lax.fori_loop(0, steps, step, start, unroll=4)
    state = jnp.concatenate([pair[0] for pair in last], axis=1)
    product = jnp.concatenate([pair[1] for pair in last], axis=1)
    seg_ref[0:segments, :] = product
    seg_ref[segments : 2 * segments, :] = state
    whole = jnp.ones((1, channels), f32)
    end = jnp.zeros((1, channels), f32)
    for s in range(segments):
        end = product[s : s + 1, :] * end + state[s : s + 1, :]
        whole = product[s : s + 1, :] * whole
    end_ref[0:1, :] = whole
    end_ref[1:2, :] = end


def mix(gate_ref, local_ref, prod_ref, seg_ref, ends_ref, index_ref, states_ref, mixed_ref, entry_ref):
    tokens, channels = gate_ref.shape
    steps = tokens // segments
    index = index_ref[0]
    carry = jnp.zeros((1, channels), f32)
    for j in range(ends_ref.shape[0]):
        new = ends_ref[j, 0:1, :] * carry + ends_ref[j, 1:2, :]
        carry = jnp.where(j < index, new, carry)
    entry_ref[...] = carry
    for s in range(segments):
        held = carry

        @pl.loop(0, steps // rows_at_once)
        def _(i):
            at = pl.ds(pl.multiple_of(s * steps + i * rows_at_once, rows_at_once), rows_at_once)
            states = joined(local_ref, at) + joined(prod_ref, at) * held
            states_ref[at, :] = states
            gate, _ = gelu_parts(gate_ref[at, :])
            mixed_ref[at, :] = (gate * states).astype(bf16)

        carry = seg_ref[s : s + 1, :] * carry + seg_ref[segments + s : segments + s + 1, :]


def backward_scan(
    d_mixed_ref, gate_ref, states_ref, recur_ref, soft_ref,
    d_gate_ref, local_ref, prod_ref, seg_ref, end_ref,
    decay, d_state,
):
    tokens, channels = gate_ref.shape
    steps = tokens // segments

    def terms(row):
        at = pl.ds(row, rows_at_once)
        d_mixed = d_mixed_ref[at, :].astype(f32)
        value, slope = gelu_parts(gate_ref[at, :])
        d_gate_ref[at, :] = (d_mixed * states_ref[at, :] * slope).astype(bf16)
        split(d_state, at, d_mixed * value)
        split(decay, at, jnp.exp(-sharpness * recur_ref[at, :] * soft_ref[...]))

    over_rows(tokens, terms)

    slabs = channels // 128

    def step(k, carried):
        at = pl.ds(steps - 1 - k, segments, stride=steps)
        new = []
        for j in range(slabs):
            into, reach = carried[j]
            a = decay[j, at, :]
            grad = d_state[j, at, :] + into
            local_ref[j, at, :] = grad
            prod_ref[j, at, :] = reach
            new.append((a * grad, a * reach))
        return tuple(new)

    start = ((jnp.zeros((segments, 128), f32), jnp.ones((segments, 128), f32)),) * slabs
    last = lax.fori_loop(0, steps, step, start, unroll=4)
    into = jnp.concatenate([pair[0] for pair in last], axis=1)
    reach = jnp.concatenate([pair[1] for pair in last], axis=1)
    seg_ref[0:segments, :] = reach
    seg_ref[segments : 2 * segments, :] = into
    end = jnp.zeros((1, channels), f32)
    for s in reversed(range(segments)):
        end = reach[s : s + 1, :] * end + into[s : s + 1, :]
    end_ref[...] = end


def backward_terms(
    local_ref, prod_ref, seg_ref, ends_ref, backs_ref, recur_ref, input_ref, conv_ref, states_ref, entry_ref,
    soft_ref, slide_ref, taps_ref, branch_ref, halo_ref, gates_ref, index_ref,
    d_both_ref, d_branch_ref, head_ref, decay_sum_ref, taps_sum_ref,
    before, d_conv, padded,
):
    tokens, channels = states_ref.shape
    taps = taps_ref.shape[0]
    steps = tokens // segments
    index = index_ref[0]
    padded[0:8, :] = halo_ref[...].astype(f32)
    before[0:8, :] = jnp.broadcast_to(entry_ref[...], (8, channels))
    carry = jnp.zeros((1, channels), f32)
    for j in reversed(range(ends_ref.shape[0])):
        new = ends_ref[j, 0:1, :] * carry + backs_ref[j, 0:1, :]
        carry = jnp.where(j > index, new, carry)
    decay_sum_ref[...] = jnp.zeros((8, channels), f32)
    taps_sum_ref[...] = jnp.zeros((8 * taps, channels), f32)

    def fill(row):
        padded[pl.ds(row + 8, rows_at_once), :] = branch_ref[pl.ds(row, rows_at_once), :].astype(f32)
        before[pl.ds(row + 8, rows_at_once), :] = states_ref[pl.ds(row, rows_at_once), :]

    over_rows(tokens, fill)
    for s in reversed(range(segments)):
        held = carry

        @pl.loop(0, steps // rows_at_once)
        def _(i):
            row = pl.multiple_of(s * steps + i * rows_at_once, rows_at_once)
            at = pl.ds(row, rows_at_once)
            grad = joined(local_ref, at) + joined(prod_ref, at) * held
            recur = recur_ref[at, :]
            inward = input_ref[at, :]
            conv = conv_ref[at, :].astype(f32)
            log_decay = -sharpness * recur * soft_ref[...]
            decay = jnp.exp(log_decay)
            root = jnp.sqrt(minus_expm1(2.0 * log_decay))
            previous = before[pl.ds(row, rows_at_once + 8), :][7 : 7 + rows_at_once, :]
            push = grad * inward
            total = decay * (grad * previous - push * decay * conv / root)
            rate = recur * total
            d_both_ref[at, 0:channels] = (-sharpness * soft_ref[...] * (1.0 - recur) * rate).astype(bf16)
            d_both_ref[at, channels : 2 * channels] = (push * root * conv * (1.0 - inward)).astype(bf16)
            d_conv[at, :] = push * root
            decay_sum_ref[...] += jnp.sum(rate.reshape(rows_at_once // 8, 8, channels), axis=0)

        carry = seg_ref[s : s + 1, :] * carry + seg_ref[segments + s : segments + s + 1, :]
    decay_sum_ref[...] = decay_sum_ref[...] * slide_ref[...]
    d_conv[0:tokens, :] += lax.dot_general(
        d_both_ref[...], gates_ref[...], (((1,), (1,)), ((), ())), preferred_element_type=f32
    )
    d_conv[tokens : tokens + 8, :] = jnp.zeros((8, channels), f32)
    first = jnp.concatenate([jnp.zeros((8, channels), f32), d_conv[0:8, :]], axis=0)
    head = taps_ref[0:1, :] * first[0:8, :]
    for k in range(1, taps):
        head = head + taps_ref[k : k + 1, :] * first[k : k + 8, :]
    head_ref[...] = head

    def finish(row):
        window = d_conv[pl.ds(row, rows_at_once + 8), :]
        now = window[0:rows_at_once, :]
        total = taps_ref[0:1, :] * now
        for k in range(1, taps):
            total = total + taps_ref[k : k + 1, :] * window[k : k + rows_at_once, :]
        d_branch_ref[pl.ds(row, rows_at_once), :] = total
        earlier = padded[pl.ds(row, rows_at_once + 8), :]
        for k in range(taps):
            product = now * earlier[8 - k : 8 - k + rows_at_once, :]
            taps_sum_ref[8 * k : 8 * k + 8, :] += jnp.sum(
                product.reshape(rows_at_once // 8, 8, channels), axis=0
            )

    over_rows(tokens, finish)


def place(me, own_ref, arrived, store):
    from_left, from_right, over, back, far = arrived
    for m, parts in enumerate(
        (
            (own_ref, from_right, back, far),
            (from_left, own_ref, from_right, over),
            (over, from_left, own_ref, from_right),
            (far, back, from_left, own_ref),
        )
    ):

        @pl.when(me == m)
        def _():
            for source, ref in enumerate(parts):
                store(source, ref)


def add_projection(
    own_ref, left_ref, right_ref, over_ref, back_ref, far_ref, weight_ref, inputs_ref, gain_ref, index_ref,
    residual_ref, normed_ref,
    mixed, rows,
):
    tokens, channels = own_ref.shape
    columns = weight_ref.shape[2]
    step = pl.program_id(0)

    def store(source, ref):
        def copy(row):
            at = pl.ds(row, rows_at_once)
            mixed[at, source * channels : (source + 1) * channels] = ref[at, :]

        over_rows(tokens, copy)

    @pl.when(step == 0)
    def _():
        place(index_ref[0], own_ref, (left_ref, right_ref, over_ref, back_ref, far_ref), store)

    total = inputs_ref[...].astype(f32) + jnp.dot(mixed[...], weight_ref[0], preferred_element_type=f32)
    residual_ref[...] = total
    rows[:, pl.ds(pl.multiple_of(step * columns, columns), columns)] = total

    @pl.when(step == pl.num_programs(0) - 1)
    def _():
        def normalise(row):
            at = pl.ds(row, rows_at_once)
            values = rows[at, :]
            inverse = inverse_rms(values)
            normed_ref[at, :] = (values * inverse * gain_ref[...]).astype(bf16)

        over_rows(tokens, normalise)


def residual_norm(own, arrived, weight, inputs, gain, index):
    tokens, channels = own.shape
    blocks, depth, columns = weight.shape
    width = inputs.shape[1]

    def whole(*dims):
        return pl.BlockSpec(dims, lambda j: (0,) * len(dims))

    return pl.pallas_call(
        add_projection,
        grid=(blocks,),
        in_specs=[whole(tokens, channels)] * 6
        + [
            pl.BlockSpec((1, depth, columns), lambda j: (j, 0, 0)),
            pl.BlockSpec((tokens, columns), lambda j: (0, j)),
            whole(1, width),
            pl.BlockSpec(memory_space=pltpu.SMEM),
        ],
        out_specs=[pl.BlockSpec((tokens, columns), lambda j: (0, j)), whole(tokens, width)],
        out_shape=[
            jax.ShapeDtypeStruct((tokens, width), f32),
            jax.ShapeDtypeStruct((tokens, width), bf16),
        ],
        scratch_shapes=[pltpu.VMEM((tokens, depth), bf16), pltpu.VMEM((tokens, width), f32)],
        compiler_params=pltpu.CompilerParams(vmem_limit_bytes=60 << 20),
        cost_estimate=pl.CostEstimate(
            flops=2 * tokens * depth * width,
            bytes_accessed=2 * (depth * width + 5 * tokens * width),
            transcendentals=0,
        ),
    )(own, *arrived, weight, inputs, gain, index)


def assembled(own, first, second, index, kind):
    size, width = own.shape
    peers = lax.axis_size("head")

    def body(index_ref, own_ref, left_ref, right_ref, over_ref, back_ref, far_ref, out_ref):
        step = pl.program_id(0)

        def store(source, ref):
            @pl.when(step == source)
            def _():
                def copy(row):
                    at = pl.ds(row, rows_at_once)
                    out_ref[at, :] = ref[at, :].astype(kind)

                over_rows(size, copy)

        place(index_ref[0], own_ref, (left_ref, right_ref, over_ref, back_ref, far_ref), store)

    return pl.pallas_call(
        body,
        grid_spec=pltpu.PrefetchScalarGridSpec(
            num_scalar_prefetch=1,
            grid=(peers,),
            in_specs=[pl.BlockSpec((size, width), lambda i, m: (0, 0))] * 6,
            out_specs=pl.BlockSpec((size, width), lambda i, m: (i, 0)),
        ),
        out_shape=jax.ShapeDtypeStruct((peers * size, width), kind),
        compiler_params=pltpu.CompilerParams(vmem_limit_bytes=26 << 20),
        cost_estimate=pl.CostEstimate(flops=1000, bytes_accessed=1000, transcendentals=0),
    )(index, own, *first, *second)


def weight_grads(products, extra=None):
    lefts = [left for left, _ in products]
    rights = [right for _, right in products]
    tokens, width = lefts[0].shape
    count = len(products)
    spans = [right.shape[1] for right in rights]
    total = sum(spans) + (0 if extra is None else extra.shape[1])
    block = 256

    def body(*refs):
        left_refs, right_refs, out_ref = refs[:count], refs[count : 2 * count], refs[-1]
        place = 0
        for left_ref, right_ref in zip(left_refs, right_refs, strict=True):
            span = right_ref.shape[1]
            out_ref[:, place : place + span] = lax.dot_general(
                left_ref[...], right_ref[...], (((0,), (0,)), ((), ())), preferred_element_type=f32
            ).astype(bf16)
            place += span
        if extra is not None:
            out_ref[:, place:] = refs[2 * count][...]

    extras = [] if extra is None else [extra]
    return pl.pallas_call(
        body,
        grid=(width // block,),
        in_specs=[pl.BlockSpec((tokens, block), lambda i: (0, i))] * count
        + [pl.BlockSpec((tokens, span), lambda i: (0, 0)) for span in spans]
        + [pl.BlockSpec((block, e.shape[1]), lambda i: (i, 0)) for e in extras],
        out_specs=pl.BlockSpec((block, total), lambda i: (i, 0)),
        out_shape=jax.ShapeDtypeStruct((width, total), bf16),
        compiler_params=pltpu.CompilerParams(vmem_limit_bytes=60 << 20),
        cost_estimate=pl.CostEstimate(
            flops=2 * tokens * width * total, bytes_accessed=2 * width * total, transcendentals=0
        ),
    )(*lefts, *rights, *extras)


def finish_ffn(summed, count):
    rows, width = summed.shape
    span = width // count

    def body(in_ref, *out_refs):
        def convert(row):
            at = pl.ds(row, rows_at_once)
            for k, ref in enumerate(out_refs[:-1]):
                ref[at, :] = in_ref[at, k * span : (k + 1) * span].astype(f32)

        over_rows(rows, convert)
        for place in range(0, span, 128):
            part = in_ref[:, (count - 1) * span + place : (count - 1) * span + place + 128]
            out_refs[-1][place : place + 128, :] = part.astype(f32).T

    shapes = [jax.ShapeDtypeStruct((rows, span), f32)] * (count - 1)
    return call(body, [*shapes, jax.ShapeDtypeStruct((span, rows), f32)], [], summed)


def finish_rest(summed, channels, blocks, block_width, taps, owners):
    rows = summed.shape[0]
    patch, kept = block_width // owners, channels // owners

    def body(in_ref, gate_ref, input_ref, out_ref, taps_ref, recur_ref, inward_ref, decay_ref):
        def convert(row):
            at = pl.ds(row, rows_at_once)
            gate_ref[at, :] = in_ref[at, 0:channels].astype(f32)
            input_ref[at, :] = in_ref[at, channels : 2 * channels].astype(f32)

        over_rows(rows, convert)
        out_ref[...] = in_ref[:, 2 * channels : 3 * channels].astype(f32).T
        small = in_ref[:, 3 * channels :].astype(f32)
        _, lanes = packed_shape(blocks, block_width, taps, owners, owners * rows)
        groups = -(-2 * block_width // lanes)
        for b in range(blocks):
            parts = []
            for g in range(groups):
                row = (g * blocks + b) * patch
                parts.append(small[row : row + patch, 0 : min(lanes, 2 * block_width - g * lanes)])
            both = jnp.concatenate(parts, axis=1)
            recur_ref[b] = both[:, 0:block_width]
            inward_ref[b] = both[:, block_width : 2 * block_width]
        used = groups * blocks * patch
        taps_ref[...] = small[used : used + taps, 0:kept]
        decay_ref[...] = small[used + taps : used + taps + 1, 0:kept]

    shapes = [
        (rows, channels),
        (rows, channels),
        (channels, rows),
        (taps, kept),
        (blocks, patch, block_width),
        (blocks, patch, block_width),
        (1, kept),
    ]
    return call(body, [jax.ShapeDtypeStruct(shape, f32) for shape in shapes], [], summed)


def add_last(base, last):
    cut = last[0].shape[0]

    def body(base_ref, first_ref, second_ref, out_ref):
        for start, ref in ((0, first_ref), (cut, second_ref)):

            def add(row):
                at = pl.ds(start + row, rows_at_once)
                out_ref[at, :] = (base_ref[at, :] + ref[pl.ds(row, rows_at_once), :].astype(f32)).astype(bf16)

            over_rows(ref.shape[0], add)

    return call(body, [jax.ShapeDtypeStruct(base.shape, bf16)], [], base, *last)[0]


def packed_shape(blocks, width, taps, owners, rows):
    groups = -(-2 * width // 128)
    if groups * blocks * (width // owners) + taps + 1 <= rows // owners:
        return 128, 128
    return groups * 128, 2 * width


def gate_grads(conv_low, d_both, taps_sums, decay_sums, blocks, owners, rows):
    channels = conv_low.shape[1]
    taps = taps_sums.shape[0] // 8
    width = channels // blocks
    patch, kept, span = width // owners, channels // owners, rows // owners
    columns, lanes = packed_shape(blocks, width, taps, owners, rows)

    def body(conv_ref, both_ref, taps_ref, decay_ref, out_ref):
        out_ref[...] = jnp.zeros((rows, columns), bf16)
        dense = lax.dot_general(
            conv_ref[...], both_ref[...], (((0,), (0,)), ((), ())), preferred_element_type=f32
        )
        sums = [jnp.sum(taps_ref[8 * k : 8 * k + 8, :], axis=0, keepdims=True) for k in range(taps)]
        sums.append(jnp.sum(decay_ref[...], axis=0, keepdims=True))
        sums = jnp.concatenate(sums, axis=0).astype(bf16)
        for b in range(blocks):
            at = slice(b * width, (b + 1) * width)
            recur = dense[at, b * width : (b + 1) * width].astype(bf16)
            inward = dense[at, channels + b * width : channels + (b + 1) * width].astype(bf16)
            both = jnp.concatenate([recur, inward], axis=1)
            for s in range(owners):
                mine = both[s * patch : (s + 1) * patch, :]
                for g, start in enumerate(range(0, 2 * width, lanes)):
                    row = s * span + (g * blocks + b) * patch
                    part = mine[:, start : start + lanes]
                    out_ref[row : row + patch, 0 : part.shape[1]] = part
        used = -(-2 * width // lanes) * blocks * patch
        for s in range(owners):
            row = s * span + used
            out_ref[row : row + taps + 1, 0:kept] = sums[:, s * kept : (s + 1) * kept]

    return call(
        body,
        [jax.ShapeDtypeStruct((rows, columns), bf16)],
        [],
        conv_low,
        d_both,
        taps_sums,
        decay_sums,
        flops=4 * conv_low.shape[0] * channels * channels,
    )[0]


def shifted(count, by):
    return [(i, (i + by) % count) for i in range(count)]


def exchanged(blocks):
    peers = lax.axis_size("head")
    return [lax.ppermute(blocks(k), "head", shifted(peers, k)) for k in range(1, peers)]


def block_of(array, where, dim):
    peers = lax.axis_size("head")
    size = array.shape[dim] // peers
    return lax.dynamic_slice_in_dim(array, (where % peers) * size, size, dim)


def shard(array, where):
    return block_of(array, where, 0)


def added(first, *others):
    total = first.astype(f32)
    for part in others:
        total = total + part.astype(f32)
    return total


def line_pairs(by):
    peers = lax.axis_size("head")
    return [(i, i + by) for i in range(peers) if 0 <= i + by < peers]


def scatter_first(low):
    me = lax.axis_index("head")
    across = shard(low, me + 2)
    return (
        lax.ppermute(across, "head", [(0, 1), (1, 2)]),
        lax.ppermute(across, "head", [(3, 2), (2, 1)]),
        lax.ppermute(shard(low, 3 - me), "head", [(0, 2), (3, 1)]),
    )


def by_rows(body, index, shares, rest, outputs, grant=60 << 20):
    peers = lax.axis_size("head")
    arrays = [array for array, _ in shares]
    rows = min(array.shape[0] // (1 if where is None else peers) for array, where in shares)
    size = min(rows, 64)
    steps = rows // size

    def row_spec(array, where):
        if where is None:
            return pl.BlockSpec((size, array.shape[1]), lambda i, m: (i, 0))
        return pl.BlockSpec(
            (size, array.shape[1]), lambda i, m, where=where: (lax.rem(m[0] + where + peers, peers) * steps + i, 0)
        )

    return pl.pallas_call(
        body,
        grid_spec=pltpu.PrefetchScalarGridSpec(
            num_scalar_prefetch=1,
            grid=(steps,),
            in_specs=[row_spec(*share) for share in shares]
            + [pl.BlockSpec(array.shape, lambda i, m: (0, 0)) for array in rest],
            out_specs=[
                pl.BlockSpec((1, width), lambda i, m: (0, 0))
                if height == 1
                else pl.BlockSpec((size, width), lambda i, m: (i, 0))
                for (height, width), _ in outputs
            ],
        ),
        out_shape=[jax.ShapeDtypeStruct(shape, kind) for shape, kind in outputs],
        compiler_params=pltpu.CompilerParams(vmem_limit_bytes=grant),
        cost_estimate=pl.CostEstimate(flops=1000, bytes_accessed=1000, transcendentals=0),
    )(index, *arrays, *rest)


def both_ways(me_ref, right_ref, left_ref, from_left_ref, from_right_ref, far_ref, to_right_ref, to_left_ref):
    far = far_ref[...].astype(f32)
    me = me_ref[0]
    to_right = right_ref[...].astype(f32) + from_left_ref[...].astype(f32)
    to_right_ref[...] = (to_right + jnp.where(me == 2, far, 0.0)).astype(bf16)
    to_left = left_ref[...].astype(f32) + from_right_ref[...].astype(f32)
    to_left_ref[...] = (to_left + jnp.where(me == 1, far, 0.0)).astype(bf16)


def scatter_second(low, first, index):
    from_left, from_right, far = first
    shape = far.shape
    to_right, to_left = by_rows(
        both_ways,
        index,
        [(low, 1), (low, -1), (from_left, None), (from_right, None), (far, None)],
        [],
        [(shape, bf16), (shape, bf16)],
    )
    return lax.ppermute(to_right, "head", line_pairs(1)), lax.ppermute(to_left, "head", line_pairs(-1))


def gather_first(own):
    return lax.ppermute(own, "head", line_pairs(1)), lax.ppermute(own, "head", line_pairs(-1))


def gather_second(first):
    me = lax.axis_index("head")
    from_left, from_right = first
    over = jnp.where(me == 1, from_left, from_right)
    back = jnp.where(me == 1, from_right, from_left)
    return (
        lax.ppermute(over, "head", [(1, 2), (2, 1)]),
        lax.ppermute(back, "head", [(1, 0), (2, 3)]),
        lax.ppermute(over, "head", [(1, 3), (2, 0)]),
    )


def line_turn(turn, sent):
    peers = lax.axis_size("head")
    return lax.ppermute(sent, "head", [(turn - 1, turn), (peers - turn, peers - turn - 1)])


together = lax.optimization_barrier


def inverse_rms(values):
    return lax.rsqrt(jnp.mean(values * values, axis=-1, keepdims=True) + epsilon)


def sum_up(ref, row):
    @pl.when(pl.program_id(0) == 0)
    def _():
        ref[...] = jnp.zeros(ref.shape, f32)

    ref[...] += row


def norm_grads(values, scales, grad):
    inverse = inverse_rms(values)
    unit = values * inverse
    scaled = grad * scales
    inner = jnp.mean(scaled * unit, axis=-1, keepdims=True)
    return inverse * (scaled - unit * inner), jnp.sum(grad * unit, axis=0, keepdims=True)


def second_norm(
    me_ref, own_ref, residual_ref, cotangent_ref, right_ref, left_ref, gain_ref, low_ref, d_resid_ref, sum_ref
):
    grad = own_ref[...].astype(f32) + right_ref[...].astype(f32) + left_ref[...].astype(f32)
    part, gains = norm_grads(residual_ref[...], gain_ref[...], grad)
    total = cotangent_ref[...].astype(f32) + part
    d_resid_ref[...] = total
    low_ref[...] = total.astype(bf16)
    sum_up(sum_ref, gains)


def first_norm(me_ref, own_ref, inputs_ref, right_ref, left_ref, d_resid_ref, gain_ref, low_ref, grad_ref, sum_ref):
    grad = own_ref[...].astype(f32) + right_ref[...].astype(f32) + left_ref[...].astype(f32)
    part, gains = norm_grads(inputs_ref[...].astype(f32), gain_ref[...], grad)
    total = d_resid_ref[...] + part
    grad_ref[...] = total
    low_ref[...] = total.astype(bf16)
    sum_up(sum_ref, gains)


def local(
    block_in,
    pre_gain,
    gate_proj,
    input_proj,
    conv_taps,
    recur_gate,
    input_gate,
    decay_param,
    out_proj,
    post_gain,
    ffn_gate,
    ffn_up,
    ffn_down,
    cotangent,
):
    tokens, width = block_in.shape
    channels = gate_proj.shape[1]
    blocks, block_width, _ = recur_gate.shape
    tap_count = conv_taps.shape[0]
    hidden_units = ffn_gate.shape[1]
    seq_count, seq_index = lax.axis_size("seq"), lax.axis_index("seq")
    head_count, head_index = lax.axis_size("head"), lax.axis_index("head")
    share = tokens // head_count
    slabs = (channels // 128, tokens, 128)
    here = seq_index.astype(jnp.int32).reshape(1)
    place_index = head_index.astype(jnp.int32).reshape(1)
    forward_pairs = [(i, i + 1) for i in range(seq_count - 1)]
    backward_pairs = [(i + 1, i) for i in range(seq_count - 1)]

    def mine(rows):
        return lax.dynamic_slice_in_dim(rows, head_index * share, share, 0)

    def struct(*dims, kind=f32):
        return jax.ShapeDtypeStruct(dims, kind)

    halo_in = lax.ppermute(block_in[tokens - 8 :], "seq", forward_pairs)
    columns = width // seq_count
    column_block = lax.dynamic_slice_in_dim(out_proj, seq_index * columns, columns, 1)
    column_block = lax.all_gather(column_block, "head").reshape(head_count * channels, columns)
    soft = jax.nn.softplus(-decay_param)[None, :]
    slide = sharpness * jax.nn.sigmoid(-decay_param)[None, :]

    def normalise(rows):
        values = rows.astype(f32)
        return (values * inverse_rms(values) * pre_gain).astype(bf16)

    normed = normalise(block_in)
    branch_in = jnp.dot(normed, input_proj, preferred_element_type=f32).astype(bf16)
    halo = jnp.dot(normalise(halo_in), input_proj, preferred_element_type=f32).astype(bf16)
    conv_low, recur_rate, input_rate, local_states, products, seg_ends, end, gates = call(
        forward_scan,
        [
            struct(tokens, channels, kind=bf16),
            struct(tokens, channels),
            struct(tokens, channels),
            struct(*slabs),
            struct(*slabs),
            struct(2 * segments, channels),
            struct(2, channels),
            struct(channels, 2 * channels, kind=bf16),
        ],
        [
            pltpu.VMEM((tokens + 8, channels), f32),
            pltpu.VMEM((tokens, 2 * channels), f32),
            pltpu.VMEM(slabs, f32),
            pltpu.VMEM(slabs, f32),
        ],
        branch_in,
        halo,
        conv_taps,
        soft,
        recur_gate,
        input_gate,
        flops=4 * tokens * channels * channels,
    )
    ends = lax.all_gather(end, "seq")
    gate_pre = jnp.dot(normed, gate_proj, preferred_element_type=f32)
    states, mixed_low, entry = call(
        mix,
        [struct(tokens, channels), struct(tokens, channels, kind=bf16), struct(1, channels)],
        [],
        gate_pre,
        local_states,
        products,
        seg_ends,
        ends,
        here,
        scalars=1,
    )
    column_block, _ = together((column_block, mixed_low))
    projection = lax.all_gather(column_block, "seq")
    if columns % 128:
        projection = jnp.moveaxis(projection, 0, 1).reshape(1, head_count * channels, width)
    first = gather_first(mixed_low)
    second = gather_second(first)
    d_hidden = jnp.einsum("td,fd->tf", cotangent, ffn_down, preferred_element_type=f32)
    second, d_hidden = together((second, d_hidden))
    residual, normed_two = residual_norm(
        mixed_low,
        (*first, *second),
        projection,
        block_in,
        post_gain[None, :],
        place_index,
    )
    ffn_gpre = jnp.dot(normed_two, ffn_gate, preferred_element_type=f32)
    ffn_upre = jnp.dot(normed_two, ffn_up, preferred_element_type=f32)
    value, slope = gelu_parts(ffn_gpre)
    hidden = (value * ffn_upre).astype(bf16)
    d_gpre = (d_hidden * ffn_upre * slope).astype(bf16)
    d_upre = (d_hidden * value).astype(bf16)
    d_normed_two = jnp.einsum(
        "tf,df->td", d_gpre, ffn_gate, preferred_element_type=f32
    ) + jnp.einsum("tf,df->td", d_upre, ffn_up, preferred_element_type=f32)
    d_normed_two = d_normed_two.astype(bf16)
    d_normed_two, hidden, d_gpre, d_upre = together((d_normed_two, hidden, d_gpre, d_upre))
    first = scatter_first(d_normed_two)
    grad_ffn = weight_grads([(normed_two, d_gpre), (normed_two, d_upre), (cotangent, hidden)])
    first, grad_ffn = together((first, grad_ffn))
    grad_ffn = lax.psum_scatter(grad_ffn, "seq", scatter_dimension=0, tiled=True)
    second = scatter_second(d_normed_two, first, place_index)
    ffn_out = jnp.dot(hidden, ffn_down, preferred_element_type=f32).astype(bf16)
    second, ffn_out = together((second, ffn_out))
    own_rows = (share, width)
    d_out_share, d_resid, grad_postgain = by_rows(
        second_norm,
        place_index,
        [(d_normed_two, 0), (residual, 0), (cotangent, 0), (second[0], None), (second[1], None)],
        [post_gain[None, :]],
        [(own_rows, bf16), (own_rows, f32), ((1, width), f32)],
        grant=26 << 20,
    )
    first = gather_first(d_out_share)
    first, ffn_out = together((first, ffn_out))
    second = gather_second(first)
    cut = tokens * 5 // 8
    ffn_halves = [ffn_out[:cut], ffn_out[cut:]]
    turn_one = [line_turn(1, ffn_halves[0])]
    d_out_low = assembled(d_out_share, first, second, place_index, bf16)
    d_out_low, ffn_halves[1] = together((d_out_low, ffn_halves[1]))
    turn_one.append(line_turn(1, ffn_halves[1]))
    d_mixed = jnp.einsum("td,cd->tc", d_out_low, out_proj, preferred_element_type=f32)
    sent = added(ffn_halves[0], turn_one[0]).astype(bf16)
    d_mixed, sent = together((d_mixed, sent))
    turn_two = [line_turn(2, sent)]
    d_gate_low, grad_local, grad_prod, grad_segs, grad_end = call(
        backward_scan,
        [
            struct(tokens, channels, kind=bf16),
            struct(*slabs),
            struct(*slabs),
            struct(2 * segments, channels),
            struct(1, channels),
        ],
        [pltpu.VMEM(slabs, f32), pltpu.VMEM(slabs, f32)],
        d_mixed,
        gate_pre,
        states,
        recur_rate,
        soft,
    )
    backs = lax.all_gather(grad_end, "seq")
    sent = added(ffn_halves[1], turn_one[1]).astype(bf16)
    backs, sent = together((backs, sent))
    turn_two.append(line_turn(2, sent))
    d_both, d_branch, head_rows, decay_sums, taps_sums = call(
        backward_terms,
        [
            struct(tokens, 2 * channels, kind=bf16),
            struct(tokens, channels),
            struct(8, channels),
            struct(8, channels),
            struct(8 * tap_count, channels),
        ],
        [
            pltpu.VMEM((tokens + 8, channels), f32),
            pltpu.VMEM((tokens + 8, channels), f32),
            pltpu.VMEM((tokens + 8, channels), f32),
        ],
        grad_local,
        grad_prod,
        grad_segs,
        ends,
        backs,
        recur_rate,
        input_rate,
        conv_low,
        states,
        entry,
        soft,
        slide,
        conv_taps,
        branch_in,
        halo,
        gates,
        here,
        scalars=1,
        flops=4 * tokens * channels * channels,
    )
    sent = added(ffn_halves[0], turn_two[0]).astype(bf16)
    head_rows, d_branch, d_both, sent = together((head_rows, d_branch, d_both, sent))
    later_rows = lax.ppermute(head_rows, "seq", backward_pairs)
    turn_three = [line_turn(3, sent)]
    d_branch_low = (d_branch + jnp.pad(later_rows, ((tokens - 8, 0), (0, 0)))).astype(bf16)
    d_normed = jnp.einsum("tc,dc->td", d_gate_low, gate_proj, preferred_element_type=f32) + jnp.einsum(
        "tc,dc->td", d_branch_low, input_proj, preferred_element_type=f32
    )
    d_normed = d_normed.astype(bf16)
    d_normed, conv_low, d_both = together((d_normed, conv_low, d_both))
    first = scatter_first(d_normed)
    packed = gate_grads(conv_low, d_both, taps_sums, decay_sums, blocks, seq_count, width)
    grad_rest = weight_grads([(normed, d_gate_low), (normed, d_branch_low), (d_out_low, mixed_low)], packed)
    grad_ffn = finish_ffn(grad_ffn, 3)
    first, grad_rest, turn_three, turn_two, grad_ffn = together(
        (first, grad_rest, turn_three, turn_two, grad_ffn)
    )
    second = scatter_second(d_normed, first, place_index)
    sent = added(ffn_halves[1], turn_two[1]).astype(bf16)
    turn_three.append(line_turn(3, sent))
    grad_rest = lax.psum_scatter(grad_rest, "seq", scatter_dimension=0, tiled=True)
    grad_low, grad_input, grad_pregain = by_rows(
        first_norm,
        place_index,
        [(d_normed, 0), (block_in, 0), (second[0], None), (second[1], None), (d_resid, None)],
        [pre_gain[None, :]],
        [(own_rows, bf16), (own_rows, f32), ((1, width), f32)],
    )
    first = gather_first(grad_low)
    gains = jnp.concatenate([grad_pregain, grad_postgain], axis=0)
    gain_pieces = exchanged(lambda k: gains)
    base = residual + added(ffn_out, jnp.concatenate(turn_one), jnp.concatenate(turn_two))
    block_out = add_last(base, turn_three)
    first, block_out = together((first, block_out))
    second = gather_second(first)
    gains = jnp.sum(lax.all_gather(sum(gain_pieces, gains), "seq"), axis=0)
    gain_share = width // seq_count
    gains = lax.dynamic_slice_in_dim(gains, seq_index * gain_share, gain_share, 1)
    grad_rest, grad_ffn = together((grad_rest, grad_ffn))
    grad_rest = finish_rest(grad_rest, channels, blocks, block_width, tap_count, seq_count)
    second, grad_rest = together((second, grad_rest))
    grad_gate_proj, grad_input_proj, grad_out_proj, grad_taps, grad_recur, grad_inward, grad_decay = grad_rest
    grad_input = assembled(grad_input, first, second, place_index, f32)
    return (
        block_out,
        grad_input,
        gains[0],
        grad_gate_proj,
        grad_input_proj,
        grad_taps,
        grad_recur,
        grad_inward,
        grad_decay[0],
        grad_out_proj,
        gains[1],
        *grad_ffn,
    )


def solution(mesh):
    placed = (
        P("seq", None),
        P(),
        P(None, "head"),
        P(None, "head"),
        P(None, "head"),
        P("head", None, None),
        P("head", None, None),
        P("head"),
        P("head", None),
        P(),
        P(None, "head"),
        P(None, "head"),
        P("head", None),
        P("seq", None),
    )
    return jax.shard_map(
        local,
        mesh=mesh,
        in_specs=placed,
        out_specs=(
            P("seq", None),
            P("seq", None),
            P("seq"),
            P("seq", "head"),
            P("seq", "head"),
            P(None, ("head", "seq")),
            P("head", "seq", None),
            P("head", "seq", None),
            P(("head", "seq")),
            P("head", "seq"),
            P("seq"),
            P("seq", "head"),
            P("seq", "head"),
            P("head", "seq"),
        ),
        check_vma=False,
    )
```
